128 devices in a mesh: row: 16 (over x, y), col: 8 (over z, core).
Axes of the slice: x: 4, y: 4, z: 4, core: 2. Of those that a mesh axis runs over, the one named last changes fastest.
Arguments:
- b_ingest: bfloat16 [131072, 1024], P(('row', 'col')), may hold values from -6 to 6
- source_point: int32 [131072], P(('row', 'col')), may hold values from 0 to 131071, as said below
- panels: bfloat16 [2, 8, 16, 1024, 1024], P(None, None, 'row', 'col'), may hold values from -0.1875 to 0.1875
- diag_inverse: bfloat16 [2, 1024, 1024], replicated, may hold values from -1 to 1.5, as said below
Outputs:
- updated: bfloat16 [8, 16, 1024, 1024], P(None, 'row', 'col')
The draws below stay inside these ranges and needn't reach their ends.
Inputs may be any that keep to these rules, and one draw needn't show every extreme that they name: source_point is a permutation of 0 to 131071. Say point i lies in block b = i // 1024 at offset o = i mod 1024; it belongs to the device with row index b mod 16 and col index o // (1024 / 8). The shard of source_point on each device along row+col holds exactly 8 points of every device. diag_inverse[k] is lower triangular with diagonal entries between 0.5 and 1.5.
All inputs are finite; a program needn't handle non-finite values.
Results may differ from the reference program's by a relative error of at most 0.0056.
Values may be sent and summed in bfloat16 or wider, within the bound.
No kernel may reach another device: no remote copies, remote signals or barrier semaphores. Data moves between devices by JAX's collectives and lax.ppermute only.
A program may use at most 64 MiB of HBM per device.

```python
import jax
import jax.numpy as jnp
from jax import lax

PANEL_WIDTH = 1024
DRAW_COUNT = 1024
LOCAL_BLOCKS = 8
POINTS = 131072
N_ROW = 16
N_COL = 8


def draw_source_point(key, part):
    row_count = N_ROW
    col_count = N_COL
    dev_count = row_count * col_count
    per_device = POINTS // dev_count
    per_peer = per_device // dev_count
    block_rows = PANEL_WIDTH // col_count
    device_ids = jnp.arange(dev_count, dtype=jnp.int32)[:, None]
    local_ids = jnp.arange(per_device, dtype=jnp.int32)[None, :]
    grid_row = device_ids // col_count
    grid_col = device_ids % col_count
    local_block = local_ids // block_rows
    offset = local_ids % block_rows
    points = (local_block * row_count + grid_row) * PANEL_WIDTH + grid_col * block_rows + offset
    first_key = jax.random.fold_in(key, 11)
    second_key = jax.random.fold_in(key, 23)
    points = jax.random.permutation(first_key, points, axis=1, independent=True)
    points = points.reshape(dev_count, dev_count, per_peer)
    points = jnp.transpose(points, (1, 0, 2)).reshape(dev_count, per_device)
    points = jax.random.permutation(second_key, points, axis=1, independent=True)
    return points.reshape(POINTS).astype(jnp.int32)


def draw_diag_inverse(key, part):
    off_key = jax.random.fold_in(key, 5)
    diag_key = jax.random.fold_in(key, 7)
    lower = jax.random.truncated_normal(off_key, -6.0, 6.0, (2, PANEL_WIDTH, PANEL_WIDTH), jnp.float32) * PANEL_WIDTH ** (-0.5)
    diagonal = jax.random.uniform(diag_key, (2, PANEL_WIDTH, 1), jnp.float32, 0.5, 1.5)
    row_ids = jnp.arange(PANEL_WIDTH, dtype=jnp.int32)[:, None]
    col_ids = jnp.arange(PANEL_WIDTH, dtype=jnp.int32)[None, :]
    below = (row_ids > col_ids)[None, :, :]
    on_diag = (row_ids == col_ids)[None, :, :]
    value = jnp.where(below, lower, 0.0) + jnp.where(on_diag, diagonal, 0.0)
    return value.astype(jnp.bfloat16)


def block_scale(rng, extent, cuts, smallest, largest):
    factor_of, own = 1.0, jax.random.fold_in(rng, 6)
    for position, blocks in cuts:
        heights = jnp.exp(jax.random.uniform(jax.random.fold_in(own, position), (blocks,), jnp.float32, smallest / len(cuts), largest / len(cuts)))
        factor_of = factor_of * jnp.repeat(heights, extent[position] // blocks).reshape([-1 if axis == position else 1 for axis in range(len(extent))])
    return factor_of


def centred(stream_key, dims, spread, reach, split=(), kind=jnp.bfloat16):
    entries = spread * jax.random.normal(stream_key, dims, jnp.float32)
    if split:
        entries = entries * block_scale(stream_key, dims, split, -0.22, 0.18)
    return jnp.clip(entries, -reach, reach).astype(kind)


def setup_inputs(seed: int = 0) -> dict:
    streams_of = jax.random.split(jax.random.key(seed), 5)
    b_ingest = centred(streams_of[0], (POINTS, DRAW_COUNT), 1.0, 6.0, ((0, 128),))
    source_point = draw_source_point(jax.random.fold_in(streams_of[4], 71), 0)
    panels = centred(streams_of[2], (2, LOCAL_BLOCKS, N_ROW, PANEL_WIDTH, PANEL_WIDTH), PANEL_WIDTH ** -0.5, 0.1875, ((2, 16), (3, 8)))
    diag_inverse = draw_diag_inverse(jax.random.fold_in(streams_of[4], 71), 0)
    return {"b_ingest": b_ingest, "source_point": source_point, "panels": panels, "diag_inverse": diag_inverse}


def reference(b_ingest, source_point, panels, diag_inverse):
    rhs = jnp.zeros((POINTS, DRAW_COUNT), jnp.bfloat16).at[source_point].set(b_ingest)
    blocks = rhs.reshape(LOCAL_BLOCKS * N_ROW, PANEL_WIDTH, DRAW_COUNT)
    factor = panels.reshape(2, LOCAL_BLOCKS * N_ROW, PANEL_WIDTH, PANEL_WIDTH)
    solved0 = jnp.dot(diag_inverse[0].astype(jnp.float32), blocks[0].astype(jnp.float32)).astype(jnp.bfloat16)
    second = (blocks[1].astype(jnp.float32) - jnp.dot(factor[0, 1].astype(jnp.float32), solved0.astype(jnp.float32))).astype(jnp.bfloat16)
    solved1 = jnp.dot(diag_inverse[1].astype(jnp.float32), second.astype(jnp.float32)).astype(jnp.bfloat16)
    first_f = solved0.astype(jnp.float32)
    second_f = solved1.astype(jnp.float32)

    def one_block(items):
        block_rhs, factor0, factor1 = items
        value = block_rhs.astype(jnp.float32) - jnp.dot(factor0.astype(jnp.float32), first_f)
        value = value - jnp.dot(factor1.astype(jnp.float32), second_f)
        return value.astype(jnp.bfloat16)

    result = lax.map(one_block, (blocks, factor[0], factor[1]))
    result = result.at[0].set(solved0).at[1].set(solved1)
    return result.reshape(LOCAL_BLOCKS, N_ROW, PANEL_WIDTH, DRAW_COUNT)
```

```python
import functools

import jax
import jax.numpy as jnp
from jax import lax
from jax.experimental import pallas as pl
from jax.experimental.pallas import tpu as pltpu
from jax.sharding import PartitionSpec as P

AXES = ("row", "col")
BF16 = jnp.bfloat16
F32 = jnp.float32
VMEM = pl.BlockSpec(memory_space=pltpu.VMEM)


def device_id(x, y, z, k):
    return (x % 4 * 4 + y % 4) * 8 + z % 4 * 2 + k


def send(value, move, only=None):
    pairs = []
    for x in range(4):
        for y in range(4):
            for z in range(4):
                for k in range(2):
                    if only is None or only(x, y, z, k):
                        pairs.append((device_id(x, y, z, k), device_id(*move(x, y, z, k))))
    return lax.ppermute(value, AXES, pairs)


def along_first(step):
    return lambda x, y, z, k: (x + step, y, z, k) if k == 0 else (x, y + step, z, k)


def along_second(step):
    return lambda x, y, z, k: (x, y + step, z, k) if k == 0 else (x + step, y, z, k)


def along_z(step):
    return lambda x, y, z, k: (x, y, z + step, k)


def other_core(x, y, z, k):
    return (x, y, z, 1 - k)


def iota(shape, axis):
    return lax.broadcasted_iota(jnp.int32, shape, axis)


def dot(a, b, contract):
    return lax.dot_general(a, b, ((contract[:1], contract[1:]), ((), ())), preferred_element_type=F32)


def order_kernel(points_ref, rows_ref, ordered_ref, early_ref, perm_ref):
    count = rows_ref.shape[0]
    points = points_ref[...]
    block = points >> 10
    offset = points & 1023
    target = (block & 15) * 8 + (offset >> 7)
    local = (block >> 4) * 128 + (offset & 127)
    wanted = (iota((128, count), 0) == target).astype(F32)
    earlier = (iota((count, count), 0) < iota((count, count), 1)).astype(F32).astype(BF16)
    seen = dot(wanted.astype(BF16), earlier, (1, 0))
    rank = jnp.sum(wanted * seen, axis=0, keepdims=True).astype(jnp.int32)
    slot = target * 8 + rank
    perm_ref[...] = (iota((count, count), 0) == slot).astype(F32).astype(BF16)
    part = iota((128, count), 0)
    digits = jnp.where(part < 6, jnp.where(part % 2 == 0, local >> 5, local & 31), 0).astype(F32).astype(BF16)
    ids = dot(perm_ref[...], digits, (1, 1))
    lane = iota((64, 128), 1)
    for r in range(16):
        mixed = jnp.where(lane < 2, ids[r * 64 : r * 64 + 64], jnp.where(lane < 4, ids[0:64], ids[64:128]))
        early_ref[r * 64 : r * 64 + 64, 128:256] = mixed.astype(BF16)
    for q in range(4):
        cols = slice(q * 256, q * 256 + 256)
        part_rows = dot(perm_ref[...], rows_ref[:, cols], (1, 0))
        ordered_ref[:, cols] = part_rows.astype(BF16)
        for h in range(2):
            first = part_rows[0:64, h * 128 : h * 128 + 128]
            second = part_rows[64:128, h * 128 : h * 128 + 128]
            r = q * 4 + h * 2
            even = jnp.where(lane < 64, first, pltpu.roll(second, 64, 1))
            odd = jnp.where(lane < 64, pltpu.roll(first, 64, 1), second)
            early_ref[r * 64 : r * 64 + 64, 0:128] = even.astype(BF16)
            early_ref[r * 64 + 64 : r * 64 + 128, 0:128] = odd.astype(BF16)


def compact_kernel(early_ref, own_ref, lead_ref, next_ref):
    count = early_ref.shape[0]
    pick = iota((8, 128), 0)
    lane = iota((8, 128), 1)
    weight = jnp.where(lane == 2 * pick, 32.0, jnp.where(lane == 2 * pick + 1, 1.0, 0.0))
    weight = jnp.where(pick < 3, weight, 0.0).astype(BF16)
    locals_ = dot(weight, early_ref[:, 128:256], (1, 1)).astype(jnp.int32)
    own_ref[...] = locals_
    place = iota((128, count), 0)
    hit0 = (place == locals_[1:2]).astype(F32).astype(BF16)
    hit1 = (place == locals_[2:3]).astype(F32).astype(BF16)
    data = early_ref[:, 0:128]
    lead_ref[...] = dot(data, hit0, (0, 1))[0:64].astype(BF16)
    next_ref[...] = dot(data, hit1, (0, 1))[64:128].astype(BF16)


def gather_cols(refs, scratch):
    col = lax.axis_index("col")
    z = col // 2
    k = col % 2
    for pair_ref, shift in zip(refs, (0, 3, 1, 2)):
        at = (z + shift) % 4
        scratch[2 * at + k] = pair_ref[0:64]
        scratch[2 * at + 1 - k] = pair_ref[64:128]
    return jnp.concatenate([scratch[c] for c in range(8)], axis=1)


def first_kernel(p0, p1, p2, p3, inverse_ref, next_ref, link_ref, solved_ref, second_ref, scratch):
    lead = gather_cols((p0, p1, p2, p3), scratch)
    solved = dot(lead, inverse_ref[...], (1, 1)).astype(BF16)
    solved_ref[...] = solved
    update = dot(solved, link_ref[...], (1, 1))
    second_ref[...] = (next_ref[...].astype(F32) - update).astype(BF16)


def second_kernel(p0, p1, p2, p3, inverse_ref, solved_ref, both_ref, scratch):
    second = gather_cols((p0, p1, p2, p3), scratch)
    solved = dot(second, inverse_ref[...], (1, 1)).astype(BF16)
    k = lax.axis_index("col") % 2
    half = pl.ds(pl.multiple_of(k * 32, 32), 32)
    scratch2 = solved
    both_ref[:, 0:1024] = solved_ref[half, :]
    both_ref[:, 1024:2048] = jnp.where(k == 0, scratch2[0:32], scratch2[32:64])


def scatter_kernel(own_ref, arrived_ref, out_ref, hit_ref):
    count = arrived_ref.shape[0]
    hit_ref[...] = (iota((count, count), 0) == own_ref[0:1]).astype(F32).astype(BF16)
    for q in range(4):
        cols = slice(q * 256, q * 256 + 256)
        out_ref[:, cols] = dot(hit_ref[...], arrived_ref[:, cols], (1, 0)).astype(BF16)


def update_kernel(*refs):
    pieces, (rows_ref, panels_ref, out_ref, solved_t, head_ref) = refs[:8], refs[8:]
    row = lax.axis_index("row")
    col = lax.axis_index("col")
    x = row // 4
    y = row % 4
    shifts = (0, 3, 1, 2)
    for i in range(8):
        k = col % 2 if i < 4 else 1 - col % 2
        first = jnp.where(k == 0, x, y)
        second = jnp.where(k == 0, y, x)
        b = (second + shifts[i % 4]) % 4
        for j in range(4):
            a = (first + shifts[j]) % 4
            r = jnp.where(k == 0, 4 * a + b, 4 * b + a)
            at = pl.multiple_of(r * 64 + k * 32, 32)
            solved_t[pl.ds(at, 32), :] = pieces[i][j * 32 : j * 32 + 32, :]
    unit = (iota((128, 1024), 1) == iota((128, 1024), 0) + col * 128).astype(F32) * -1.0
    for p in range(2):
        kept = jnp.where(row < 2, 0.0, panels_ref[p, 0, 0].astype(F32))
        head_ref[p] = jnp.where(row == p, unit, kept).astype(BF16)
    keep = jnp.where(row < 2, 0.0, 1.0)
    for q in range(4):
        draws = slice(q * 256, q * 256 + 256)
        s0 = solved_t[draws, 0:1024]
        s1 = solved_t[draws, 1024:2048]
        head = dot(head_ref[0], s0, (1, 1)) + dot(head_ref[1], s1, (1, 1))
        out_ref[0, 0, :, draws] = (rows_ref[0:128, draws].astype(F32) * keep - head).astype(BF16)
        tail0 = panels_ref[0, 1:8, 0].reshape(896, 1024)
        tail1 = panels_ref[1, 1:8, 0].reshape(896, 1024)
        tail = dot(tail0, s0, (1, 1)) + dot(tail1, s1, (1, 1))
        rest = rows_ref[128:1024, draws].astype(F32) - tail
        out_ref[1:8, 0, :, draws] = rest.astype(BF16).reshape(7, 128, 256)


def run(kernel, args, outs, scratch=(), flops=0, moved=0):
    return pl.pallas_call(
        kernel,
        out_shape=[jax.ShapeDtypeStruct(s, d) for s, d in outs],
        in_specs=[VMEM] * len(args),
        out_specs=[VMEM] * len(outs),
        scratch_shapes=list(scratch),
        compiler_params=pltpu.CompilerParams(vmem_limit_bytes=56 << 20),
        cost_estimate=pl.CostEstimate(flops=flops, bytes_accessed=moved, transcendentals=0),
    )(*args)


def spread_rows(piece):
    row = lax.axis_index("row")
    held = jnp.where(row == 1, piece, jnp.zeros_like(piece))

    def at_first(step):
        return lambda x, y, z, k: (y == 1 + step and x == 0) if k == 0 else (x == step and y == 1)

    def at_second(step):
        return lambda x, y, z, k: x == step if k == 0 else y == 1 + step

    def first(step):
        return lambda x, y, z, k: (x, y + step, z, k) if k == 0 else (x + step, y, z, k)

    def second(step):
        return lambda x, y, z, k: (x + step, y, z, k) if k == 0 else (x, y + step, z, k)

    up = send(held, first(1), at_first(0))
    down = send(held, first(-1), at_first(0))
    far = send(up, first(1), at_first(1))
    line = held + up + down + far
    up = send(line, second(1), at_second(0))
    down = send(line, second(-1), at_second(0))
    far = send(up, second(1), at_second(1))
    return line + up + down + far


def around_cols(piece):
    pair = jnp.concatenate([piece, send(piece, other_core)], axis=0)
    return (pair, send(pair, along_z(1)), send(pair, along_z(-1)), send(pair, along_z(2)))


def around_rows(piece):
    line = jnp.concatenate(
        [piece, send(piece, along_first(1)), send(piece, along_first(-1)), send(piece, along_first(2))], axis=0
    )
    held = [line, send(line, along_second(1)), send(line, along_second(-1)), send(line, along_second(2))]
    return held + [send(h, other_core) for h in held]


def per_device(b_ingest, source_point, panels, diag_inverse):
    link = spread_rows(panels[0, 0, 0])
    ordered, early = run(
        order_kernel,
        (source_point.reshape(1, 1024), b_ingest),
        [((1024, 1024), BF16), ((1024, 256), BF16)],
        [pltpu.VMEM((1024, 1024), BF16)],
        3 << 30,
        5 << 20,
    )
    exchange = functools.partial(lax.all_to_all, axis_name=AXES, split_axis=0, concat_axis=0, tiled=True)
    early = exchange(early.reshape(128, 8, 256)).reshape(1024, 256)
    arrived = exchange(ordered.reshape(128, 8, 1024)).reshape(1024, 1024)
    own, lead, follow = run(
        compact_kernel,
        (early,),
        [((8, 1024), jnp.int32), ((64, 128), BF16), ((64, 128), BF16)],
        (),
        1 << 27,
        1 << 20,
    )
    pairs = around_cols(lead)
    solved, second = run(
        first_kernel,
        (*pairs, diag_inverse[0], follow, link),
        [((64, 1024), BF16), ((64, 128), BF16)],
        [pltpu.VMEM((8, 64, 128), BF16)],
        1 << 28,
        3 << 20,
    )
    pairs = around_cols(second)
    (both,) = run(
        second_kernel,
        (*pairs, diag_inverse[1], solved),
        [((32, 2048), BF16)],
        [pltpu.VMEM((8, 64, 128), BF16)],
        1 << 28,
        3 << 20,
    )
    pieces = around_rows(both)
    (rows,) = run(
        scatter_kernel,
        (own, arrived),
        [((1024, 1024), BF16)],
        [pltpu.VMEM((1024, 1024), BF16)],
        1 << 31,
        4 << 20,
    )
    (updated,) = run(
        update_kernel,
        (*pieces, rows, panels),
        [((8, 1, 128, 1024), BF16)],
        [pltpu.VMEM((1024, 2048), BF16), pltpu.VMEM((2, 128, 1024), BF16)],
        1 << 32,
        14 << 20,
    )
    return updated


def solution(mesh):
    return jax.shard_map(
        per_device,
        mesh=mesh,
        in_specs=(
            P(("row", "col"), None),
            P(("row", "col")),
            P(None, None, "row", "col", None),
            P(),
        ),
        out_specs=P(None, "row", "col", None),
        check_vma=False,
    )
```

```python
import functools

import jax
import jax.numpy as jnp
from jax import lax
from jax.experimental import pallas as pl
from jax.experimental.pallas import tpu as pltpu
from jax.sharding import PartitionSpec as P

AXES = ("row", "col")
BF16 = jnp.bfloat16
F32 = jnp.float32
VMEM = pl.BlockSpec(memory_space=pltpu.VMEM)


def device_id(x, y, z, k):
    return (x % 4 * 4 + y % 4) * 8 + z % 4 * 2 + k


def send(value, move, only=None):
    pairs = []
    for x in range(4):
        for y in range(4):
            for z in range(4):
                for k in range(2):
                    if only is None or only(x, y, z, k):
                        pairs.append((device_id(x, y, z, k), device_id(*move(x, y, z, k))))
    return lax.ppermute(value, AXES, pairs)


def along_first(step):
    return lambda x, y, z, k: (x + step, y, z, k) if k == 0 else (x, y + step, z, k)


def along_second(step):
    return lambda x, y, z, k: (x, y + step, z, k) if k == 0 else (x + step, y, z, k)


def along_z(step):
    return lambda x, y, z, k: (x, y, z + step, k)


def other_core(x, y, z, k):
    return (x, y, z, 1 - k)


def iota(shape, axis):
    return lax.broadcasted_iota(jnp.int32, shape, axis)


def dot(a, b, contract):
    return lax.dot_general(a, b, ((contract[:1], contract[1:]), ((), ())), preferred_element_type=F32)


def order_kernel(points_ref, rows_ref, out_ref, perm_ref, head_ref):
    count = rows_ref.shape[0]
    points = points_ref[...]
    block = points >> 10
    offset = points & 1023
    target = (block & 15) * 8 + (offset >> 7)
    local = (block >> 4) * 128 + (offset & 127)
    wanted = (iota((128, count), 0) == target).astype(F32)
    earlier = (iota((count, count), 0) < iota((count, count), 1)).astype(F32).astype(BF16)
    seen = dot(wanted.astype(BF16), earlier, (1, 0))
    rank = jnp.sum(wanted * seen, axis=0, keepdims=True).astype(jnp.int32)
    slot = target * 8 + rank
    perm_ref[...] = (iota((count, count), 0) == slot).astype(F32).astype(BF16)
    part = iota((128, count), 0)
    digits = jnp.where(part < 10, jnp.where(part % 2 == 0, local >> 5, local & 31), 0).astype(F32).astype(BF16)
    ids = dot(perm_ref[...], digits, (1, 1))
    for q in range(4):
        part_rows = dot(perm_ref[...], rows_ref[:, q * 256 : q * 256 + 256], (1, 0))
        out_ref[:, 384 + q * 256 : 640 + q * 256] = part_rows.astype(BF16)
        head_ref[:, q * 256 : q * 256 + 256] = part_rows[0:128]
    lane = iota((64, 128), 1)

    def both(value, first, odd):
        tiles = [value[first + 16 * z + 8 * odd : first + 16 * z + 8 * odd + 8] for z in range(4)]
        return jnp.concatenate([t for t in tiles for _ in range(2)], axis=0)

    shared = [both(ids, 64 * t, odd) for t in range(2) for odd in range(2)]
    heads = [[both(head_ref[:, 128 * i : 128 * i + 128], 64 * t, odd) for i in range(8)] for t in range(2) for odd in range(2)]
    for r in range(16):
        x, y = r // 4, r % 4
        rows = slice(r * 64, r * 64 + 64)
        mixed = ids[rows]
        for i in range(4):
            mixed = jnp.where(lane < 2 + 2 * i, mixed, shared[i])
        out_ref[rows, 256:384] = mixed.astype(BF16)
        for t in range(2):
            cut = None
            for p in range(4):
                tiles = heads[2 * t + p // 2]
                tile, at = (tiles[y], 32 * x) if p % 2 == 0 else (tiles[4 + x], 32 * y)
                moved = pltpu.roll(tile, (32 * p - at) % 128, 1) if (32 * p - at) % 128 else tile
                cut = moved if cut is None else jnp.where(lane < 32 * p, cut, moved)
            out_ref[rows, t * 128 : t * 128 + 128] = cut.astype(BF16)


def compact_kernel(early_ref, own_ref, lead_ref, next_ref):
    count = early_ref.shape[0]
    pick = iota((8, 128), 0)
    lane = iota((8, 128), 1)
    weight = jnp.where(lane == 2 * pick, 32.0, jnp.where(lane == 2 * pick + 1, 1.0, 0.0))
    weight = jnp.where(pick < 5, weight, 0.0).astype(BF16)
    locals_ = dot(weight, early_ref[:, 256:384], (1, 1)).astype(jnp.int32)
    own_ref[...] = locals_
    place = iota((128, count), 0)
    for t, ref in enumerate((lead_ref, next_ref)):
        data = early_ref[:, 128 * t : 128 * t + 128]
        for odd in range(2):
            i = 1 + 2 * t + odd
            hit = (place == locals_[i : i + 1]).astype(F32).astype(BF16)
            found = dot(data, hit, (0, 1))[64 * odd : 64 * odd + 64]
            ref[:, 128 * odd : 128 * odd + 128] = found.astype(BF16)


def gather_cols(refs, scratch):
    z = lax.axis_index("col") // 2
    for ref, shift in zip(refs, (0, 3, 1, 2)):
        scratch[(z + shift) % 4] = ref[...]
    return jnp.concatenate([scratch[i] for i in range(4)], axis=1)


def first_kernel(p0, p1, p2, p3, inverse_ref, next_ref, own_ref, other_ref, solved_ref, second_ref, scratch):
    lead = gather_cols((p0, p1, p2, p3), scratch)
    solved = dot(lead, inverse_ref[0], (1, 1)).astype(BF16)
    solved_ref[...] = solved
    own = dot(solved, own_ref[...], (1, 1))
    other = dot(solved, other_ref[...], (1, 1))
    even = lax.axis_index("col") % 2 == 0
    low = jnp.where(even, own, other)
    high = jnp.where(even, other, own)
    second_ref[:, 0:128] = (next_ref[:, 0:128].astype(F32) - low).astype(BF16)
    second_ref[:, 128:256] = (next_ref[:, 128:256].astype(F32) - high).astype(BF16)


def second_kernel(p0, p1, p2, p3, inverse_ref, solved_ref, both_ref, scratch):
    second = gather_cols((p0, p1, p2, p3), scratch)
    solved = dot(second, inverse_ref[0], (1, 1)).astype(BF16)
    even = lax.axis_index("col") % 2 == 0
    both_ref[:, 0:1024] = jnp.where(even, solved_ref[0:32], solved_ref[32:64])
    both_ref[:, 1024:2048] = jnp.where(even, solved[0:32], solved[32:64])


def scatter_kernel(own_ref, arrived_ref, out_ref, hit_ref, rows_ref, sem):
    count = arrived_ref.shape[0]
    copy = pltpu.make_async_copy(arrived_ref.at[:, 384:1408], rows_ref, sem)
    copy.start()
    hit_ref[...] = (iota((count, count), 0) == own_ref[0:1]).astype(F32).astype(BF16)
    copy.wait()
    for q in range(4):
        cols = slice(q * 256, q * 256 + 256)
        out_ref[:, cols] = dot(hit_ref[...], rows_ref[:, cols], (1, 0)).astype(BF16)


def place_of(kind):
    row = lax.axis_index("row")
    core = lax.axis_index("col") % 2
    x, y = row // 4, row % 4
    if kind:
        core = 1 - core
    return jnp.where(core == 0, x, y), jnp.where(core == 0, y, x), core


def heads_of(panels_ref, head_ref):
    row = lax.axis_index("row")
    col = lax.axis_index("col")
    unit = (iota((128, 1024), 1) == iota((128, 1024), 0) + col * 128).astype(F32) * -1.0
    for p in range(2):
        kept = jnp.where(row < 2, 0.0, panels_ref[p, 0, 0].astype(F32))
        head_ref[p] = jnp.where(row == p, unit, kept).astype(BF16)


def product(panels_ref, head_ref, solved_t):
    s0 = solved_t[:, 0:1024]
    s1 = solved_t[:, 1024:2048]
    head = dot(head_ref[0], s0, (1, 1)) + dot(head_ref[1], s1, (1, 1))
    tail0 = panels_ref[0, 1:8, 0].reshape(896, 1024)
    tail1 = panels_ref[1, 1:8, 0].reshape(896, 1024)
    return head, dot(tail0, s0, (1, 1)) + dot(tail1, s1, (1, 1))


SHIFTS = (0, 3, 1, 2)


def most_kernel(own0, own1, own2, oth0, oth1, oth2, rows_ref, panels_ref, out_ref, solved_t, head_ref):
    heads_of(panels_ref, head_ref)
    keep = jnp.where(lax.axis_index("row") < 2, 0.0, 1.0)
    for i in range(3):
        for kind, piece in enumerate(((own0, oth0), (own1, oth1), (own2, oth2))[i]):
            first, _, _ = place_of(kind)
            for j in range(4):
                at = pl.multiple_of(128 * kind + 32 * ((first + SHIFTS[j]) % 4), 32)
                solved_t[i, pl.ds(at, 32), :] = piece[j * 32 : j * 32 + 32, :]
        head, tail = product(panels_ref, head_ref, solved_t.at[i])
        for kind in range(2):
            _, second, core = place_of(kind)
            draws = pl.ds(pl.multiple_of(128 * (4 * core + (second + SHIFTS[i]) % 4), 128), 128)
            part = slice(128 * kind, 128 * kind + 128)
            out_ref[0, 0, :, draws] = (rows_ref[0:128, draws].astype(F32) * keep - head[:, part]).astype(BF16)
            rest = rows_ref[128:1024, draws].astype(F32) - tail[:, part]
            out_ref[1:8, 0, :, draws] = rest.astype(BF16).reshape(7, 128, 128)


def last_kernel(own_a, own_b, oth_a, oth_b, rows_ref, panels_ref, done_ref, out_ref, solved_t, head_ref, in_ref, res_ref, sems):
    keep = jnp.where(lax.axis_index("row") < 2, 0.0, 1.0)
    draws = []
    for kind in range(2):
        _, second, core = place_of(kind)
        draws.append(pl.ds(pl.multiple_of(128 * (4 * core + (second + 2) % 4), 128), 128))
    loads = [pltpu.make_async_copy(rows_ref.at[:, draws[i]], in_ref.at[i], sems.at[i]) for i in range(2)]
    for load in loads:
        load.start()
    heads_of(panels_ref, head_ref)
    for kind, (a, b) in enumerate(((own_a, own_b), (oth_a, oth_b))):
        first, _, _ = place_of(kind)
        for j in range(4):
            at = pl.multiple_of(128 * kind + 32 * ((first + SHIFTS[j]) % 4), 32)
            piece = a if j < 2 else b
            solved_t[pl.ds(at, 32), :] = piece[j % 2 * 32 : j % 2 * 32 + 32, :]
    head, tail = product(panels_ref, head_ref, solved_t)
    stores = []
    for kind in range(2):
        loads[kind].wait()
        part = slice(128 * kind, 128 * kind + 128)
        res_ref[kind, 0, 0] = (in_ref[kind, 0:128].astype(F32) * keep - head[:, part]).astype(BF16)
        rest = in_ref[kind, 128:1024].astype(F32) - tail[:, part]
        res_ref[kind, 1:8, 0] = rest.astype(BF16).reshape(7, 128, 128)
        stores.append(pltpu.make_async_copy(res_ref.at[kind], out_ref.at[:, :, :, draws[kind]], sems.at[2 + kind]))
        stores[kind].start()
    for store in stores:
        store.wait()


ANY = pl.BlockSpec(memory_space=pl.ANY)


def run(kernel, args, outs, scratch=(), specs=None, out_specs=None, aliases=None, limit=16, flops=0, moved=0):
    return pl.pallas_call(
        kernel,
        out_shape=[jax.ShapeDtypeStruct(s, d) for s, d in outs],
        grid=(1,),
        in_specs=specs or [VMEM] * len(args),
        out_specs=out_specs or [VMEM] * len(outs),
        scratch_shapes=list(scratch),
        input_output_aliases=aliases or {},
        compiler_params=pltpu.CompilerParams(vmem_limit_bytes=limit << 20),
        cost_estimate=pl.CostEstimate(flops=flops, bytes_accessed=moved, transcendentals=0),
    )(*args)


def spread_rows(piece):
    row = lax.axis_index("row")
    held = jnp.where(row == 1, piece, jnp.zeros_like(piece))

    def at_first(step):
        return lambda x, y, z, k: (y == 1 + step and x == 0) if k == 0 else (x == step and y == 1)

    def at_second(step):
        return lambda x, y, z, k: x == step if k == 0 else y == 1 + step

    def first(step):
        return lambda x, y, z, k: (x, y + step, z, k) if k == 0 else (x + step, y, z, k)

    def second(step):
        return lambda x, y, z, k: (x + step, y, z, k) if k == 0 else (x, y + step, z, k)

    up = send(held, first(1), at_first(0))
    down = send(held, first(-1), at_first(0))
    far = send(up, first(1), at_first(1))
    line = held + up + down + far
    up = send(line, second(1), at_second(0))
    down = send(line, second(-1), at_second(0))
    far = send(up, second(1), at_second(1))
    return line + up + down + far


def around_cols(piece):
    return (piece, send(piece, along_z(1)), send(piece, along_z(-1)), send(piece, along_z(2)))


def around_rows(piece):
    line = jnp.concatenate(
        [piece, send(piece, along_first(1)), send(piece, along_first(-1)), send(piece, along_first(2))], axis=0
    )
    up, down = send(line, along_second(1)), send(line, along_second(-1))
    far = [send(up[0:64], along_second(1)), send(down[64:128], along_second(-1))]
    return [line, up, down], far


def inverse_spec(panel):
    return pl.BlockSpec((1, 1024, 1024), lambda i: (panel, 0, 0))


def per_device(b_ingest, source_point, panels, diag_inverse):
    (ordered,) = run(
        order_kernel,
        (source_point.reshape(1, 1024), b_ingest),
        [((1024, 1408), BF16)],
        [pltpu.VMEM((1024, 1024), BF16), pltpu.VMEM((128, 1024), F32)],
        limit=32,
        flops=3 << 30,
        moved=5 << 20,
    )
    piece, ordered = lax.optimization_barrier((panels[0, 0, 0], ordered))
    link = spread_rows(piece)
    link_other = send(link, other_core)
    arrived = lax.all_to_all(ordered.reshape(128, 8, 1408), AXES, split_axis=0, concat_axis=0, tiled=True)
    arrived = arrived.reshape(1024, 1408)
    own, lead, follow = run(
        compact_kernel,
        (arrived,),
        [((8, 1024), jnp.int32), ((64, 256), BF16), ((64, 256), BF16)],
        specs=[pl.BlockSpec((1024, 384), lambda i: (0, 0))],
        limit=12,
        flops=1 << 27,
        moved=1 << 20,
    )
    solved, second = run(
        first_kernel,
        (*around_cols(lead), diag_inverse, follow, link, link_other),
        [((64, 1024), BF16), ((64, 256), BF16)],
        [pltpu.VMEM((4, 64, 256), BF16)],
        specs=[VMEM] * 4 + [inverse_spec(0)] + [VMEM] * 3,
        limit=12,
        flops=1 << 28,
        moved=3 << 20,
    )
    (both,) = run(
        second_kernel,
        (*around_cols(second), diag_inverse, solved),
        [((32, 2048), BF16)],
        [pltpu.VMEM((4, 64, 256), BF16)],
        specs=[VMEM] * 4 + [inverse_spec(1), VMEM],
        limit=12,
        flops=1 << 28,
        moved=3 << 20,
    )
    near, far = around_rows(both)
    near_other = [send(n, other_core) for n in near]
    far_other = [send(f, other_core) for f in far]
    (rows,) = run(
        scatter_kernel,
        (own, arrived),
        [((1024, 1024), BF16)],
        [pltpu.VMEM((1024, 1024), BF16), pltpu.VMEM((1024, 1024), BF16), pltpu.SemaphoreType.DMA],
        specs=[VMEM, ANY],
        limit=20,
        flops=1 << 31,
        moved=4 << 20,
    )
    shape = ((8, 1, 128, 1024), BF16)
    (most,) = run(
        most_kernel,
        (*near, *near_other, rows, panels),
        [shape],
        [pltpu.VMEM((3, 256, 2048), BF16), pltpu.VMEM((2, 128, 1024), BF16)],
        limit=32,
        flops=3 << 30,
        moved=12 << 20,
    )
    (updated,) = run(
        last_kernel,
        (*far, *far_other, rows, panels, most),
        [shape],
        [
            pltpu.VMEM((256, 2048), BF16),
            pltpu.VMEM((2, 128, 1024), BF16),
            pltpu.VMEM((2, 1024, 128), BF16),
            pltpu.VMEM((2, 8, 1, 128, 128), BF16),
            pltpu.SemaphoreType.DMA((4,)),
        ],
        specs=[VMEM] * 4 + [ANY, VMEM, ANY],
        out_specs=[ANY],
        aliases={6: 0},
        limit=24,
        flops=1 << 30,
        moved=6 << 20,
    )
    return updated


def solution(mesh):
    return jax.shard_map(
        per_device,
        mesh=mesh,
        in_specs=(
            P(("row", "col"), None),
            P(("row", "col")),
            P(None, None, "row", "col", None),
            P(),
        ),
        out_specs=P(None, "row", "col", None),
        check_vma=False,
    )
```

```python
import functools

import jax
import jax.numpy as jnp
from jax import lax
from jax.experimental import pallas as pl
from jax.experimental.pallas import tpu as pltpu
from jax.sharding import PartitionSpec as P

AXES = ("row", "col")
BF16 = jnp.bfloat16
F32 = jnp.float32
VMEM = pl.BlockSpec(memory_space=pltpu.VMEM)


def device_id(x, y, z, k):
    return (x % 4 * 4 + y % 4) * 8 + z % 4 * 2 + k


def send(value, move, only=None):
    pairs = []
    for x in range(4):
        for y in range(4):
            for z in range(4):
                for k in range(2):
                    if only is None or only(x, y, z, k):
                        pairs.append((device_id(x, y, z, k), device_id(*move(x, y, z, k))))
    return lax.ppermute(value, AXES, pairs)


def swap(kind, at):
    return (at ^ 1, 3 - at, at ^ 2)[kind]


def along_first(kind):
    return lambda x, y, z, k: (swap(kind, x), y, z, k) if k == 0 else (x, swap(kind, y), z, k)


def along_second(kind):
    return lambda x, y, z, k: (x, swap(kind, y), z, k) if k == 0 else (swap(kind, x), y, z, k)


def along_z(kind):
    return lambda x, y, z, k: (x, y, swap(kind, z), k)


def other_core(x, y, z, k):
    return (x, y, z, 1 - k)


def iota(shape, axis):
    return lax.broadcasted_iota(jnp.int32, shape, axis)


def dot(a, b, contract):
    return lax.dot_general(a, b, ((contract[:1], contract[1:]), ((), ())), preferred_element_type=F32)


def order_kernel(points_ref, rows_hbm, out_hbm, rows_ref, out_ref, perm_ref, head_ref, in_sems, out_sems):
    count = rows_ref.shape[0]
    loads = []
    for q in range(4):
        cols = pl.ds(q * 256, 256)
        loads.append(pltpu.make_async_copy(rows_hbm.at[:, cols], rows_ref.at[:, cols], in_sems.at[q]))
        loads[q].start()
    points = points_ref[...]
    block = points >> 10
    offset = points & 1023
    target = (block & 15) * 8 + (offset >> 7)
    local = (block >> 4) * 128 + (offset & 127)
    wanted = (iota((128, count), 0) == target).astype(F32)
    earlier = (iota((count, count), 0) < iota((count, count), 1)).astype(F32).astype(BF16)
    seen = dot(wanted.astype(BF16), earlier, (1, 0))
    rank = jnp.sum(wanted * seen, axis=0, keepdims=True).astype(jnp.int32)
    slot = target * 8 + rank
    perm_ref[...] = (iota((count, count), 0) == slot).astype(F32).astype(BF16)
    part = iota((128, count), 0)
    digits = jnp.where(part < 10, jnp.where(part % 2 == 0, local >> 5, local & 31), 0).astype(F32).astype(BF16)
    ids = dot(perm_ref[...], digits, (1, 1))
    stores = []
    for q in range(4):
        loads[q].wait()
        part_rows = dot(perm_ref[...], rows_ref[:, q * 256 : q * 256 + 256], (1, 0))
        out_ref[:, 384 + q * 256 : 640 + q * 256] = part_rows.astype(BF16)
        head_ref[:, q * 256 : q * 256 + 256] = part_rows[0:128]
        cols = pl.ds(384 + q * 256, 256)
        stores.append(pltpu.make_async_copy(out_ref.at[:, cols], out_hbm.at[:, cols], out_sems.at[q]))
        stores[q].start()
    lane = iota((64, 128), 1)

    def both(value, first, odd):
        tiles = [value[first + 16 * z + 8 * odd : first + 16 * z + 8 * odd + 8] for z in range(4)]
        return jnp.concatenate([t for t in tiles for _ in range(2)], axis=0)

    shared = [both(ids, 64 * t, odd) for t in range(2) for odd in range(2)]
    heads = [[both(head_ref[:, 128 * i : 128 * i + 128], 64 * t, odd) for i in range(8)] for t in range(2) for odd in range(2)]
    for r in range(16):
        x, y = r // 4, r % 4
        rows = slice(r * 64, r * 64 + 64)
        mixed = ids[rows]
        for i in range(4):
            mixed = jnp.where(lane < 2 + 2 * i, mixed, shared[i])
        out_ref[rows, 256:384] = mixed.astype(BF16)
        for t in range(2):
            cut = None
            for p in range(4):
                tiles = heads[2 * t + p // 2]
                tile, at = (tiles[y], 32 * x) if p % 2 == 0 else (tiles[4 + x], 32 * y)
                moved = pltpu.roll(tile, (32 * p - at) % 128, 1) if (32 * p - at) % 128 else tile
                cut = moved if cut is None else jnp.where(lane < 32 * p, cut, moved)
            out_ref[rows, t * 128 : t * 128 + 128] = cut.astype(BF16)
    cols = pl.ds(0, 384)
    stores.append(pltpu.make_async_copy(out_ref.at[:, cols], out_hbm.at[:, cols], out_sems.at[4]))
    stores[4].start()
    for store in stores:
        store.wait()


def compact_kernel(early_ref, own_ref, lead_ref, next_ref):
    count = early_ref.shape[0]
    pick = iota((8, 128), 0)
    lane = iota((8, 128), 1)
    weight = jnp.where(lane == 2 * pick, 32.0, jnp.where(lane == 2 * pick + 1, 1.0, 0.0))
    weight = jnp.where(pick < 5, weight, 0.0).astype(BF16)
    locals_ = dot(weight, early_ref[:, 256:384], (1, 1)).astype(jnp.int32)
    own_ref[...] = locals_
    place = iota((128, count), 0)
    for t, ref in enumerate((lead_ref, next_ref)):
        data = early_ref[:, 128 * t : 128 * t + 128]
        for odd in range(2):
            i = 1 + 2 * t + odd
            hit = (place == locals_[i : i + 1]).astype(F32).astype(BF16)
            found = dot(data, hit, (0, 1))[64 * odd : 64 * odd + 64]
            ref[:, 128 * odd : 128 * odd + 128] = found.astype(BF16)


def gather_cols(refs, scratch):
    z = lax.axis_index("col") // 2
    for ref, at in zip(refs, (z, z ^ 1, 3 - z, z ^ 2)):
        scratch[at] = ref[...]
    return jnp.concatenate([scratch[i] for i in range(4)], axis=1)


def first_kernel(p0, p1, p2, p3, inverse_ref, next_ref, own_ref, other_ref, solved_ref, second_ref, scratch):
    lead = gather_cols((p0, p1, p2, p3), scratch)
    solved = dot(lead, inverse_ref[...], (1, 1)).astype(BF16)
    solved_ref[...] = solved
    own = dot(solved, own_ref[...], (1, 1))
    other = dot(solved, other_ref[...], (1, 1))
    even = lax.axis_index("col") % 2 == 0
    low = jnp.where(even, own, other)
    high = jnp.where(even, other, own)
    second_ref[:, 0:128] = (next_ref[:, 0:128].astype(F32) - low).astype(BF16)
    second_ref[:, 128:256] = (next_ref[:, 128:256].astype(F32) - high).astype(BF16)


def second_kernel(p0, p1, p2, p3, inverse_ref, solved_ref, both_ref, scratch):
    second = gather_cols((p0, p1, p2, p3), scratch)
    solved = dot(second, inverse_ref[...], (1, 1)).astype(BF16)
    even = lax.axis_index("col") % 2 == 0
    both_ref[:, 0:1024] = jnp.where(even, solved_ref[0:32], solved_ref[32:64])
    both_ref[:, 1024:2048] = jnp.where(even, solved[0:32], solved[32:64])


def scatter_kernel(own_ref, arrived_ref, out_ref, hit_ref, rows_ref, sem):
    count = arrived_ref.shape[0]
    copy = pltpu.make_async_copy(arrived_ref.at[:, 384:1408], rows_ref, sem)
    copy.start()
    hit_ref[...] = (iota((count, count), 0) == own_ref[0:1]).astype(F32).astype(BF16)
    copy.wait()
    for q in range(4):
        cols = slice(q * 256, q * 256 + 256)
        out_ref[:, cols] = dot(hit_ref[...], rows_ref[:, cols], (1, 0)).astype(BF16)


def place_of(kind):
    row = lax.axis_index("row")
    core = lax.axis_index("col") % 2
    x, y = row // 4, row % 4
    if kind:
        core = 1 - core
    return jnp.where(core == 0, x, y), jnp.where(core == 0, y, x), core


def load_kernel(source_hbm, first_ref, second_ref, sems):
    copies = [pltpu.make_async_copy(source_hbm.at[i], ref, sems.at[i]) for i, ref in enumerate((first_ref, second_ref))]
    for copy in copies:
        copy.start()
    for copy in copies:
        copy.wait()


def heads_of(panels_ref, head_ref):
    row = lax.axis_index("row")
    col = lax.axis_index("col")
    unit = (iota((128, 1024), 1) == iota((128, 1024), 0) + col * 128).astype(F32) * -1.0
    for p in range(2):
        kept = jnp.where(row < 2, 0.0, panels_ref[p, 0, 0].astype(F32))
        head_ref[p] = jnp.where(row == p, unit, kept).astype(BF16)


def product(panels_ref, head_ref, solved_t):
    s0 = solved_t[:, 0:1024]
    s1 = solved_t[:, 1024:2048]
    head = dot(head_ref[0], s0, (1, 1)) + dot(head_ref[1], s1, (1, 1))
    tail0 = panels_ref[0, 1:8, 0].reshape(896, 1024)
    tail1 = panels_ref[1, 1:8, 0].reshape(896, 1024)
    return head, dot(tail0, s0, (1, 1)) + dot(tail1, s1, (1, 1))


def update_kernel(lines, *refs):
    count = 2 * sum(parts for _, parts in lines)
    pieces = list(refs[:count])
    panels_ref, rows_hbm, out_hbm, solved_t, head_ref, in_ref, res_ref, sems = refs[count:]
    keep = jnp.where(lax.axis_index("row") < 2, 0.0, 1.0)
    draws = []
    for which, _ in lines:
        for kind in range(2):
            _, second, core = place_of(kind)
            at = second if which == 3 else swap(which, second)
            draws.append(pl.ds(pl.multiple_of(128 * (4 * core + at), 128), 128))
    loads = [pltpu.make_async_copy(rows_hbm.at[:, :, :, d], in_ref.at[i], sems.at[0, i]) for i, d in enumerate(draws)]
    for load in loads:
        load.start()
    heads_of(panels_ref, head_ref)
    stores = []
    for n, (_, parts) in enumerate(lines):
        for kind in range(2):
            first, _, _ = place_of(kind)
            places = (first, first ^ 1, 3 - first, first ^ 2)
            held = [pieces.pop(0) for _ in range(parts)]
            for j in range(4):
                at = pl.multiple_of(128 * kind + 32 * places[j], 32)
                ref, j = (held[0], j) if parts == 1 else (held[j // 2], j % 2)
                solved_t[n, pl.ds(at, 32), :] = ref[j * 32 : j * 32 + 32, :]
        head, tail = product(panels_ref, head_ref, solved_t.at[n])
        for kind in range(2):
            i = 2 * n + kind
            loads[i].wait()
            part = slice(128 * kind, 128 * kind + 128)
            res_ref[i, 0, 0] = (in_ref[i, 0, 0].astype(F32) * keep - head[:, part]).astype(BF16)
            rest = in_ref[i, 1:8, 0].reshape(896, 128).astype(F32) - tail[:, part]
            res_ref[i, 1:8, 0] = rest.astype(BF16).reshape(7, 128, 128)
            stores.append(pltpu.make_async_copy(res_ref.at[i], out_hbm.at[:, :, :, draws[i]], sems.at[1, i]))
            stores[i].start()
    for store in stores:
        store.wait()


HBM = pl.BlockSpec(memory_space=pltpu.HBM)
ANY = pl.BlockSpec(memory_space=pl.ANY)


def launch(kernel, args, outs, scratch=(), specs=None, out_specs=None, aliases=None, limit=16, flops=0, moved=0):
    return pl.pallas_call(
        kernel,
        out_shape=[jax.ShapeDtypeStruct(s, d) for s, d in outs],
        grid=(1,),
        in_specs=specs or [VMEM] * len(args),
        out_specs=out_specs or [VMEM] * len(outs),
        scratch_shapes=list(scratch),
        input_output_aliases=aliases or {},
        compiler_params=pltpu.CompilerParams(vmem_limit_bytes=limit << 20),
        cost_estimate=pl.CostEstimate(flops=flops, bytes_accessed=moved, transcendentals=0),
    )(*args)


def spread_along(value, first, source):
    def move(kind):
        return along_first(kind) if first else along_second(kind)

    return [send(value, move(kind), source) for kind in range(3)]


def spread_first(piece):
    return spread_along(piece, True, lambda x, y, z, k: x == 0 and y == 1)


def spread_second(piece):
    return spread_along(piece, False, lambda x, y, z, k: y == 1 if k == 0 else x == 0)


def around_cols(piece):
    return (piece, send(piece, along_z(0)), send(piece, along_z(1)), send(piece, along_z(2)))


def update(lines, pieces, panels, rows):
    count = 2 * len(lines)
    kernel = functools.partial(update_kernel, lines)
    return launch(
        kernel,
        (*pieces, panels, rows),
        [((8, 1, 128, 1024), BF16)],
        [
            pltpu.VMEM((len(lines), 256, 2048), BF16),
            pltpu.VMEM((2, 128, 1024), BF16),
            pltpu.VMEM((count, 8, 1, 128, 128), BF16),
            pltpu.VMEM((count, 8, 1, 128, 128), BF16),
            pltpu.SemaphoreType.DMA((2, count)),
        ],
        specs=[VMEM] * (len(pieces) + 1) + [HBM],
        out_specs=[HBM],
        aliases={len(pieces) + 1: 0},
        limit=22,
        flops=len(lines) << 30,
        moved=2 << 20,
    )[0]


def steps(b_ingest, source_point, panels, diag_inverse):
    row = lax.axis_index("row")
    piece = panels[0, 0, 0]
    line = spread_first(piece)
    (ordered,) = launch(
        order_kernel,
        (source_point.reshape(1, 1024), b_ingest),
        [((1024, 1408), BF16)],
        [
            pltpu.VMEM((1024, 1024), BF16),
            pltpu.VMEM((1024, 1408), BF16),
            pltpu.VMEM((1024, 1024), BF16),
            pltpu.VMEM((128, 1024), F32),
            pltpu.SemaphoreType.DMA((4,)),
            pltpu.SemaphoreType.DMA((5,)),
        ],
        specs=[VMEM, HBM],
        out_specs=[HBM],
        limit=63,
        flops=3 << 30,
        moved=5 << 20,
    )
    line = jnp.where(row == 1, piece, jnp.zeros_like(piece)) + line[0] + line[1] + line[2]
    line, ordered = lax.optimization_barrier((line, ordered))
    plane = spread_second(line)
    arrived = lax.all_to_all(ordered.reshape(128, 8, 1408), AXES, split_axis=0, concat_axis=0, tiled=True)
    inverses, _ = lax.optimization_barrier((diag_inverse, ordered))
    inverses = launch(
        load_kernel,
        (inverses,),
        [((1024, 1024), BF16)] * 2,
        [pltpu.SemaphoreType.DMA((2,))],
        specs=[HBM],
        limit=6,
        moved=8 << 20,
    )
    link = line + plane[0] + plane[1] + plane[2]
    link_other = send(link, other_core)
    arrived = arrived.reshape(1024, 1408)
    own, lead, follow = launch(
        compact_kernel,
        (arrived,),
        [((8, 1024), jnp.int32), ((64, 256), BF16), ((64, 256), BF16)],
        specs=[pl.BlockSpec((1024, 384), lambda i: (0, 0))],
        limit=12,
        flops=1 << 27,
        moved=1 << 20,
    )
    solved, second = launch(
        first_kernel,
        (*around_cols(lead), inverses[0], follow, link, link_other),
        [((64, 1024), BF16), ((64, 256), BF16)],
        [pltpu.VMEM((4, 64, 256), BF16)],
        limit=12,
        flops=1 << 28,
        moved=3 << 20,
    )
    (both,) = launch(
        second_kernel,
        (*around_cols(second), inverses[1], solved),
        [((32, 2048), BF16)],
        [pltpu.VMEM((4, 64, 256), BF16)],
        limit=12,
        flops=1 << 28,
        moved=3 << 20,
    )
    (rows,) = launch(
        scatter_kernel,
        (own, arrived),
        [((1024, 1024), BF16)],
        [pltpu.VMEM((1024, 1024), BF16), pltpu.VMEM((1024, 1024), BF16), pltpu.SemaphoreType.DMA],
        specs=[VMEM, ANY],
        limit=20,
        flops=1 << 31,
        moved=4 << 20,
    )
    rows = rows.reshape(8, 1, 128, 1024)
    line = [both] + [send(both, along_first(i)) for i in range(3)]
    line = jnp.concatenate(line, axis=0)
    side0, side1 = send(line, along_second(0)), send(line, along_second(1))
    far0, far1 = send(side1[0:64], along_second(0)), send(side0[64:128], along_second(1))
    rows = update(((3, 1),), (line, send(line, other_core)), panels, rows)
    pieces = (side0, send(side0, other_core), side1, send(side1, other_core))
    rows = update(((0, 1), (1, 1)), pieces, panels, rows)
    pieces = (far0, far1, send(far0, other_core), send(far1, other_core))
    return update(((2, 2),), pieces, panels, rows)


def solution(mesh):
    return jax.shard_map(
        steps,
        mesh=mesh,
        in_specs=(
            P(("row", "col"), None),
            P(("row", "col")),
            P(None, None, "row", "col", None),
            P(),
        ),
        out_specs=P(None, "row", "col", None),
        check_vma=False,
    )
```

```python
import functools

import jax
import jax.numpy as jnp
from jax import lax
from jax.experimental import pallas as pl
from jax.experimental.pallas import tpu as pltpu
from jax.sharding import PartitionSpec as P

AXES = ("row", "col")
BF16 = jnp.bfloat16
F32 = jnp.float32
VMEM = pl.BlockSpec(memory_space=pltpu.VMEM)


def device_id(x, y, z, k):
    return (x % 4 * 4 + y % 4) * 8 + z % 4 * 2 + k


def send(value, move, only=None):
    pairs = []
    for x in range(4):
        for y in range(4):
            for z in range(4):
                for k in range(2):
                    if only is None or only(x, y, z, k):
                        pairs.append((device_id(x, y, z, k), device_id(*move(x, y, z, k))))
    return lax.ppermute(value, AXES, pairs)


def swap(kind, at):
    return (at ^ 1, 3 - at, at ^ 2)[kind]


def along_first(kind):
    return lambda x, y, z, k: (swap(kind, x), y, z, k) if k == 0 else (x, swap(kind, y), z, k)


def along_second(kind):
    return lambda x, y, z, k: (x, swap(kind, y), z, k) if k == 0 else (swap(kind, x), y, z, k)


def along_z(kind):
    return lambda x, y, z, k: (x, y, swap(kind, z), k)


def other_core(x, y, z, k):
    return (x, y, z, 1 - k)


def iota(shape, axis):
    return lax.broadcasted_iota(jnp.int32, shape, axis)


def dot(a, b, contract):
    return lax.dot_general(a, b, ((contract[:1], contract[1:]), ((), ())), preferred_element_type=F32)


def order_kernel(points_ref, rows_hbm, out_hbm, rows_ref, out_ref, perm_ref, head_ref, in_sems, out_sems):
    count = rows_ref.shape[0]
    load = pltpu.make_async_copy(rows_hbm, rows_ref, in_sems.at[0])
    load.start()
    points = points_ref[...]
    block = points >> 10
    offset = points & 1023
    target = (block & 15) * 8 + (offset >> 7)
    local = (block >> 4) * 128 + (offset & 127)
    wanted = (iota((128, count), 0) == target).astype(F32)
    earlier = (iota((count, count), 0) < iota((count, count), 1)).astype(F32).astype(BF16)
    seen = dot(wanted.astype(BF16), earlier, (1, 0))
    rank = jnp.sum(wanted * seen, axis=0, keepdims=True).astype(jnp.int32)
    slot = target * 8 + rank
    perm_ref[...] = (iota((count, count), 0) == slot).astype(F32).astype(BF16)
    part = iota((128, count), 0)
    digits = jnp.where(part < 10, jnp.where(part % 2 == 0, local >> 5, local & 31), 0).astype(F32).astype(BF16)
    ids = dot(perm_ref[...], digits, (1, 1))
    lane = iota((64, 128), 1)

    def both(value, first, odd):
        tiles = [value[first + 16 * z + 8 * odd : first + 16 * z + 8 * odd + 8] for z in range(4)]
        return jnp.concatenate([t for t in tiles for _ in range(2)], axis=0)

    kinds = [(64 * t, odd) for t in range(2) for odd in range(2)]
    shared = [both(ids, *kind) for kind in kinds]
    stores = []
    load.wait()
    for x in range(4):
        chunk = slice(x * 256, x * 256 + 256)
        part_rows = dot(perm_ref[chunk, :], rows_ref[...], (1, 0))
        out_ref[chunk, 384:1408] = part_rows.astype(BF16)
        if x == 0:
            head_ref[...] = part_rows[0:128]
        for y in range(4):
            rows = slice(x * 256 + y * 64, x * 256 + y * 64 + 64)
            mixed = ids[rows]
            for i in range(4):
                mixed = jnp.where(lane < 2 + 2 * i, mixed, shared[i])
            out_ref[rows, 256:384] = mixed.astype(BF16)
            for t in range(2):
                cut = None
                for p in range(4):
                    tile, at = (y, 32 * x) if p % 2 == 0 else (4 + x, 32 * y)
                    tile = both(head_ref[:, 128 * tile : 128 * tile + 128], *kinds[2 * t + p // 2])
                    moved = pltpu.roll(tile, (32 * p - at) % 128, 1) if (32 * p - at) % 128 else tile
                    cut = moved if cut is None else jnp.where(lane < 32 * p, cut, moved)
                out_ref[rows, t * 128 : t * 128 + 128] = cut.astype(BF16)
        span = pl.ds(x * 256, 256)
        stores.append(pltpu.make_async_copy(out_ref.at[span], out_hbm.at[span], out_sems.at[x]))
        stores[x].start()
    for store in stores:
        store.wait()


def compact_kernel(early_ref, own_ref, lead_ref, next_ref):
    count = early_ref.shape[0]
    pick = iota((8, 128), 0)
    lane = iota((8, 128), 1)
    weight = jnp.where(lane == 2 * pick, 32.0, jnp.where(lane == 2 * pick + 1, 1.0, 0.0))
    weight = jnp.where(pick < 5, weight, 0.0).astype(BF16)
    locals_ = dot(weight, early_ref[:, 256:384], (1, 1)).astype(jnp.int32)
    own_ref[...] = locals_
    place = iota((128, count), 0)
    for t, ref in enumerate((lead_ref, next_ref)):
        data = early_ref[:, 128 * t : 128 * t + 128]
        for odd in range(2):
            i = 1 + 2 * t + odd
            hit = (place == locals_[i : i + 1]).astype(F32).astype(BF16)
            found = dot(data, hit, (0, 1))[64 * odd : 64 * odd + 64]
            ref[:, 128 * odd : 128 * odd + 128] = found.astype(BF16)


def gather_cols(refs, scratch):
    z = lax.axis_index("col") // 2
    for ref, at in zip(refs, (z, z ^ 1, 3 - z, z ^ 2)):
        scratch[at] = ref[...]
    return jnp.concatenate([scratch[i] for i in range(4)], axis=1)


def first_kernel(p0, p1, p2, p3, inverse_ref, next_ref, own_ref, other_ref, solved_ref, second_ref, scratch):
    lead = gather_cols((p0, p1, p2, p3), scratch)
    solved = dot(lead, inverse_ref[...], (1, 1)).astype(BF16)
    solved_ref[...] = solved
    own = dot(solved, own_ref[...], (1, 1))
    other = dot(solved, other_ref[...], (1, 1))
    even = lax.axis_index("col") % 2 == 0
    low = jnp.where(even, own, other)
    high = jnp.where(even, other, own)
    second_ref[:, 0:128] = (next_ref[:, 0:128].astype(F32) - low).astype(BF16)
    second_ref[:, 128:256] = (next_ref[:, 128:256].astype(F32) - high).astype(BF16)


def second_kernel(p0, p1, p2, p3, inverse_ref, solved_ref, both_ref, scratch):
    second = gather_cols((p0, p1, p2, p3), scratch)
    solved = dot(second, inverse_ref[...], (1, 1)).astype(BF16)
    even = lax.axis_index("col") % 2 == 0
    both_ref[:, 0:1024] = jnp.where(even, solved_ref[0:32], solved_ref[32:64])
    both_ref[:, 1024:2048] = jnp.where(even, solved[0:32], solved[32:64])


def scatter_kernel(own_ref, arrived_ref, out_ref, hit_ref, rows_ref, sem):
    count = arrived_ref.shape[0]
    copy = pltpu.make_async_copy(arrived_ref.at[:, 384:1408], rows_ref, sem)
    copy.start()
    hit_ref[...] = (iota((count, count), 0) == own_ref[0:1]).astype(F32).astype(BF16)
    copy.wait()
    for q in range(4):
        cols = slice(q * 256, q * 256 + 256)
        out_ref[:, cols] = dot(hit_ref[...], rows_ref[:, cols], (1, 0)).astype(BF16)


def place_of(kind):
    row = lax.axis_index("row")
    core = lax.axis_index("col") % 2
    x, y = row // 4, row % 4
    if kind:
        core = 1 - core
    return jnp.where(core == 0, x, y), jnp.where(core == 0, y, x), core


def load_kernel(source_hbm, first_ref, second_ref, sems):
    copies = [pltpu.make_async_copy(source_hbm.at[i], ref, sems.at[i]) for i, ref in enumerate((first_ref, second_ref))]
    for copy in copies:
        copy.start()
    for copy in copies:
        copy.wait()


def heads_of(panels_ref, head_ref):
    row = lax.axis_index("row")
    col = lax.axis_index("col")
    unit = (iota((128, 1024), 1) == iota((128, 1024), 0) + col * 128).astype(F32) * -1.0
    for p in range(2):
        kept = jnp.where(row < 2, 0.0, panels_ref[p, 0, 0].astype(F32))
        head_ref[p] = jnp.where(row == p, unit, kept).astype(BF16)


def product(panels_ref, head_ref, solved_t):
    s0 = solved_t[:, 0:1024]
    s1 = solved_t[:, 1024:2048]
    head = dot(head_ref[0], s0, (1, 1)) + dot(head_ref[1], s1, (1, 1))
    tail0 = panels_ref[0, 1:8, 0].reshape(896, 1024)
    tail1 = panels_ref[1, 1:8, 0].reshape(896, 1024)
    return head, dot(tail0, s0, (1, 1)) + dot(tail1, s1, (1, 1))


def update_kernel(blocks, *refs):
    count = sum(parts for _, _, parts in blocks)
    pieces = list(refs[:count])
    panels_ref, rows_hbm, out_hbm, solved_t, head_ref, in_ref, res_ref, sems = refs[count:]
    keep = jnp.where(lax.axis_index("row") < 2, 0.0, 1.0)
    draws, loads, stores = [], [], []
    for i, (kind, which, _) in enumerate(blocks):
        _, second, core = place_of(kind)
        at = second if which == 3 else swap(which, second)
        draws.append(pl.ds(pl.multiple_of(128 * (4 * core + at), 128), 128))
        loads.append(pltpu.make_async_copy(rows_hbm.at[:, :, :, draws[i]], in_ref.at[i], sems.at[0, i]))
        loads[i].start()
    heads_of(panels_ref, head_ref)
    for i, (kind, _, parts) in enumerate(blocks):
        first, _, _ = place_of(kind)
        places = (first, first ^ 1, 3 - first, first ^ 2)
        held = [pieces.pop(0) for _ in range(parts)]
        for j in range(4):
            at = pl.multiple_of(128 * i + 32 * places[j], 32)
            ref, j = (held[0], j) if parts == 1 else (held[j // 2], j % 2)
            solved_t[pl.ds(at, 32), :] = ref[j * 32 : j * 32 + 32, :]
    head, tail = product(panels_ref, head_ref, solved_t)
    for i in range(2):
        loads[i].wait()
        part = slice(128 * i, 128 * i + 128)
        res_ref[i, 0, 0] = (in_ref[i, 0, 0].astype(F32) * keep - head[:, part]).astype(BF16)
        rest = in_ref[i, 1:8, 0].reshape(896, 128).astype(F32) - tail[:, part]
        res_ref[i, 1:8, 0] = rest.astype(BF16).reshape(7, 128, 128)
        stores.append(pltpu.make_async_copy(res_ref.at[i], out_hbm.at[:, :, :, draws[i]], sems.at[1, i]))
        stores[i].start()
    for store in stores:
        store.wait()


HBM = pl.BlockSpec(memory_space=pltpu.HBM)
ANY = pl.BlockSpec(memory_space=pl.ANY)


def launch(kernel, args, outs, scratch=(), specs=None, out_specs=None, aliases=None, limit=16, flops=0, moved=0):
    return pl.pallas_call(
        kernel,
        out_shape=[jax.ShapeDtypeStruct(s, d) for s, d in outs],
        grid=(1,),
        in_specs=specs or [VMEM] * len(args),
        out_specs=out_specs or [VMEM] * len(outs),
        scratch_shapes=list(scratch),
        input_output_aliases=aliases or {},
        compiler_params=pltpu.CompilerParams(vmem_limit_bytes=limit << 20),
        cost_estimate=pl.CostEstimate(flops=flops, bytes_accessed=moved, transcendentals=0),
    )(*args)


def spread_along(value, first, source):
    def move(kind):
        return along_first(kind) if first else along_second(kind)

    return [send(value, move(kind), source) for kind in range(3)]


def spread_first(piece):
    return spread_along(piece, True, lambda x, y, z, k: x == 0 and y == 1)


def spread_second(piece):
    return spread_along(piece, False, lambda x, y, z, k: y == 1 if k == 0 else x == 0)


def around_cols(piece):
    return (piece, send(piece, along_z(0)), send(piece, along_z(1)), send(piece, along_z(2)))


def update(blocks, pieces, panels, rows):
    return launch(
        functools.partial(update_kernel, blocks),
        (*pieces, panels, rows),
        [((8, 1, 128, 1024), BF16)],
        [
            pltpu.VMEM((256, 2048), BF16),
            pltpu.VMEM((2, 128, 1024), BF16),
            pltpu.VMEM((2, 8, 1, 128, 128), BF16),
            pltpu.VMEM((2, 8, 1, 128, 128), BF16),
            pltpu.SemaphoreType.DMA((2, 2)),
        ],
        specs=[VMEM] * (len(pieces) + 1) + [HBM],
        out_specs=[HBM],
        aliases={len(pieces) + 1: 0},
        limit=20,
        flops=1 << 30,
        moved=2 << 20,
    )[0]


def steps(b_ingest, source_point, panels, diag_inverse):
    row = lax.axis_index("row")
    (ordered,) = launch(
        order_kernel,
        (source_point.reshape(1, 1024), b_ingest),
        [((1024, 1408), BF16)],
        [
            pltpu.VMEM((1024, 1024), BF16),
            pltpu.VMEM((1024, 1408), BF16),
            pltpu.VMEM((1024, 1024), BF16),
            pltpu.VMEM((128, 1024), F32),
            pltpu.SemaphoreType.DMA((1,)),
            pltpu.SemaphoreType.DMA((4,)),
        ],
        specs=[VMEM, HBM],
        out_specs=[HBM],
        limit=63,
        flops=3 << 30,
        moved=5 << 20,
    )
    piece = panels[0, 0, 0]
    line = spread_first(piece)
    line = jnp.where(row == 1, piece, jnp.zeros_like(piece)) + line[0] + line[1] + line[2]
    plane = spread_second(line)
    arrived = lax.all_to_all(ordered.reshape(128, 8, 1408), AXES, split_axis=0, concat_axis=0, tiled=True)
    inverses, _ = lax.optimization_barrier((diag_inverse, ordered))
    inverses = launch(
        load_kernel,
        (inverses,),
        [((1024, 1024), BF16)] * 2,
        [pltpu.SemaphoreType.DMA((2,))],
        specs=[HBM],
        limit=6,
        moved=8 << 20,
    )
    arrived = arrived.reshape(1024, 1408)
    own, lead, follow = launch(
        compact_kernel,
        (arrived,),
        [((8, 1024), jnp.int32), ((64, 256), BF16), ((64, 256), BF16)],
        specs=[pl.BlockSpec((1024, 384), lambda i: (0, 0))],
        limit=12,
        flops=1 << 27,
        moved=1 << 20,
    )
    line, plane, _ = lax.optimization_barrier((line, plane, own))
    link = line + plane[0] + plane[1] + plane[2]
    link_other = send(link, other_core)
    solved, second = launch(
        first_kernel,
        (*around_cols(lead), inverses[0], follow, link, link_other),
        [((64, 1024), BF16), ((64, 256), BF16)],
        [pltpu.VMEM((4, 64, 256), BF16)],
        limit=12,
        flops=1 << 28,
        moved=3 << 20,
    )
    (both,) = launch(
        second_kernel,
        (*around_cols(second), inverses[1], solved),
        [((32, 2048), BF16)],
        [pltpu.VMEM((4, 64, 256), BF16)],
        limit=12,
        flops=1 << 28,
        moved=3 << 20,
    )
    (rows,) = launch(
        scatter_kernel,
        (own, arrived),
        [((1024, 1024), BF16)],
        [pltpu.VMEM((1024, 1024), BF16), pltpu.VMEM((1024, 1024), BF16), pltpu.SemaphoreType.DMA],
        specs=[VMEM, ANY],
        limit=20,
        flops=1 << 31,
        moved=4 << 20,
    )
    rows = rows.reshape(8, 1, 128, 1024)
    line = [both] + [send(both, along_first(i)) for i in range(3)]
    line = jnp.concatenate(line, axis=0)
    side0, side1 = send(line, along_second(0)), send(line, along_second(1))
    far0, far1 = send(side1[0:64], along_second(0)), send(side0[64:128], along_second(1))
    line_other = send(line, other_core)
    side0_other, side1_other = send(side0, other_core), send(side1, other_core)
    far_other = send(far0, other_core), send(far1, other_core)
    rows = update(((0, 3, 1), (1, 3, 1)), (line, line_other), panels, rows)
    rows = update(((0, 0, 1), (0, 1, 1)), (side0, side1), panels, rows)
    rows = update(((1, 0, 1), (1, 1, 1)), (side0_other, side1_other), panels, rows)
    return update(((0, 2, 2), (1, 2, 2)), (far0, far1, *far_other), panels, rows)


def solution(mesh):
    return jax.shard_map(
        steps,
        mesh=mesh,
        in_specs=(
            P(("row", "col"), None),
            P(("row", "col")),
            P(None, None, "row", "col", None),
            P(),
        ),
        out_specs=P(None, "row", "col", None),
        check_vma=False,
    )
```

```python
import functools

import jax
import jax.numpy as jnp
from jax import lax
from jax.experimental import pallas as pl
from jax.experimental.pallas import tpu as pltpu
from jax.sharding import PartitionSpec as P

AXES = ("row", "col")
BF16 = jnp.bfloat16
F32 = jnp.float32
VMEM = pl.BlockSpec(memory_space=pltpu.VMEM)


def device_id(x, y, z, k):
    return (x % 4 * 4 + y % 4) * 8 + z % 4 * 2 + k


def send(value, move, only=None):
    pairs = []
    for x in range(4):
        for y in range(4):
            for z in range(4):
                for k in range(2):
                    if only is None or only(x, y, z, k):
                        pairs.append((device_id(x, y, z, k), device_id(*move(x, y, z, k))))
    return lax.ppermute(value, AXES, pairs)


def swap(kind, at):
    return (at ^ 1, 3 - at, at ^ 2)[kind]


def along_first(kind):
    return lambda x, y, z, k: (swap(kind, x), y, z, k) if k == 0 else (x, swap(kind, y), z, k)


def along_second(kind):
    return lambda x, y, z, k: (x, swap(kind, y), z, k) if k == 0 else (swap(kind, x), y, z, k)


def along_z(kind):
    return lambda x, y, z, k: (x, y, swap(kind, z), k)


def other_core(x, y, z, k):
    return (x, y, z, 1 - k)


def iota(shape, axis):
    return lax.broadcasted_iota(jnp.int32, shape, axis)


def dot(a, b, contract):
    return lax.dot_general(a, b, ((contract[:1], contract[1:]), ((), ())), preferred_element_type=F32)


def order_kernel(points_ref, rows_hbm, panels_hbm, out_hbm, piece_ref, rows_ref, out_ref, perm_ref, head_ref, in_sems, out_sems):
    count = rows_ref.shape[0]
    load = pltpu.make_async_copy(rows_hbm, rows_ref, in_sems.at[0])
    load.start()
    piece = pltpu.make_async_copy(panels_hbm.at[0, 0, 0], piece_ref, in_sems.at[1])
    piece.start()
    points = points_ref[...]
    block = points >> 10
    offset = points & 1023
    target = (block & 15) * 8 + (offset >> 7)
    local = (block >> 4) * 128 + (offset & 127)
    wanted = (iota((128, count), 0) == target).astype(F32)
    earlier = (iota((count, count), 0) < iota((count, count), 1)).astype(F32).astype(BF16)
    seen = dot(wanted.astype(BF16), earlier, (1, 0))
    rank = jnp.sum(wanted * seen, axis=0, keepdims=True).astype(jnp.int32)
    slot = target * 8 + rank
    perm_ref[...] = (iota((count, count), 0) == slot).astype(F32).astype(BF16)
    part = iota((128, count), 0)
    digits = jnp.where(part < 10, jnp.where(part % 2 == 0, local >> 5, local & 31), 0).astype(F32).astype(BF16)
    ids = dot(perm_ref[...], digits, (1, 1))
    lane = iota((64, 128), 1)

    def both(value, first, odd):
        tiles = [value[first + 16 * z + 8 * odd : first + 16 * z + 8 * odd + 8] for z in range(4)]
        return jnp.concatenate([t for t in tiles for _ in range(2)], axis=0)

    kinds = [(64 * t, odd) for t in range(2) for odd in range(2)]
    shared = [both(ids, *kind) for kind in kinds]
    stores = []
    load.wait()
    for x in range(4):
        chunk = slice(x * 256, x * 256 + 256)
        part_rows = dot(perm_ref[chunk, :], rows_ref[...], (1, 0))
        out_ref[chunk, 384:1408] = part_rows.astype(BF16)
        if x == 0:
            head_ref[...] = part_rows[0:128]
        for y in range(4):
            rows = slice(x * 256 + y * 64, x * 256 + y * 64 + 64)
            mixed = ids[rows]
            for i in range(4):
                mixed = jnp.where(lane < 2 + 2 * i, mixed, shared[i])
            out_ref[rows, 256:384] = mixed.astype(BF16)
            for t in range(2):
                cut = None
                for p in range(4):
                    tile, at = (y, 32 * x) if p % 2 == 0 else (4 + x, 32 * y)
                    tile = both(head_ref[:, 128 * tile : 128 * tile + 128], *kinds[2 * t + p // 2])
                    moved = pltpu.roll(tile, (32 * p - at) % 128, 1) if (32 * p - at) % 128 else tile
                    cut = moved if cut is None else jnp.where(lane < 32 * p, cut, moved)
                out_ref[rows, t * 128 : t * 128 + 128] = cut.astype(BF16)
        span = pl.ds(x * 256, 256)
        stores.append(pltpu.make_async_copy(out_ref.at[span], out_hbm.at[span], out_sems.at[x]))
        stores[x].start()
    piece.wait()
    for store in stores:
        store.wait()


def compact_kernel(early_ref, own_ref, lead_ref, next_ref):
    count = early_ref.shape[0]
    pick = iota((8, 128), 0)
    lane = iota((8, 128), 1)
    weight = jnp.where(lane == 2 * pick, 32.0, jnp.where(lane == 2 * pick + 1, 1.0, 0.0))
    weight = jnp.where(pick < 5, weight, 0.0).astype(BF16)
    locals_ = dot(weight, early_ref[:, 256:384], (1, 1)).astype(jnp.int32)
    own_ref[...] = locals_
    place = iota((128, count), 0)
    for t, ref in enumerate((lead_ref, next_ref)):
        data = early_ref[:, 128 * t : 128 * t + 128]
        for odd in range(2):
            i = 1 + 2 * t + odd
            hit = (place == locals_[i : i + 1]).astype(F32).astype(BF16)
            found = dot(data, hit, (0, 1))[64 * odd : 64 * odd + 64]
            ref[:, 128 * odd : 128 * odd + 128] = found.astype(BF16)


def gather_cols(refs, scratch):
    z = lax.axis_index("col") // 2
    for ref, at in zip(refs, (z, z ^ 1, 3 - z, z ^ 2)):
        scratch[at] = ref[...]
    return jnp.concatenate([scratch[i] for i in range(4)], axis=1)


def first_kernel(p0, p1, p2, p3, inverse_ref, next_ref, own_ref, other_ref, solved_ref, second_ref, scratch):
    lead = gather_cols((p0, p1, p2, p3), scratch)
    solved = dot(lead, inverse_ref[...], (1, 1)).astype(BF16)
    solved_ref[...] = solved
    own = dot(solved, own_ref[...], (1, 1))
    other = dot(solved, other_ref[...], (1, 1))
    even = lax.axis_index("col") % 2 == 0
    low = jnp.where(even, own, other)
    high = jnp.where(even, other, own)
    second_ref[:, 0:128] = (next_ref[:, 0:128].astype(F32) - low).astype(BF16)
    second_ref[:, 128:256] = (next_ref[:, 128:256].astype(F32) - high).astype(BF16)


def second_kernel(p0, p1, p2, p3, inverse_ref, solved_ref, both_ref, scratch):
    second = gather_cols((p0, p1, p2, p3), scratch)
    solved = dot(second, inverse_ref[...], (1, 1)).astype(BF16)
    even = lax.axis_index("col") % 2 == 0
    both_ref[:, 0:1024] = jnp.where(even, solved_ref[0:32], solved_ref[32:64])
    both_ref[:, 1024:2048] = jnp.where(even, solved[0:32], solved[32:64])


def scatter_kernel(own_ref, arrived_hbm, out_hbm, hit_ref, rows_ref, out_ref, sems):
    count = hit_ref.shape[0]
    loads, stores = [], []
    for q in range(4):
        cols = pl.ds(q * 256, 256)
        loads.append(pltpu.make_async_copy(arrived_hbm.at[:, pl.ds(384 + q * 256, 256)], rows_ref.at[:, cols], sems.at[0, q]))
        loads[q].start()
    hit_ref[...] = (iota((count, count), 0) == own_ref[0:1]).astype(F32).astype(BF16)
    for q in range(4):
        cols = pl.ds(q * 256, 256)
        loads[q].wait()
        out_ref[:, cols] = dot(hit_ref[...], rows_ref[:, cols], (1, 0)).astype(BF16)
        stores.append(pltpu.make_async_copy(out_ref.at[:, cols], out_hbm.at[:, cols], sems.at[1, q]))
        stores[q].start()
    for store in stores:
        store.wait()


def place_of(kind):
    row = lax.axis_index("row")
    core = lax.axis_index("col") % 2
    x, y = row // 4, row % 4
    if kind:
        core = 1 - core
    return jnp.where(core == 0, x, y), jnp.where(core == 0, y, x), core


def load_kernel(source_hbm, first_ref, second_ref, sems):
    copies = [pltpu.make_async_copy(source_hbm.at[i], ref, sems.at[i]) for i, ref in enumerate((first_ref, second_ref))]
    for copy in copies:
        copy.start()
    for copy in copies:
        copy.wait()


def heads_of(panels_ref, head_ref):
    row = lax.axis_index("row")
    col = lax.axis_index("col")
    unit = (iota((128, 1024), 1) == iota((128, 1024), 0) + col * 128).astype(F32) * -1.0
    for p in range(2):
        kept = jnp.where(row < 2, 0.0, panels_ref[p, 0, 0].astype(F32))
        head_ref[p] = jnp.where(row == p, unit, kept).astype(BF16)


def product(panels_ref, head_ref, solved_t):
    s0 = solved_t[:, 0:1024]
    s1 = solved_t[:, 1024:2048]
    head = dot(head_ref[0], s0, (1, 1)) + dot(head_ref[1], s1, (1, 1))
    tail0 = panels_ref[0, 1:8, 0].reshape(896, 1024)
    tail1 = panels_ref[1, 1:8, 0].reshape(896, 1024)
    return head, dot(tail0, s0, (1, 1)) + dot(tail1, s1, (1, 1))


def update_kernel(blocks, *refs):
    count = sum(parts for _, _, parts in blocks)
    pieces = list(refs[:count])
    panels_ref, rows_hbm, out_hbm, solved_t, head_ref, in_ref, res_ref, sems = refs[count:]
    keep = jnp.where(lax.axis_index("row") < 2, 0.0, 1.0)
    draws, loads, stores = [], [], []
    for i, (kind, which, _) in enumerate(blocks):
        _, second, core = place_of(kind)
        at = second if which == 3 else swap(which, second)
        draws.append(pl.ds(pl.multiple_of(128 * (4 * core + at), 128), 128))
        loads.append(pltpu.make_async_copy(rows_hbm.at[:, :, :, draws[i]], in_ref.at[i], sems.at[0, i]))
        loads[i].start()
    heads_of(panels_ref, head_ref)
    for i, (kind, _, parts) in enumerate(blocks):
        first, _, _ = place_of(kind)
        places = (first, first ^ 1, 3 - first, first ^ 2)
        held = [pieces.pop(0) for _ in range(parts)]
        for j in range(4):
            at = pl.multiple_of(128 * i + 32 * places[j], 32)
            ref, j = (held[0], j) if parts == 1 else (held[j // 2], j % 2)
            solved_t[pl.ds(at, 32), :] = ref[j * 32 : j * 32 + 32, :]
        if i % 2 == 0:
            continue
        head, tail = product(panels_ref, head_ref, solved_t.at[128 * i - 128 : 128 * i + 128])
        for n in (i - 1, i):
            loads[n].wait()
            part = slice(128 * (n % 2), 128 * (n % 2) + 128)
            res_ref[n, 0, 0] = (in_ref[n, 0, 0].astype(F32) * keep - head[:, part]).astype(BF16)
            rest = in_ref[n, 1:8, 0].reshape(896, 128).astype(F32) - tail[:, part]
            res_ref[n, 1:8, 0] = rest.astype(BF16).reshape(7, 128, 128)
            stores.append(pltpu.make_async_copy(res_ref.at[n], out_hbm.at[:, :, :, draws[n]], sems.at[1, n]))
            stores[n].start()
    for store in stores:
        store.wait()


HBM = pl.BlockSpec(memory_space=pltpu.HBM)
ANY = pl.BlockSpec(memory_space=pl.ANY)


def launch(kernel, args, outs, scratch=(), specs=None, out_specs=None, aliases=None, limit=16, flops=0, moved=0):
    return pl.pallas_call(
        kernel,
        out_shape=[jax.ShapeDtypeStruct(s, d) for s, d in outs],
        grid=(1,),
        in_specs=specs or [VMEM] * len(args),
        out_specs=out_specs or [VMEM] * len(outs),
        scratch_shapes=list(scratch),
        input_output_aliases=aliases or {},
        compiler_params=pltpu.CompilerParams(vmem_limit_bytes=limit << 20),
        cost_estimate=pl.CostEstimate(flops=flops, bytes_accessed=moved, transcendentals=0),
    )(*args)


def spread_along(value, first, source):
    def move(kind):
        return along_first(kind) if first else along_second(kind)

    return [send(value, move(kind), source) for kind in range(3)]


def spread_first(piece):
    return spread_along(piece, True, lambda x, y, z, k: x == 0 and y == 1)


def spread_second(piece):
    return spread_along(piece, False, lambda x, y, z, k: y == 1 if k == 0 else x == 0)


def around_cols(piece):
    return (piece, send(piece, along_z(0)), send(piece, along_z(1)), send(piece, along_z(2)))


def update(blocks, pieces, panels, rows):
    return launch(
        functools.partial(update_kernel, blocks),
        (*pieces, panels, rows),
        [((8, 1, 128, 1024), BF16)],
        [
            pltpu.VMEM((128 * len(blocks), 2048), BF16),
            pltpu.VMEM((2, 128, 1024), BF16),
            pltpu.VMEM((len(blocks), 8, 1, 128, 128), BF16),
            pltpu.VMEM((len(blocks), 8, 1, 128, 128), BF16),
            pltpu.SemaphoreType.DMA((2, len(blocks))),
        ],
        specs=[VMEM] * (len(pieces) + 1) + [HBM],
        out_specs=[HBM],
        aliases={len(pieces) + 1: 0},
        limit=20,
        flops=1 << 30,
        moved=2 << 20,
    )[0]


def steps(b_ingest, source_point, panels, diag_inverse):
    row = lax.axis_index("row")
    ordered, piece = launch(
        order_kernel,
        (source_point.reshape(1, 1024), b_ingest, panels),
        [((1024, 1408), BF16), ((128, 1024), BF16)],
        [
            pltpu.VMEM((1024, 1024), BF16),
            pltpu.VMEM((1024, 1408), BF16),
            pltpu.VMEM((1024, 1024), BF16),
            pltpu.VMEM((128, 1024), F32),
            pltpu.SemaphoreType.DMA((2,)),
            pltpu.SemaphoreType.DMA((4,)),
        ],
        specs=[VMEM, HBM, HBM],
        out_specs=[HBM, VMEM],
        limit=63,
        flops=3 << 30,
        moved=5 << 20,
    )
    line = spread_first(piece)
    line = jnp.where(row == 1, piece, jnp.zeros_like(piece)) + line[0] + line[1] + line[2]
    plane = spread_second(line)
    arrived = lax.all_to_all(ordered.reshape(128, 8, 1408), AXES, split_axis=0, concat_axis=0, tiled=True)
    inverses, _ = lax.optimization_barrier((diag_inverse, ordered))
    inverses = launch(
        load_kernel,
        (inverses,),
        [((1024, 1024), BF16)] * 2,
        [pltpu.SemaphoreType.DMA((2,))],
        specs=[HBM],
        limit=6,
        moved=8 << 20,
    )
    arrived = arrived.reshape(1024, 1408)
    own, lead, follow = launch(
        compact_kernel,
        (arrived,),
        [((8, 1024), jnp.int32), ((64, 256), BF16), ((64, 256), BF16)],
        specs=[pl.BlockSpec((1024, 384), lambda i: (0, 0))],
        limit=12,
        flops=1 << 27,
        moved=1 << 20,
    )
    plane, inverses = lax.optimization_barrier((plane, inverses))
    link = line + plane[0] + plane[1] + plane[2]
    link_other = send(link, other_core)
    solved, second = launch(
        first_kernel,
        (*around_cols(lead), inverses[0], follow, link, link_other),
        [((64, 1024), BF16), ((64, 256), BF16)],
        [pltpu.VMEM((4, 64, 256), BF16)],
        limit=12,
        flops=1 << 28,
        moved=3 << 20,
    )
    (both,) = launch(
        second_kernel,
        (*around_cols(second), inverses[1], solved),
        [((32, 2048), BF16)],
        [pltpu.VMEM((4, 64, 256), BF16)],
        limit=12,
        flops=1 << 28,
        moved=3 << 20,
    )
    (rows,) = launch(
        scatter_kernel,
        (own, arrived),
        [((1024, 1024), BF16)],
        [pltpu.VMEM((1024, 1024), BF16)] * 3 + [pltpu.SemaphoreType.DMA((2, 4))],
        specs=[VMEM, HBM],
        out_specs=[HBM],
        limit=20,
        flops=1 << 31,
        moved=4 << 20,
    )
    rows = rows.reshape(8, 1, 128, 1024)
    line = [both] + [send(both, along_first(i)) for i in range(3)]
    line = jnp.concatenate(line, axis=0)
    side0, side1 = send(line, along_second(0)), send(line, along_second(1))
    far0, far1 = send(side1[0:64], along_second(0)), send(side0[64:128], along_second(1))
    line_other = send(line, other_core)
    side0_other, side1_other = send(side0, other_core), send(side1, other_core)
    far_other = send(far0, other_core), send(far1, other_core)
    rows = update(((0, 3, 1), (1, 3, 1)), (line, line_other), panels, rows)
    rows = update(((0, 0, 1), (0, 1, 1)), (side0, side1), panels, rows)
    blocks = ((1, 0, 1), (1, 1, 1), (0, 2, 2), (1, 2, 2))
    return update(blocks, (side0_other, side1_other, far0, far1, *far_other), panels, rows)


def solution(mesh):
    return jax.shard_map(
        steps,
        mesh=mesh,
        in_specs=(
            P(("row", "col"), None),
            P(("row", "col")),
            P(None, None, "row", "col", None),
            P(),
        ),
        out_specs=P(None, "row", "col", None),
        check_vma=False,
    )
```

```python
import functools

import jax
import jax.numpy as jnp
from jax import lax
from jax.experimental import pallas as pl
from jax.experimental.pallas import tpu as pltpu
from jax.sharding import PartitionSpec as P

AXES = ("row", "col")
BF16 = jnp.bfloat16
F32 = jnp.float32
VMEM = pl.BlockSpec(memory_space=pltpu.VMEM)


def device_id(x, y, z, k):
    return (x % 4 * 4 + y % 4) * 8 + z % 4 * 2 + k


def send(value, move, only=None):
    pairs = []
    for x in range(4):
        for y in range(4):
            for z in range(4):
                for k in range(2):
                    if only is None or only(x, y, z, k):
                        pairs.append((device_id(x, y, z, k), device_id(*move(x, y, z, k))))
    return lax.ppermute(value, AXES, pairs)


def swap(kind, at):
    return (at ^ 1, 3 - at, at ^ 2)[kind]


def along_first(kind):
    return lambda x, y, z, k: (swap(kind, x), y, z, k) if k == 0 else (x, swap(kind, y), z, k)


def along_second(kind):
    return lambda x, y, z, k: (x, swap(kind, y), z, k) if k == 0 else (swap(kind, x), y, z, k)


def along_z(kind):
    return lambda x, y, z, k: (x, y, swap(kind, z), k)


def other_core(x, y, z, k):
    return (x, y, z, 1 - k)


def iota(shape, axis):
    return lax.broadcasted_iota(jnp.int32, shape, axis)


def dot(a, b, contract):
    return lax.dot_general(a, b, ((contract[:1], contract[1:]), ((), ())), preferred_element_type=F32)


def order_kernel(points_ref, rows_hbm, out_hbm, rows_ref, out_ref, perm_ref, head_ref, in_sems, out_sems):
    count = rows_ref.shape[0]
    load = pltpu.make_async_copy(rows_hbm, rows_ref, in_sems.at[0])
    load.start()
    points = points_ref[...]
    block = points >> 10
    offset = points & 1023
    target = (block & 15) * 8 + (offset >> 7)
    local = (block >> 4) * 128 + (offset & 127)
    wanted = (iota((128, count), 0) == target).astype(F32)
    earlier = (iota((count, count), 0) < iota((count, count), 1)).astype(F32).astype(BF16)
    seen = dot(wanted.astype(BF16), earlier, (1, 0))
    rank = jnp.sum(wanted * seen, axis=0, keepdims=True).astype(jnp.int32)
    slot = target * 8 + rank
    perm_ref[...] = (iota((count, count), 0) == slot).astype(F32).astype(BF16)
    part = iota((128, count), 0)
    digits = jnp.where(part < 10, jnp.where(part % 2 == 0, local >> 5, local & 31), 0).astype(F32).astype(BF16)
    ids = dot(perm_ref[...], digits, (1, 1))
    lane = iota((64, 128), 1)

    def both(value, first, odd):
        tiles = [value[first + 16 * z + 8 * odd : first + 16 * z + 8 * odd + 8] for z in range(4)]
        return jnp.concatenate([t for t in tiles for _ in range(2)], axis=0)

    kinds = [(64 * t, odd) for t in range(2) for odd in range(2)]
    shared = [both(ids, *kind) for kind in kinds]
    stores = []
    load.wait()
    for x in range(4):
        chunk = slice(x * 256, x * 256 + 256)
        part_rows = dot(perm_ref[chunk, :], rows_ref[...], (1, 0))
        out_ref[chunk, 384:1408] = part_rows.astype(BF16)
        if x == 0:
            head_ref[...] = part_rows[0:128]
        for y in range(4):
            rows = slice(x * 256 + y * 64, x * 256 + y * 64 + 64)
            mixed = ids[rows]
            for i in range(4):
                mixed = jnp.where(lane < 2 + 2 * i, mixed, shared[i])
            out_ref[rows, 256:384] = mixed.astype(BF16)
            for t in range(2):
                cut = None
                for p in range(4):
                    tile, at = (y, 32 * x) if p % 2 == 0 else (4 + x, 32 * y)
                    tile = both(head_ref[:, 128 * tile : 128 * tile + 128], *kinds[2 * t + p // 2])
                    moved = pltpu.roll(tile, (32 * p - at) % 128, 1) if (32 * p - at) % 128 else tile
                    cut = moved if cut is None else jnp.where(lane < 32 * p, cut, moved)
                out_ref[rows, t * 128 : t * 128 + 128] = cut.astype(BF16)
        span = pl.ds(x * 256, 256)
        stores.append(pltpu.make_async_copy(out_ref.at[span], out_hbm.at[span], out_sems.at[x]))
        stores[x].start()
    for store in stores:
        store.wait()


def compact_kernel(early_ref, own_ref, lead_ref, next_ref):
    count = early_ref.shape[0]
    pick = iota((8, 128), 0)
    lane = iota((8, 128), 1)
    weight = jnp.where(lane == 2 * pick, 32.0, jnp.where(lane == 2 * pick + 1, 1.0, 0.0))
    weight = jnp.where(pick < 5, weight, 0.0).astype(BF16)
    locals_ = dot(weight, early_ref[:, 256:384], (1, 1)).astype(jnp.int32)
    own_ref[...] = locals_
    place = iota((128, count), 0)
    for t, ref in enumerate((lead_ref, next_ref)):
        data = early_ref[:, 128 * t : 128 * t + 128]
        for odd in range(2):
            i = 1 + 2 * t + odd
            hit = (place == locals_[i : i + 1]).astype(F32).astype(BF16)
            found = dot(data, hit, (0, 1))[64 * odd : 64 * odd + 64]
            ref[:, 128 * odd : 128 * odd + 128] = found.astype(BF16)


def gather_cols(refs, scratch):
    z = lax.axis_index("col") // 2
    for ref, at in zip(refs, (z, z ^ 1, 3 - z, z ^ 2)):
        scratch[at] = ref[...]
    return jnp.concatenate([scratch[i] for i in range(4)], axis=1)


def first_kernel(p0, p1, p2, p3, inverse_ref, next_ref, *refs):
    own_ref, other_ref = refs[0:4], refs[4:8]
    solved_ref, second_ref, scratch = refs[8:]
    lead = gather_cols((p0, p1, p2, p3), scratch)
    solved = dot(lead, inverse_ref[...], (1, 1)).astype(BF16)
    solved_ref[...] = solved
    own = dot(solved, sum(ref[...] for ref in own_ref), (1, 1))
    other = dot(solved, sum(ref[...] for ref in other_ref), (1, 1))
    even = lax.axis_index("col") % 2 == 0
    low = jnp.where(even, own, other)
    high = jnp.where(even, other, own)
    second_ref[:, 0:128] = (next_ref[:, 0:128].astype(F32) - low).astype(BF16)
    second_ref[:, 128:256] = (next_ref[:, 128:256].astype(F32) - high).astype(BF16)


def second_kernel(p0, p1, p2, p3, inverse_ref, solved_ref, both_ref, scratch):
    second = gather_cols((p0, p1, p2, p3), scratch)
    solved = dot(second, inverse_ref[...], (1, 1)).astype(BF16)
    even = lax.axis_index("col") % 2 == 0
    both_ref[:, 0:1024] = jnp.where(even, solved_ref[0:32], solved_ref[32:64])
    both_ref[:, 1024:2048] = jnp.where(even, solved[0:32], solved[32:64])


def scatter_kernel(own_ref, arrived_ref, out_ref, hit_ref, rows_ref, sem):
    count = arrived_ref.shape[0]
    copy = pltpu.make_async_copy(arrived_ref.at[:, 384:1408], rows_ref, sem)
    copy.start()
    hit_ref[...] = (iota((count, count), 0) == own_ref[0:1]).astype(F32).astype(BF16)
    copy.wait()
    for q in range(4):
        cols = slice(q * 256, q * 256 + 256)
        out_ref[:, cols] = dot(hit_ref[...], rows_ref[:, cols], (1, 0)).astype(BF16)


def place_of(kind):
    row = lax.axis_index("row")
    core = lax.axis_index("col") % 2
    x, y = row // 4, row % 4
    if kind:
        core = 1 - core
    return jnp.where(core == 0, x, y), jnp.where(core == 0, y, x), core


def load_kernel(source_hbm, first_ref, second_ref, sems):
    copies = [pltpu.make_async_copy(source_hbm.at[i], ref, sems.at[i]) for i, ref in enumerate((first_ref, second_ref))]
    for copy in copies:
        copy.start()
    for copy in copies:
        copy.wait()


def heads_of(panels_ref, head_ref):
    row = lax.axis_index("row")
    col = lax.axis_index("col")
    unit = (iota((128, 1024), 1) == iota((128, 1024), 0) + col * 128).astype(F32) * -1.0
    for p in range(2):
        kept = jnp.where(row < 2, 0.0, panels_ref[p, 0, 0].astype(F32))
        head_ref[p] = jnp.where(row == p, unit, kept).astype(BF16)


def product(panels_ref, head_ref, solved_t):
    s0 = solved_t[:, 0:1024]
    s1 = solved_t[:, 1024:2048]
    head = dot(head_ref[0], s0, (1, 1)) + dot(head_ref[1], s1, (1, 1))
    tail0 = panels_ref[0, 1:8, 0].reshape(896, 1024)
    tail1 = panels_ref[1, 1:8, 0].reshape(896, 1024)
    return head, dot(tail0, s0, (1, 1)) + dot(tail1, s1, (1, 1))


def updated_blocks(blocks, pieces, panels_ref, rows_ref, solved_t, head_ref, write):
    keep = jnp.where(lax.axis_index("row") < 2, 0.0, 1.0)
    heads_of(panels_ref, head_ref)
    pieces = list(pieces)
    for i, (kind, _, parts) in enumerate(blocks):
        first, _, _ = place_of(kind)
        places = (first, first ^ 1, 3 - first, first ^ 2)
        held = [pieces.pop(0) for _ in range(parts)]
        for j in range(4):
            at = pl.multiple_of(128 * i + 32 * places[j], 32)
            ref, j = (held[0], j) if parts == 1 else (held[j // 2], j % 2)
            solved_t[pl.ds(at, 32), :] = ref[j * 32 : j * 32 + 32, :]
        if i % 2 == 0:
            continue
        head, tail = product(panels_ref, head_ref, solved_t.at[128 * i - 128 : 128 * i + 128])
        for n in (i - 1, i):
            draws = draws_of(blocks[n])
            part = slice(128 * (n % 2), 128 * (n % 2) + 128)
            write(n, slice(0, 128), rows_ref[0:128, draws].astype(F32) * keep - head[:, part])
            write(n, slice(128, 1024), rows_ref[128:1024, draws].astype(F32) - tail[:, part])


def draws_of(block):
    kind, which, _ = block
    _, second, core = place_of(kind)
    at = second if which == 3 else swap(which, second)
    return pl.ds(pl.multiple_of(128 * (4 * core + at), 128), 128)


def update_kernel(blocks, *refs):
    count = sum(parts for _, _, parts in blocks)
    panels_ref, rows_ref, out_ref, solved_t, head_ref = refs[count:]

    def write(n, rows, value):
        out_ref[rows, 128 * n : 128 * n + 128] = value.astype(BF16)

    updated_blocks(blocks, refs[:count], panels_ref, rows_ref, solved_t, head_ref, write)


def last_kernel(before, blocks, *refs):
    count = sum(parts for _, _, parts in blocks)
    pieces, refs = refs[:count], refs[count:]
    done, (panels_ref, rows_ref, out_ref, solved_t, head_ref) = refs[: len(before)], refs[len(before) :]
    for held, ref in zip(before, done):
        for n, block in enumerate(held):
            out_ref[:, draws_of(block)] = ref[:, 128 * n : 128 * n + 128]

    def write(n, rows, value):
        out_ref[rows, draws_of(blocks[n])] = value.astype(BF16)

    updated_blocks(blocks, pieces, panels_ref, rows_ref, solved_t, head_ref, write)


HBM = pl.BlockSpec(memory_space=pltpu.HBM)
ANY = pl.BlockSpec(memory_space=pl.ANY)


def launch(kernel, args, outs, scratch=(), specs=None, out_specs=None, aliases=None, limit=16, flops=0, moved=0):
    return pl.pallas_call(
        kernel,
        out_shape=[jax.ShapeDtypeStruct(s, d) for s, d in outs],
        grid=(1,),
        in_specs=specs or [VMEM] * len(args),
        out_specs=out_specs or [VMEM] * len(outs),
        scratch_shapes=list(scratch),
        input_output_aliases=aliases or {},
        compiler_params=pltpu.CompilerParams(vmem_limit_bytes=int(limit * (1 << 20))),
        cost_estimate=pl.CostEstimate(flops=flops, bytes_accessed=moved, transcendentals=0),
    )(*args)


def spread_along(value, first, source):
    def move(kind):
        return along_first(kind) if first else along_second(kind)

    return [send(value, move(kind), source) for kind in range(3)]


def spread_first(piece):
    return spread_along(piece, True, lambda x, y, z, k: x == 0 and y == 1)


def spread_second(piece):
    return spread_along(piece, False, lambda x, y, z, k: y == 1 if k == 0 else x == 0)


def spread_third(line):
    return spread_along(line, True, lambda x, y, z, k: x == 0 if k == 0 else y == 1)


def around_cols(piece):
    return (piece, send(piece, along_z(0)), send(piece, along_z(1)), send(piece, along_z(2)))


def update(kernel, blocks, pieces, panels, rows, width):
    return launch(
        kernel,
        (*pieces, panels, rows),
        [((1024, width), BF16)],
        [pltpu.VMEM((128 * len(blocks), 2048), BF16), pltpu.VMEM((2, 128, 1024), BF16)],
        limit=16,
        flops=len(blocks) << 29,
        moved=2 << 20,
    )[0]


def steps(b_ingest, source_point, panels, diag_inverse):
    row = lax.axis_index("row")
    (ordered,) = launch(
        order_kernel,
        (source_point.reshape(1, 1024), b_ingest),
        [((1024, 1408), BF16)],
        [
            pltpu.VMEM((1024, 1024), BF16),
            pltpu.VMEM((1024, 1408), BF16),
            pltpu.VMEM((1024, 1024), BF16),
            pltpu.VMEM((128, 1024), F32),
            pltpu.SemaphoreType.DMA((1,)),
            pltpu.SemaphoreType.DMA((4,)),
        ],
        specs=[VMEM, HBM],
        out_specs=[HBM],
        limit=61.4,
        flops=3 << 30,
        moved=5 << 20,
    )
    piece = panels[0, 0, 0]
    line = spread_first(piece)
    line = jnp.where(row == 1, piece, jnp.zeros_like(piece)) + line[0] + line[1] + line[2]
    plane = [line] + spread_second(line)
    other = send(line, other_core)
    other = [other] + spread_third(other)
    arrived = lax.all_to_all(ordered.reshape(128, 8, 1408), AXES, split_axis=0, concat_axis=0, tiled=True)
    inverses, _ = lax.optimization_barrier((diag_inverse, ordered))
    inverses = launch(
        load_kernel,
        (inverses,),
        [((1024, 1024), BF16)] * 2,
        [pltpu.SemaphoreType.DMA((2,))],
        specs=[HBM],
        limit=6,
        moved=8 << 20,
    )
    arrived = arrived.reshape(1024, 1408)
    own, lead, follow = launch(
        compact_kernel,
        (arrived,),
        [((8, 1024), jnp.int32), ((64, 256), BF16), ((64, 256), BF16)],
        specs=[pl.BlockSpec((1024, 384), lambda i: (0, 0))],
        limit=12,
        flops=1 << 27,
        moved=1 << 20,
    )
    solved, second = launch(
        first_kernel,
        (*around_cols(lead), inverses[0], follow, *plane, *other),
        [((64, 1024), BF16), ((64, 256), BF16)],
        [pltpu.VMEM((4, 64, 256), BF16)],
        limit=12,
        flops=1 << 28,
        moved=3 << 20,
    )
    (both,) = launch(
        second_kernel,
        (*around_cols(second), inverses[1], solved),
        [((32, 2048), BF16)],
        [pltpu.VMEM((4, 64, 256), BF16)],
        limit=12,
        flops=1 << 28,
        moved=3 << 20,
    )
    (rows,) = launch(
        scatter_kernel,
        (own, arrived),
        [((1024, 1024), BF16)],
        [pltpu.VMEM((1024, 1024), BF16), pltpu.VMEM((1024, 1024), BF16), pltpu.SemaphoreType.DMA],
        specs=[VMEM, ANY],
        limit=20,
        flops=1 << 31,
        moved=4 << 20,
    )
    line = [both] + [send(both, along_first(i)) for i in range(3)]
    line = jnp.concatenate(line, axis=0)
    side0, side1 = send(line, along_second(0)), send(line, along_second(1))
    far0, far1 = send(side1[0:64], along_second(0)), send(side0[64:128], along_second(1))
    line_other = send(line, other_core)
    side0_other, side1_other = send(side0, other_core), send(side1, other_core)
    far_other = send(far0, other_core), send(far1, other_core)
    lines = ((0, 3, 1), (1, 3, 1))
    sides = ((0, 0, 1), (0, 1, 1))
    rest = ((1, 0, 1), (1, 1, 1), (0, 2, 2), (1, 2, 2))
    part0 = update(functools.partial(update_kernel, lines), lines, (line, line_other), panels, rows, 256)
    part1 = update(functools.partial(update_kernel, sides), sides, (side0, side1), panels, rows, 256)
    pieces = (side0_other, side1_other, far0, far1, *far_other, part0, part1)
    kernel = functools.partial(last_kernel, (lines, sides), rest)
    return update(kernel, rest, pieces, panels, rows, 1024).reshape(8, 1, 128, 1024)


def solution(mesh):
    return jax.shard_map(
        steps,
        mesh=mesh,
        in_specs=(
            P(("row", "col"), None),
            P(("row", "col")),
            P(None, None, "row", "col", None),
            P(),
        ),
        out_specs=P(None, "row", "col", None),
        check_vma=False,
    )
```

```python
import functools

import jax
import jax.numpy as jnp
from jax import lax
from jax.experimental import pallas as pl
from jax.experimental.pallas import tpu as pltpu
from jax.sharding import PartitionSpec as P

AXES = ("row", "col")
BF16 = jnp.bfloat16
F32 = jnp.float32
VMEM = pl.BlockSpec(memory_space=pltpu.VMEM)


def device_id(x, y, z, k):
    return (x % 4 * 4 + y % 4) * 8 + z % 4 * 2 + k


def send(value, move, only=None):
    pairs = []
    for x in range(4):
        for y in range(4):
            for z in range(4):
                for k in range(2):
                    if only is None or only(x, y, z, k):
                        pairs.append((device_id(x, y, z, k), device_id(*move(x, y, z, k))))
    return lax.ppermute(value, AXES, pairs)


def swap(kind, at):
    return (at ^ 1, 3 - at, at ^ 2)[kind]


def along_first(kind):
    return lambda x, y, z, k: (swap(kind, x), y, z, k) if k == 0 else (x, swap(kind, y), z, k)


def along_second(kind):
    return lambda x, y, z, k: (x, swap(kind, y), z, k) if k == 0 else (swap(kind, x), y, z, k)


def along_z(kind):
    return lambda x, y, z, k: (x, y, swap(kind, z), k)


def other_core(x, y, z, k):
    return (x, y, z, 1 - k)


def iota(shape, axis):
    return lax.broadcasted_iota(jnp.int32, shape, axis)


def dot(a, b, contract):
    return lax.dot_general(a, b, ((contract[:1], contract[1:]), ((), ())), preferred_element_type=F32)


def order_kernel(points_ref, rows_hbm, out_hbm, rows_ref, out_ref, perm_ref, head_ref, in_sems, out_sems):
    count = rows_ref.shape[0]
    load = pltpu.make_async_copy(rows_hbm, rows_ref, in_sems.at[0])
    load.start()
    points = points_ref[...]
    block = points >> 10
    offset = points & 1023
    target = (block & 15) * 8 + (offset >> 7)
    local = (block >> 4) * 128 + (offset & 127)
    wanted = (iota((128, count), 0) == target).astype(F32)
    earlier = (iota((count, count), 0) < iota((count, count), 1)).astype(F32).astype(BF16)
    seen = dot(wanted.astype(BF16), earlier, (1, 0))
    rank = jnp.sum(wanted * seen, axis=0, keepdims=True).astype(jnp.int32)
    slot = target * 8 + rank
    perm_ref[...] = (iota((count, count), 0) == slot).astype(F32).astype(BF16)
    part = iota((128, count), 0)
    digits = jnp.where(part < 10, jnp.where(part % 2 == 0, local >> 5, local & 31), 0).astype(F32).astype(BF16)
    ids = dot(perm_ref[...], digits, (1, 1))
    lane = iota((64, 128), 1)

    def both(value, first, odd):
        tiles = [value[first + 16 * z + 8 * odd : first + 16 * z + 8 * odd + 8] for z in range(4)]
        return jnp.concatenate([t for t in tiles for _ in range(2)], axis=0)

    kinds = [(64 * t, odd) for t in range(2) for odd in range(2)]
    shared = [both(ids, *kind) for kind in kinds]
    stores = []
    load.wait()
    for x in range(4):
        chunk = slice(x * 256, x * 256 + 256)
        part_rows = dot(perm_ref[chunk, :], rows_ref[...], (1, 0))
        out_ref[chunk, 384:1408] = part_rows.astype(BF16)
        if x == 0:
            head_ref[...] = part_rows[0:128]
        for y in range(4):
            rows = slice(x * 256 + y * 64, x * 256 + y * 64 + 64)
            mixed = ids[rows]
            for i in range(4):
                mixed = jnp.where(lane < 2 + 2 * i, mixed, shared[i])
            out_ref[rows, 256:384] = mixed.astype(BF16)
            for t in range(2):
                cut = None
                for p in range(4):
                    tile, at = (y, 32 * x) if p % 2 == 0 else (4 + x, 32 * y)
                    tile = both(head_ref[:, 128 * tile : 128 * tile + 128], *kinds[2 * t + p // 2])
                    moved = pltpu.roll(tile, (32 * p - at) % 128, 1) if (32 * p - at) % 128 else tile
                    cut = moved if cut is None else jnp.where(lane < 32 * p, cut, moved)
                out_ref[rows, t * 128 : t * 128 + 128] = cut.astype(BF16)
        span = pl.ds(x * 256, 256)
        stores.append(pltpu.make_async_copy(out_ref.at[span], out_hbm.at[span], out_sems.at[x]))
        stores[x].start()
    for store in stores:
        store.wait()


def compact_kernel(early_ref, own_ref, lead_ref, next_ref):
    count = early_ref.shape[0]
    pick = iota((8, 128), 0)
    lane = iota((8, 128), 1)
    weight = jnp.where(lane == 2 * pick, 32.0, jnp.where(lane == 2 * pick + 1, 1.0, 0.0))
    weight = jnp.where(pick < 5, weight, 0.0).astype(BF16)
    locals_ = dot(weight, early_ref[:, 256:384], (1, 1)).astype(jnp.int32)
    own_ref[...] = locals_
    place = iota((128, count), 0)
    for t, ref in enumerate((lead_ref, next_ref)):
        data = early_ref[:, 128 * t : 128 * t + 128]
        for odd in range(2):
            i = 1 + 2 * t + odd
            hit = (place == locals_[i : i + 1]).astype(F32).astype(BF16)
            found = dot(data, hit, (0, 1))[64 * odd : 64 * odd + 64]
            ref[:, 128 * odd : 128 * odd + 128] = found.astype(BF16)


def gather_cols(refs, scratch):
    z = lax.axis_index("col") // 2
    for ref, at in zip(refs, (z, z ^ 1, 3 - z, z ^ 2)):
        scratch[at] = ref[...]
    return jnp.concatenate([scratch[i] for i in range(4)], axis=1)


def first_kernel(p0, p1, p2, p3, inverse_ref, next_ref, own_ref, other_ref, solved_ref, second_ref, scratch):
    lead = gather_cols((p0, p1, p2, p3), scratch)
    solved = dot(lead, inverse_ref[...], (1, 1)).astype(BF16)
    solved_ref[...] = solved
    own = dot(solved, own_ref[...], (1, 1))
    other = dot(solved, other_ref[...], (1, 1))
    even = lax.axis_index("col") % 2 == 0
    low = jnp.where(even, own, other)
    high = jnp.where(even, other, own)
    second_ref[:, 0:128] = (next_ref[:, 0:128].astype(F32) - low).astype(BF16)
    second_ref[:, 128:256] = (next_ref[:, 128:256].astype(F32) - high).astype(BF16)


def second_kernel(p0, p1, p2, p3, inverse_ref, solved_ref, both_ref, scratch):
    second = gather_cols((p0, p1, p2, p3), scratch)
    solved = dot(second, inverse_ref[...], (1, 1)).astype(BF16)
    even = lax.axis_index("col") % 2 == 0
    both_ref[:, 0:1024] = jnp.where(even, solved_ref[0:32], solved_ref[32:64])
    both_ref[:, 1024:2048] = jnp.where(even, solved[0:32], solved[32:64])


def scatter_kernel(own_ref, arrived_ref, out_ref, hit_ref, rows_ref, sem):
    count = arrived_ref.shape[0]
    copy = pltpu.make_async_copy(arrived_ref.at[:, 384:1408], rows_ref, sem)
    copy.start()
    hit_ref[...] = (iota((count, count), 0) == own_ref[0:1]).astype(F32).astype(BF16)
    copy.wait()
    for q in range(4):
        cols = slice(q * 256, q * 256 + 256)
        out_ref[:, cols] = dot(hit_ref[...], rows_ref[:, cols], (1, 0)).astype(BF16)


def place_of(kind):
    row = lax.axis_index("row")
    core = lax.axis_index("col") % 2
    x, y = row // 4, row % 4
    if kind:
        core = 1 - core
    return jnp.where(core == 0, x, y), jnp.where(core == 0, y, x), core


def load_kernel(source_hbm, first_ref, second_ref, sems):
    copies = [pltpu.make_async_copy(source_hbm.at[i], ref, sems.at[i]) for i, ref in enumerate((first_ref, second_ref))]
    for copy in copies:
        copy.start()
    for copy in copies:
        copy.wait()


def heads_of(panels_ref, head_ref):
    row = lax.axis_index("row")
    col = lax.axis_index("col")
    unit = (iota((128, 1024), 1) == iota((128, 1024), 0) + col * 128).astype(F32) * -1.0
    for p in range(2):
        kept = jnp.where(row < 2, 0.0, panels_ref[p, 0, 0].astype(F32))
        head_ref[p] = jnp.where(row == p, unit, kept).astype(BF16)


def product(panels_ref, head_ref, solved_t):
    s0 = solved_t[:, 0:1024]
    s1 = solved_t[:, 1024:2048]
    head = dot(head_ref[0], s0, (1, 1)) + dot(head_ref[1], s1, (1, 1))
    tail0 = panels_ref[0, 1:8, 0].reshape(896, 1024)
    tail1 = panels_ref[1, 1:8, 0].reshape(896, 1024)
    return head, dot(tail0, s0, (1, 1)) + dot(tail1, s1, (1, 1))


def updated_blocks(blocks, pieces, panels_ref, rows_ref, solved_t, head_ref, write):
    keep = jnp.where(lax.axis_index("row") < 2, 0.0, 1.0)
    heads_of(panels_ref, head_ref)
    for i, (kind, _) in enumerate(blocks):
        first, _, _ = place_of(kind)
        for j, place in enumerate((first, first ^ 1, 3 - first, first ^ 2)):
            at = pl.multiple_of(128 * i + 32 * place, 32)
            solved_t[pl.ds(at, 32), :] = pieces[i][j * 32 : j * 32 + 32, :]
    head, tail = product(panels_ref, head_ref, solved_t)
    for n in range(2):
        draws = draws_of(blocks[n])
        part = slice(128 * n, 128 * n + 128)
        write(n, slice(0, 128), rows_ref[0:128, draws].astype(F32) * keep - head[:, part])
        write(n, slice(128, 1024), rows_ref[128:1024, draws].astype(F32) - tail[:, part])


def draws_of(block):
    kind, which = block
    _, second, core = place_of(kind)
    at = second if which == 3 else swap(which, second)
    return pl.ds(pl.multiple_of(128 * (4 * core + at), 128), 128)


def update_kernel(blocks, a_ref, b_ref, panels_ref, rows_ref, out_ref, solved_t, head_ref):
    def write(n, rows, value):
        out_ref[rows, 128 * n : 128 * n + 128] = value.astype(BF16)

    updated_blocks(blocks, (a_ref, b_ref), panels_ref, rows_ref, solved_t, head_ref, write)


def last_kernel(before, blocks, a_ref, b_ref, *refs):
    done, (panels_ref, rows_ref, out_ref, solved_t, head_ref) = refs[: len(before)], refs[len(before) :]
    for held, ref in zip(before, done):
        for n, block in enumerate(held):
            out_ref[:, draws_of(block)] = ref[:, 128 * n : 128 * n + 128]

    def write(n, rows, value):
        out_ref[rows, draws_of(blocks[n])] = value.astype(BF16)

    updated_blocks(blocks, (a_ref, b_ref), panels_ref, rows_ref, solved_t, head_ref, write)


HBM = pl.BlockSpec(memory_space=pltpu.HBM)
ANY = pl.BlockSpec(memory_space=pl.ANY)


def launch(kernel, args, outs, scratch=(), specs=None, out_specs=None, aliases=None, limit=16, flops=0, moved=0):
    return pl.pallas_call(
        kernel,
        out_shape=[jax.ShapeDtypeStruct(s, d) for s, d in outs],
        grid=(1,),
        in_specs=specs or [VMEM] * len(args),
        out_specs=out_specs or [VMEM] * len(outs),
        scratch_shapes=list(scratch),
        input_output_aliases=aliases or {},
        compiler_params=pltpu.CompilerParams(vmem_limit_bytes=int(limit * (1 << 20))),
        cost_estimate=pl.CostEstimate(flops=flops, bytes_accessed=moved, transcendentals=0),
    )(*args)


def spread_along(value, first, source):
    def move(kind):
        return along_first(kind) if first else along_second(kind)

    return [send(value, move(kind), source) for kind in range(3)]


def spread_first(piece):
    return spread_along(piece, True, lambda x, y, z, k: x == 0 and y == 1)


def spread_second(piece):
    return spread_along(piece, False, lambda x, y, z, k: y == 1 if k == 0 else x == 0)


def around_cols(piece):
    return (piece, send(piece, along_z(0)), send(piece, along_z(1)), send(piece, along_z(2)))


def update(kernel, blocks, pieces, panels, rows, width=256):
    return launch(
        functools.partial(kernel, blocks),
        (*pieces, panels, rows),
        [((1024, width), BF16)],
        [pltpu.VMEM((256, 2048), BF16), pltpu.VMEM((2, 128, 1024), BF16)],
        limit=16,
        flops=1 << 30,
        moved=2 << 20,
    )[0]


def steps(b_ingest, source_point, panels, diag_inverse):
    row = lax.axis_index("row")
    (ordered,) = launch(
        order_kernel,
        (source_point.reshape(1, 1024), b_ingest),
        [((1024, 1408), BF16)],
        [
            pltpu.VMEM((1024, 1024), BF16),
            pltpu.VMEM((1024, 1408), BF16),
            pltpu.VMEM((1024, 1024), BF16),
            pltpu.VMEM((128, 1024), F32),
            pltpu.SemaphoreType.DMA((1,)),
            pltpu.SemaphoreType.DMA((4,)),
        ],
        specs=[VMEM, HBM],
        out_specs=[HBM],
        limit=61.4,
        flops=3 << 30,
        moved=5 << 20,
    )
    piece = panels[0, 0, 0]
    line = spread_first(piece)
    line = jnp.where(row == 1, piece, jnp.zeros_like(piece)) + line[0] + line[1] + line[2]
    plane = spread_second(line)
    arrived = lax.all_to_all(ordered.reshape(128, 8, 1408), AXES, split_axis=0, concat_axis=0, tiled=True)
    inverses, _ = lax.optimization_barrier((diag_inverse, ordered))
    inverses = launch(
        load_kernel,
        (inverses,),
        [((1024, 1024), BF16)] * 2,
        [pltpu.SemaphoreType.DMA((2,))],
        specs=[HBM],
        limit=6,
        moved=8 << 20,
    )
    arrived = arrived.reshape(1024, 1408)
    own, lead, follow = launch(
        compact_kernel,
        (arrived,),
        [((8, 1024), jnp.int32), ((64, 256), BF16), ((64, 256), BF16)],
        specs=[pl.BlockSpec((1024, 384), lambda i: (0, 0))],
        limit=12,
        flops=1 << 27,
        moved=1 << 20,
    )
    line, plane, _ = lax.optimization_barrier((line, plane, own))
    link = line + plane[0] + plane[1] + plane[2]
    link_other = send(link, other_core)
    solved, second = launch(
        first_kernel,
        (*around_cols(lead), inverses[0], follow, link, link_other),
        [((64, 1024), BF16), ((64, 256), BF16)],
        [pltpu.VMEM((4, 64, 256), BF16)],
        limit=12,
        flops=1 << 28,
        moved=3 << 20,
    )
    (both,) = launch(
        second_kernel,
        (*around_cols(second), inverses[1], solved),
        [((32, 2048), BF16)],
        [pltpu.VMEM((4, 64, 256), BF16)],
        limit=12,
        flops=1 << 28,
        moved=3 << 20,
    )
    (rows,) = launch(
        scatter_kernel,
        (own, arrived),
        [((1024, 1024), BF16)],
        [pltpu.VMEM((1024, 1024), BF16), pltpu.VMEM((1024, 1024), BF16), pltpu.SemaphoreType.DMA],
        specs=[VMEM, ANY],
        limit=20,
        flops=1 << 31,
        moved=4 << 20,
    )
    line = [both] + [send(both, along_first(i)) for i in range(3)]
    line = jnp.concatenate(line, axis=0)
    side2, side0 = send(line, along_second(2)), send(line, along_second(0))
    side1 = send(line, along_second(1))
    line_other = send(line, other_core)
    side2_other, side0_other = send(side2, other_core), send(side0, other_core)
    side1_other = send(side1, other_core)
    lines = ((0, 3), (1, 3))
    owns = ((0, 2), (0, 0))
    others = ((1, 2), (1, 0))
    last = ((0, 1), (1, 1))
    part0 = update(update_kernel, lines, (line, line_other), panels, rows)
    part1 = update(update_kernel, owns, (side2, side0), panels, rows)
    part2 = update(update_kernel, others, (side2_other, side0_other), panels, rows)
    kernel = functools.partial(last_kernel, (lines, owns, others))
    pieces = (side1, side1_other, part0, part1, part2)
    return update(kernel, last, pieces, panels, rows, 1024).reshape(8, 1, 128, 1024)


def solution(mesh):
    return jax.shard_map(
        steps,
        mesh=mesh,
        in_specs=(
            P(("row", "col"), None),
            P(("row", "col")),
            P(None, None, "row", "col", None),
            P(),
        ),
        out_specs=P(None, "row", "col", None),
        check_vma=False,
    )
```

```python
import functools

import jax
import jax.numpy as jnp
from jax import lax
from jax.experimental import pallas as pl
from jax.experimental.pallas import tpu as pltpu
from jax.sharding import PartitionSpec as P

AXES = ("row", "col")
BF16 = jnp.bfloat16
F32 = jnp.float32
VMEM = pl.BlockSpec(memory_space=pltpu.VMEM)


def device_id(x, y, z, k):
    return (x % 4 * 4 + y % 4) * 8 + z % 4 * 2 + k


def send(value, move, only=None):
    pairs = []
    for x in range(4):
        for y in range(4):
            for z in range(4):
                for k in range(2):
                    if only is None or only(x, y, z, k):
                        pairs.append((device_id(x, y, z, k), device_id(*move(x, y, z, k))))
    return lax.ppermute(value, AXES, pairs)


def swap(kind, at):
    return (at ^ 1, 3 - at, at ^ 2)[kind]


def along_first(kind):
    return lambda x, y, z, k: (swap(kind, x), y, z, k) if k == 0 else (x, swap(kind, y), z, k)


def along_second(kind):
    return lambda x, y, z, k: (x, swap(kind, y), z, k) if k == 0 else (swap(kind, x), y, z, k)


def along_z(kind):
    return lambda x, y, z, k: (x, y, swap(kind, z), k)


def other_core(x, y, z, k):
    return (x, y, z, 1 - k)


def iota(shape, axis):
    return lax.broadcasted_iota(jnp.int32, shape, axis)


def dot(a, b, contract):
    return lax.dot_general(a, b, ((contract[:1], contract[1:]), ((), ())), preferred_element_type=F32)


def order_kernel(points_ref, rows_hbm, out_hbm, rows_ref, out_ref, perm_ref, head_ref, in_sems, out_sems):
    count = rows_ref.shape[0]
    load = pltpu.make_async_copy(rows_hbm, rows_ref, in_sems.at[0])
    load.start()
    points = points_ref[...]
    block = points >> 10
    offset = points & 1023
    target = (block & 15) * 8 + (offset >> 7)
    local = (block >> 4) * 128 + (offset & 127)
    wanted = (iota((128, count), 0) == target).astype(F32)
    earlier = (iota((count, count), 0) < iota((count, count), 1)).astype(F32).astype(BF16)
    seen = dot(wanted.astype(BF16), earlier, (1, 0))
    rank = jnp.sum(wanted * seen, axis=0, keepdims=True).astype(jnp.int32)
    slot = target * 8 + rank
    perm_ref[...] = (iota((count, count), 0) == slot).astype(F32).astype(BF16)
    part = iota((128, count), 0)
    digits = jnp.where(part < 10, jnp.where(part % 2 == 0, local >> 5, local & 31), 0).astype(F32).astype(BF16)
    ids = dot(perm_ref[...], digits, (1, 1))
    lane = iota((64, 128), 1)

    def both(value, first, odd):
        tiles = [value[first + 16 * z + 8 * odd : first + 16 * z + 8 * odd + 8] for z in range(4)]
        return jnp.concatenate([t for t in tiles for _ in range(2)], axis=0)

    kinds = [(64 * t, odd) for t in range(2) for odd in range(2)]
    shared = [both(ids, *kind) for kind in kinds]
    stores = []
    load.wait()
    for x in range(4):
        chunk = slice(x * 256, x * 256 + 256)
        part_rows = dot(perm_ref[chunk, :], rows_ref[...], (1, 0))
        out_ref[chunk, 384:1408] = part_rows.astype(BF16)
        if x == 0:
            head_ref[...] = part_rows[0:128]
        for y in range(4):
            rows = slice(x * 256 + y * 64, x * 256 + y * 64 + 64)
            mixed = ids[rows]
            for i in range(4):
                mixed = jnp.where(lane < 2 + 2 * i, mixed, shared[i])
            out_ref[rows, 256:384] = mixed.astype(BF16)
            for t in range(2):
                cut = None
                for p in range(4):
                    tile, at = (y, 32 * x) if p % 2 == 0 else (4 + x, 32 * y)
                    tile = both(head_ref[:, 128 * tile : 128 * tile + 128], *kinds[2 * t + p // 2])
                    moved = pltpu.roll(tile, (32 * p - at) % 128, 1) if (32 * p - at) % 128 else tile
                    cut = moved if cut is None else jnp.where(lane < 32 * p, cut, moved)
                out_ref[rows, t * 128 : t * 128 + 128] = cut.astype(BF16)
        span = pl.ds(x * 256, 256)
        stores.append(pltpu.make_async_copy(out_ref.at[span], out_hbm.at[span], out_sems.at[x]))
        stores[x].start()
    for store in stores:
        store.wait()


def compact_kernel(early_ref, own_ref, lead_ref, next_ref):
    count = early_ref.shape[0]
    pick = iota((8, 128), 0)
    lane = iota((8, 128), 1)
    weight = jnp.where(lane == 2 * pick, 32.0, jnp.where(lane == 2 * pick + 1, 1.0, 0.0))
    weight = jnp.where(pick < 5, weight, 0.0).astype(BF16)
    locals_ = dot(weight, early_ref[:, 256:384], (1, 1)).astype(jnp.int32)
    own_ref[...] = locals_
    place = iota((128, count), 0)
    for t, ref in enumerate((lead_ref, next_ref)):
        data = early_ref[:, 128 * t : 128 * t + 128]
        for odd in range(2):
            i = 1 + 2 * t + odd
            hit = (place == locals_[i : i + 1]).astype(F32).astype(BF16)
            found = dot(data, hit, (0, 1))[64 * odd : 64 * odd + 64]
            ref[:, 128 * odd : 128 * odd + 128] = found.astype(BF16)


def gather_cols(refs, scratch):
    z = lax.axis_index("col") // 2
    for ref, at in zip(refs, (z, z ^ 1, 3 - z, z ^ 2)):
        scratch[at] = ref[...]
    return jnp.concatenate([scratch[i] for i in range(4)], axis=1)


def first_kernel(p0, p1, p2, p3, inverse_ref, next_ref, own_ref, other_ref, solved_ref, second_ref, scratch):
    lead = gather_cols((p0, p1, p2, p3), scratch)
    solved = dot(lead, inverse_ref[...], (1, 1)).astype(BF16)
    solved_ref[...] = solved
    own = dot(solved, own_ref[...], (1, 1))
    other = dot(solved, other_ref[...], (1, 1))
    even = lax.axis_index("col") % 2 == 0
    low = jnp.where(even, own, other)
    high = jnp.where(even, other, own)
    second_ref[:, 0:128] = (next_ref[:, 0:128].astype(F32) - low).astype(BF16)
    second_ref[:, 128:256] = (next_ref[:, 128:256].astype(F32) - high).astype(BF16)


def second_kernel(p0, p1, p2, p3, inverse_ref, solved_ref, both_ref, scratch):
    second = gather_cols((p0, p1, p2, p3), scratch)
    solved = dot(second, inverse_ref[...], (1, 1)).astype(BF16)
    even = lax.axis_index("col") % 2 == 0
    both_ref[:, 0:1024] = jnp.where(even, solved_ref[0:32], solved_ref[32:64])
    both_ref[:, 1024:2048] = jnp.where(even, solved[0:32], solved[32:64])


def scatter_kernel(own_ref, arrived_ref, out_ref, hit_ref, rows_ref, sem):
    count = arrived_ref.shape[0]
    copy = pltpu.make_async_copy(arrived_ref.at[:, 384:1408], rows_ref, sem)
    copy.start()
    hit_ref[...] = (iota((count, count), 0) == own_ref[0:1]).astype(F32).astype(BF16)
    copy.wait()
    for q in range(4):
        cols = slice(q * 256, q * 256 + 256)
        out_ref[:, cols] = dot(hit_ref[...], rows_ref[:, cols], (1, 0)).astype(BF16)


def place_of(kind):
    row = lax.axis_index("row")
    core = lax.axis_index("col") % 2
    x, y = row // 4, row % 4
    if kind:
        core = 1 - core
    return jnp.where(core == 0, x, y), jnp.where(core == 0, y, x), core


def load_kernel(source_hbm, first_ref, second_ref, sems):
    copies = [pltpu.make_async_copy(source_hbm.at[i], ref, sems.at[i]) for i, ref in enumerate((first_ref, second_ref))]
    for copy in copies:
        copy.start()
    for copy in copies:
        copy.wait()


def heads_of(panels_ref, head_ref):
    row = lax.axis_index("row")
    col = lax.axis_index("col")
    unit = (iota((128, 1024), 1) == iota((128, 1024), 0) + col * 128).astype(F32) * -1.0
    for p in range(2):
        kept = jnp.where(row < 2, 0.0, panels_ref[p, 0, 0].astype(F32))
        head_ref[p] = jnp.where(row == p, unit, kept).astype(BF16)


def product(panels_ref, head_ref, solved_t):
    s0 = solved_t[:, 0:1024]
    s1 = solved_t[:, 1024:2048]
    head = dot(head_ref[0], s0, (1, 1)) + dot(head_ref[1], s1, (1, 1))
    tail0 = panels_ref[0, 1:8, 0].reshape(896, 1024)
    tail1 = panels_ref[1, 1:8, 0].reshape(896, 1024)
    return head, dot(tail0, s0, (1, 1)) + dot(tail1, s1, (1, 1))


def updated_blocks(blocks, pieces, panels_ref, rows_ref, solved_t, head_ref, write):
    keep = jnp.where(lax.axis_index("row") < 2, 0.0, 1.0)
    heads_of(panels_ref, head_ref)
    place_blocks(blocks, pieces, solved_t)
    head, tail = product(panels_ref, head_ref, solved_t)
    for n in range(2):
        draws = draws_of(blocks[n])
        part = slice(128 * n, 128 * n + 128)
        write(n, slice(0, 128), rows_ref[0:128, draws].astype(F32) * keep - head[:, part])
        write(n, slice(128, 1024), rows_ref[128:1024, draws].astype(F32) - tail[:, part])


def place_blocks(blocks, pieces, solved_t):
    for i, (kind, _) in enumerate(blocks):
        first, _, _ = place_of(kind)
        for j, place in enumerate((first, first ^ 1, 3 - first, first ^ 2)):
            at = pl.multiple_of(128 * i + 32 * place, 32)
            solved_t[pl.ds(at, 32), :] = pieces[i][j * 32 : j * 32 + 32, :]


def draws_of(block):
    kind, which = block
    _, second, core = place_of(kind)
    at = second if which == 3 else swap(which, second)
    return pl.ds(pl.multiple_of(128 * (4 * core + at), 128), 128)


def update_kernel(blocks, a_ref, b_ref, panels_ref, rows_ref, out_ref, solved_t, head_ref):
    def write(n, rows, value):
        out_ref[rows, 128 * n : 128 * n + 128] = value.astype(BF16)

    updated_blocks(blocks, (a_ref, b_ref), panels_ref, rows_ref, solved_t, head_ref, write)


def last_kernel(before, blocks, a_ref, b_ref, *refs):
    done, (panels_ref, rows_ref, out_hbm, solved_t, head_ref, out_ref, sems) = refs[: len(before)], refs[len(before) :]
    keep = jnp.where(lax.axis_index("row") < 2, 0.0, 1.0)
    heads_of(panels_ref, head_ref)
    place_blocks(blocks, (a_ref, b_ref), solved_t)
    stores = []
    for q in range(4):
        value = 0.0
        for p in range(2):
            solved = solved_t[:, p * 1024 : p * 1024 + 1024]
            if q == 0:
                factor = jnp.concatenate([head_ref[p], panels_ref[p, 1, 0]], axis=0)
            else:
                factor = panels_ref[p, 2 * q : 2 * q + 2, 0].reshape(256, 1024)
            value = value + dot(factor, solved, (1, 1))
        span = slice(q * 256, q * 256 + 256)
        for held, ref in zip(before, done):
            for n, block in enumerate(held):
                out_ref[span, draws_of(block)] = ref[span, 128 * n : 128 * n + 128]
        for n in range(2):
            draws = draws_of(blocks[n])
            rest = rows_ref[span, draws].astype(F32)
            if q == 0:
                rest = rest * jnp.where(iota((256, 128), 0) < 128, keep, 1.0)
            out_ref[span, draws] = (rest - value[:, 128 * n : 128 * n + 128]).astype(BF16)
        stores.append(pltpu.make_async_copy(out_ref.at[pl.ds(q * 256, 256)], out_hbm.at[pl.ds(q * 256, 256)], sems.at[q]))
        stores[q].start()
    for store in stores:
        store.wait()


HBM = pl.BlockSpec(memory_space=pltpu.HBM)
ANY = pl.BlockSpec(memory_space=pl.ANY)


def launch(kernel, args, outs, scratch=(), specs=None, out_specs=None, aliases=None, limit=16, flops=0, moved=0):
    return pl.pallas_call(
        kernel,
        out_shape=[jax.ShapeDtypeStruct(s, d) for s, d in outs],
        grid=(1,),
        in_specs=specs or [VMEM] * len(args),
        out_specs=out_specs or [VMEM] * len(outs),
        scratch_shapes=list(scratch),
        input_output_aliases=aliases or {},
        compiler_params=pltpu.CompilerParams(vmem_limit_bytes=int(limit * (1 << 20))),
        cost_estimate=pl.CostEstimate(flops=flops, bytes_accessed=moved, transcendentals=0),
    )(*args)


def spread_along(value, first, source):
    def move(kind):
        return along_first(kind) if first else along_second(kind)

    return [send(value, move(kind), source) for kind in range(3)]


def spread_first(piece):
    moved = [send(piece, along_first(kind)) for kind in range(3)]
    first, second, core = place_of(0)
    source = jnp.where(core == 0, 0, 1)
    line = jnp.where(first ^ 1 == source, moved[0], jnp.where(3 - first == source, moved[1], moved[2]))
    line = jnp.where(first == source, piece, line)
    return jnp.where(second == 1 - source, line, jnp.zeros_like(line))


def spread_second(piece):
    return spread_along(piece, False, lambda x, y, z, k: y == 1 if k == 0 else x == 0)


def around_cols(piece):
    return (piece, send(piece, along_z(0)), send(piece, along_z(1)), send(piece, along_z(2)))


def update(kernel, blocks, pieces, panels, rows, width=256, extra=(), out=VMEM):
    return launch(
        functools.partial(kernel, blocks),
        (*pieces, panels, rows),
        [((1024, width), BF16)],
        [pltpu.VMEM((256, 2048), BF16), pltpu.VMEM((2, 128, 1024), BF16), *extra],
        out_specs=[out],
        limit=16,
        flops=1 << 30,
        moved=2 << 20,
    )[0]


def steps(b_ingest, source_point, panels, diag_inverse):
    (ordered,) = launch(
        order_kernel,
        (source_point.reshape(1, 1024), b_ingest),
        [((1024, 1408), BF16)],
        [
            pltpu.VMEM((1024, 1024), BF16),
            pltpu.VMEM((1024, 1408), BF16),
            pltpu.VMEM((1024, 1024), BF16),
            pltpu.VMEM((128, 1024), F32),
            pltpu.SemaphoreType.DMA((1,)),
            pltpu.SemaphoreType.DMA((4,)),
        ],
        specs=[VMEM, HBM],
        out_specs=[HBM],
        limit=61.4,
        flops=3 << 30,
        moved=5 << 20,
    )
    piece = panels[0, 0, 0]
    line = spread_first(piece)
    plane = spread_second(line)
    arrived = lax.all_to_all(ordered.reshape(128, 8, 1408), AXES, split_axis=0, concat_axis=0, tiled=True)
    inverses, _ = lax.optimization_barrier((diag_inverse, ordered))
    inverses = launch(
        load_kernel,
        (inverses,),
        [((1024, 1024), BF16)] * 2,
        [pltpu.SemaphoreType.DMA((2,))],
        specs=[HBM],
        limit=6,
        moved=8 << 20,
    )
    arrived = arrived.reshape(1024, 1408)
    own, lead, follow = launch(
        compact_kernel,
        (arrived,),
        [((8, 1024), jnp.int32), ((64, 256), BF16), ((64, 256), BF16)],
        specs=[pl.BlockSpec((1024, 384), lambda i: (0, 0))],
        limit=12,
        flops=1 << 27,
        moved=1 << 20,
    )
    line, plane, _ = lax.optimization_barrier((line, plane, own))
    link = line + plane[0] + plane[1] + plane[2]
    link_other = send(link, other_core)
    solved, second = launch(
        first_kernel,
        (*around_cols(lead), inverses[0], follow, link, link_other),
        [((64, 1024), BF16), ((64, 256), BF16)],
        [pltpu.VMEM((4, 64, 256), BF16)],
        limit=12,
        flops=1 << 28,
        moved=3 << 20,
    )
    (both,) = launch(
        second_kernel,
        (*around_cols(second), inverses[1], solved),
        [((32, 2048), BF16)],
        [pltpu.VMEM((4, 64, 256), BF16)],
        limit=12,
        flops=1 << 28,
        moved=3 << 20,
    )
    (rows,) = launch(
        scatter_kernel,
        (own, arrived),
        [((1024, 1024), BF16)],
        [pltpu.VMEM((1024, 1024), BF16), pltpu.VMEM((1024, 1024), BF16), pltpu.SemaphoreType.DMA],
        specs=[VMEM, ANY],
        limit=20,
        flops=1 << 31,
        moved=4 << 20,
    )
    line = [both] + [send(both, along_first(i)) for i in range(3)]
    line = jnp.concatenate(line, axis=0)
    side2, side0 = send(line, along_second(2)), send(line, along_second(0))
    side1 = send(line, along_second(1))
    line_other = send(line, other_core)
    side2_other, side0_other = send(side2, other_core), send(side0, other_core)
    side1_other = send(side1, other_core)
    lines = ((0, 3), (1, 3))
    owns = ((0, 2), (0, 0))
    others = ((1, 2), (1, 0))
    last = ((0, 1), (1, 1))
    part0 = update(update_kernel, lines, (line, line_other), panels, rows)
    part1 = update(update_kernel, owns, (side2, side0), panels, rows)
    part2 = update(update_kernel, others, (side2_other, side0_other), panels, rows)
    kernel = functools.partial(last_kernel, (lines, owns, others))
    pieces = (side1, side1_other, part0, part1, part2)
    extra = (pltpu.VMEM((1024, 1024), BF16), pltpu.SemaphoreType.DMA((4,)))
    updated = update(kernel, last, pieces, panels, rows, 1024, extra, HBM)
    return updated.reshape(8, 1, 128, 1024)


def solution(mesh):
    return jax.shard_map(
        steps,
        mesh=mesh,
        in_specs=(
            P(("row", "col"), None),
            P(("row", "col")),
            P(None, None, "row", "col", None),
            P(),
        ),
        out_specs=P(None, "row", "col", None),
        check_vma=False,
    )
```

```python
import functools

import jax
import jax.numpy as jnp
from jax import lax
from jax.experimental import pallas as pl
from jax.experimental.pallas import tpu as pltpu
from jax.sharding import PartitionSpec as P

AXES = ("row", "col")
BF16 = jnp.bfloat16
F32 = jnp.float32
VMEM = pl.BlockSpec(memory_space=pltpu.VMEM)


def device_id(x, y, z, k):
    return (x % 4 * 4 + y % 4) * 8 + z % 4 * 2 + k


def send(value, move, only=None):
    pairs = []
    for x in range(4):
        for y in range(4):
            for z in range(4):
                for k in range(2):
                    if only is None or only(x, y, z, k):
                        pairs.append((device_id(x, y, z, k), device_id(*move(x, y, z, k))))
    return lax.ppermute(value, AXES, pairs)


def swap(kind, at):
    return (at ^ 1, 3 - at, at ^ 2)[kind]


def along_first(kind):
    return lambda x, y, z, k: (swap(kind, x), y, z, k) if k == 0 else (x, swap(kind, y), z, k)


def along_second(kind):
    return lambda x, y, z, k: (x, swap(kind, y), z, k) if k == 0 else (swap(kind, x), y, z, k)


def along_z(kind):
    return lambda x, y, z, k: (x, y, swap(kind, z), k)


def other_core(x, y, z, k):
    return (x, y, z, 1 - k)


def iota(shape, axis):
    return lax.broadcasted_iota(jnp.int32, shape, axis)


def dot(a, b, contract):
    return lax.dot_general(a, b, ((contract[:1], contract[1:]), ((), ())), preferred_element_type=F32)


def order_kernel(points_ref, rows_hbm, out_hbm, rows_ref, out_ref, perm_ref, head_ref, in_sems, out_sems):
    count = rows_ref.shape[0]
    load = pltpu.make_async_copy(rows_hbm, rows_ref, in_sems.at[0])
    load.start()
    points = points_ref[...]
    block = points >> 10
    offset = points & 1023
    target = (block & 15) * 8 + (offset >> 7)
    local = (block >> 4) * 128 + (offset & 127)
    wanted = (iota((128, count), 0) == target).astype(F32)
    earlier = (iota((count, count), 0) < iota((count, count), 1)).astype(F32).astype(BF16)
    seen = dot(wanted.astype(BF16), earlier, (1, 0))
    rank = jnp.sum(wanted * seen, axis=0, keepdims=True).astype(jnp.int32)
    slot = target * 8 + rank
    perm_ref[...] = (iota((count, count), 0) == slot).astype(F32).astype(BF16)
    part = iota((128, count), 0)
    digits = jnp.where(part < 10, jnp.where(part % 2 == 0, local >> 5, local & 31), 0).astype(F32).astype(BF16)
    ids = dot(perm_ref[...], digits, (1, 1))
    lane = iota((64, 128), 1)

    def both(value, first, odd):
        tiles = [value[first + 16 * z + 8 * odd : first + 16 * z + 8 * odd + 8] for z in range(4)]
        return jnp.concatenate([t for t in tiles for _ in range(2)], axis=0)

    kinds = [(64 * t, odd) for t in range(2) for odd in range(2)]
    shared = [both(ids, *kind) for kind in kinds]
    stores = []
    load.wait()
    for x in range(4):
        chunk = slice(x * 256, x * 256 + 256)
        part_rows = dot(perm_ref[chunk, :], rows_ref[...], (1, 0))
        out_ref[chunk, 384:1408] = part_rows.astype(BF16)
        if x == 0:
            head_ref[...] = part_rows[0:128]
        for y in range(4):
            rows = slice(x * 256 + y * 64, x * 256 + y * 64 + 64)
            mixed = ids[rows]
            for i in range(4):
                mixed = jnp.where(lane < 2 + 2 * i, mixed, shared[i])
            out_ref[rows, 256:384] = mixed.astype(BF16)
            for t in range(2):
                cut = None
                for p in range(4):
                    tile, at = (y, 32 * x) if p % 2 == 0 else (4 + x, 32 * y)
                    tile = both(head_ref[:, 128 * tile : 128 * tile + 128], *kinds[2 * t + p // 2])
                    moved = pltpu.roll(tile, (32 * p - at) % 128, 1) if (32 * p - at) % 128 else tile
                    cut = moved if cut is None else jnp.where(lane < 32 * p, cut, moved)
                out_ref[rows, t * 128 : t * 128 + 128] = cut.astype(BF16)
        span = pl.ds(x * 256, 256)
        stores.append(pltpu.make_async_copy(out_ref.at[span], out_hbm.at[span], out_sems.at[x]))
        stores[x].start()
    for store in stores:
        store.wait()


def compact_kernel(early_ref, own_ref, lead_ref, next_ref):
    count = early_ref.shape[0]
    pick = iota((8, 128), 0)
    lane = iota((8, 128), 1)
    weight = jnp.where(lane == 2 * pick, 32.0, jnp.where(lane == 2 * pick + 1, 1.0, 0.0))
    weight = jnp.where(pick < 5, weight, 0.0).astype(BF16)
    locals_ = dot(weight, early_ref[:, 256:384], (1, 1)).astype(jnp.int32)
    own_ref[...] = locals_
    place = iota((128, count), 0)
    for t, ref in enumerate((lead_ref, next_ref)):
        data = early_ref[:, 128 * t : 128 * t + 128]
        for odd in range(2):
            i = 1 + 2 * t + odd
            hit = (place == locals_[i : i + 1]).astype(F32).astype(BF16)
            found = dot(data, hit, (0, 1))[64 * odd : 64 * odd + 64]
            ref[:, 128 * odd : 128 * odd + 128] = found.astype(BF16)


def gather_cols(refs, scratch):
    z = lax.axis_index("col") // 2
    for ref, at in zip(refs, (z, z ^ 1, 3 - z, z ^ 2)):
        scratch[at] = ref[...]
    return jnp.concatenate([scratch[i] for i in range(4)], axis=1)


def first_kernel(p0, p1, p2, p3, inverse_ref, next_ref, own_ref, other_ref, solved_ref, second_ref, scratch):
    lead = gather_cols((p0, p1, p2, p3), scratch)
    solved = dot(lead, inverse_ref[...], (1, 1)).astype(BF16)
    solved_ref[...] = solved
    own = dot(solved, own_ref[...], (1, 1))
    other = dot(solved, other_ref[...], (1, 1))
    even = lax.axis_index("col") % 2 == 0
    low = jnp.where(even, own, other)
    high = jnp.where(even, other, own)
    second_ref[:, 0:128] = (next_ref[:, 0:128].astype(F32) - low).astype(BF16)
    second_ref[:, 128:256] = (next_ref[:, 128:256].astype(F32) - high).astype(BF16)


def second_kernel(p0, p1, p2, p3, inverse_ref, solved_ref, both_ref, scratch):
    second = gather_cols((p0, p1, p2, p3), scratch)
    solved = dot(second, inverse_ref[...], (1, 1)).astype(BF16)
    even = lax.axis_index("col") % 2 == 0
    both_ref[:, 0:1024] = jnp.where(even, solved_ref[0:32], solved_ref[32:64])
    both_ref[:, 1024:2048] = jnp.where(even, solved[0:32], solved[32:64])


def scatter_kernel(own_ref, arrived_ref, out_ref, hit_ref, rows_ref, sem):
    count = arrived_ref.shape[0]
    copy = pltpu.make_async_copy(arrived_ref.at[:, 384:1408], rows_ref, sem)
    copy.start()
    hit_ref[...] = (iota((count, count), 0) == own_ref[0:1]).astype(F32).astype(BF16)
    copy.wait()
    for q in range(4):
        cols = slice(q * 256, q * 256 + 256)
        out_ref[:, cols] = dot(hit_ref[...], rows_ref[:, cols], (1, 0)).astype(BF16)


def place_of(kind):
    row = lax.axis_index("row")
    core = lax.axis_index("col") % 2
    x, y = row // 4, row % 4
    if kind:
        core = 1 - core
    return jnp.where(core == 0, x, y), jnp.where(core == 0, y, x), core


def load_kernel(source_hbm, first_ref, second_ref, sems):
    copies = [pltpu.make_async_copy(source_hbm.at[i], ref, sems.at[i]) for i, ref in enumerate((first_ref, second_ref))]
    for copy in copies:
        copy.start()
    for copy in copies:
        copy.wait()


def heads_of(panels_ref, head_ref):
    row = lax.axis_index("row")
    col = lax.axis_index("col")
    unit = (iota((128, 1024), 1) == iota((128, 1024), 0) + col * 128).astype(F32) * -1.0
    for p in range(2):
        kept = jnp.where(row < 2, 0.0, panels_ref[p, 0, 0].astype(F32))
        head_ref[p] = jnp.where(row == p, unit, kept).astype(BF16)


def product(panels_ref, head_ref, solved_t):
    s0 = solved_t[:, 0:1024]
    s1 = solved_t[:, 1024:2048]
    head = dot(head_ref[0], s0, (1, 1)) + dot(head_ref[1], s1, (1, 1))
    tail0 = panels_ref[0, 1:8, 0].reshape(896, 1024)
    tail1 = panels_ref[1, 1:8, 0].reshape(896, 1024)
    return head, dot(tail0, s0, (1, 1)) + dot(tail1, s1, (1, 1))


def updated_blocks(blocks, pieces, panels_ref, rows_ref, solved_t, head_ref, write):
    keep = jnp.where(lax.axis_index("row") < 2, 0.0, 1.0)
    heads_of(panels_ref, head_ref)
    place_blocks(blocks, pieces, solved_t)
    head, tail = product(panels_ref, head_ref, solved_t)
    for n in range(2):
        draws = draws_of(blocks[n])
        part = slice(128 * n, 128 * n + 128)
        write(n, slice(0, 128), rows_ref[0:128, draws].astype(F32) * keep - head[:, part])
        write(n, slice(128, 1024), rows_ref[128:1024, draws].astype(F32) - tail[:, part])


def place_blocks(blocks, pieces, solved_t):
    for i, (kind, _) in enumerate(blocks):
        first, _, _ = place_of(kind)
        for j, place in enumerate((first, first ^ 1, 3 - first, first ^ 2)):
            at = pl.multiple_of(128 * i + 32 * place, 32)
            solved_t[pl.ds(at, 32), :] = pieces[i][j * 32 : j * 32 + 32, :]


def draws_of(block):
    kind, which = block
    _, second, core = place_of(kind)
    at = second if which == 3 else swap(which, second)
    return pl.ds(pl.multiple_of(128 * (4 * core + at), 128), 128)


def update_kernel(blocks, a_ref, b_ref, panels_ref, rows_ref, out_ref, solved_t, head_ref):
    def write(n, rows, value):
        out_ref[rows, 128 * n : 128 * n + 128] = value.astype(BF16)

    updated_blocks(blocks, (a_ref, b_ref), panels_ref, rows_ref, solved_t, head_ref, write)


def last_kernel(before, blocks, a_ref, b_ref, *refs):
    done, (panels_ref, rows_ref, out_hbm, solved_t, head_ref, out_ref, sems) = refs[: len(before)], refs[len(before) :]
    keep = jnp.where(lax.axis_index("row") < 2, 0.0, 1.0)
    heads_of(panels_ref, head_ref)
    place_blocks(blocks, (a_ref, b_ref), solved_t)
    stores = []
    for q in range(4):
        value = 0.0
        for p in range(2):
            solved = solved_t[:, p * 1024 : p * 1024 + 1024]
            if q == 0:
                factor = jnp.concatenate([head_ref[p], panels_ref[p, 1, 0]], axis=0)
            else:
                factor = panels_ref[p, 2 * q : 2 * q + 2, 0].reshape(256, 1024)
            value = value + dot(factor, solved, (1, 1))
        span = slice(q * 256, q * 256 + 256)
        for held, ref in zip(before, done):
            for n, block in enumerate(held):
                out_ref[span, draws_of(block)] = ref[span, 128 * n : 128 * n + 128]
        for n in range(2):
            draws = draws_of(blocks[n])
            rest = rows_ref[span, draws].astype(F32)
            if q == 0:
                rest = rest * jnp.where(iota((256, 128), 0) < 128, keep, 1.0)
            out_ref[span, draws] = (rest - value[:, 128 * n : 128 * n + 128]).astype(BF16)
        stores.append(pltpu.make_async_copy(out_ref.at[pl.ds(q * 256, 256)], out_hbm.at[pl.ds(q * 256, 256)], sems.at[q]))
        stores[q].start()
    for store in stores:
        store.wait()


HBM = pl.BlockSpec(memory_space=pltpu.HBM)
ANY = pl.BlockSpec(memory_space=pl.ANY)


def launch(kernel, args, outs, scratch=(), specs=None, out_specs=None, aliases=None, limit=16, flops=0, moved=0):
    return pl.pallas_call(
        kernel,
        out_shape=[jax.ShapeDtypeStruct(s, d) for s, d in outs],
        grid=(1,),
        in_specs=specs or [VMEM] * len(args),
        out_specs=out_specs or [VMEM] * len(outs),
        scratch_shapes=list(scratch),
        input_output_aliases=aliases or {},
        compiler_params=pltpu.CompilerParams(vmem_limit_bytes=int(limit * (1 << 20))),
        cost_estimate=pl.CostEstimate(flops=flops, bytes_accessed=moved, transcendentals=0),
    )(*args)


def spread_along(value, first, source):
    def move(kind):
        return along_first(kind) if first else along_second(kind)

    return [send(value, move(kind), source) for kind in range(3)]


def spread_first(piece):
    moved = [send(piece, along_first(kind)) for kind in range(3)]
    first, second, core = place_of(0)
    source = jnp.where(core == 0, 0, 1)
    line = jnp.where(first ^ 1 == source, moved[0], jnp.where(3 - first == source, moved[1], moved[2]))
    line = jnp.where(first == source, piece, line)
    return jnp.where(second == 1 - source, line, jnp.zeros_like(line))


def spread_second(piece):
    return spread_along(piece, False, lambda x, y, z, k: y == 1 if k == 0 else x == 0)


def around_cols(piece):
    return (piece, send(piece, along_z(0)), send(piece, along_z(1)), send(piece, along_z(2)))


def update(kernel, blocks, pieces, panels, rows, width=256, extra=(), out=VMEM):
    return launch(
        functools.partial(kernel, blocks),
        (*pieces, panels, rows),
        [((1024, width), BF16)],
        [pltpu.VMEM((256, 2048), BF16), pltpu.VMEM((2, 128, 1024), BF16), *extra],
        out_specs=[out],
        limit=16,
        flops=1 << 30,
        moved=2 << 20,
    )[0]


def steps(b_ingest, source_point, panels, diag_inverse):
    (ordered,) = launch(
        order_kernel,
        (source_point.reshape(1, 1024), b_ingest),
        [((1024, 1408), BF16)],
        [
            pltpu.VMEM((1024, 1024), BF16),
            pltpu.VMEM((1024, 1408), BF16),
            pltpu.VMEM((1024, 1024), BF16),
            pltpu.VMEM((128, 1024), F32),
            pltpu.SemaphoreType.DMA((1,)),
            pltpu.SemaphoreType.DMA((4,)),
        ],
        specs=[VMEM, HBM],
        out_specs=[HBM],
        limit=61.4,
        flops=3 << 30,
        moved=5 << 20,
    )
    piece = panels[0, 0, 0]
    line = spread_first(piece)
    plane = spread_second(line)
    arrived = lax.all_to_all(ordered.reshape(128, 8, 1408), AXES, split_axis=0, concat_axis=0, tiled=True)
    inverses, _ = lax.optimization_barrier((diag_inverse, ordered))
    inverses = launch(
        load_kernel,
        (inverses,),
        [((1024, 1024), BF16)] * 2,
        [pltpu.SemaphoreType.DMA((2,))],
        specs=[HBM],
        limit=6,
        moved=8 << 20,
    )
    arrived = arrived.reshape(1024, 1408)
    own, lead, follow = launch(
        compact_kernel,
        (arrived,),
        [((8, 1024), jnp.int32), ((64, 256), BF16), ((64, 256), BF16)],
        specs=[pl.BlockSpec((1024, 384), lambda i: (0, 0))],
        limit=12,
        flops=1 << 27,
        moved=1 << 20,
    )
    line, plane, _ = lax.optimization_barrier((line, plane, own))
    link = line + plane[0] + plane[1] + plane[2]
    link_other = send(link, other_core)
    solved, second = launch(
        first_kernel,
        (*around_cols(lead), inverses[0], follow, link, link_other),
        [((64, 1024), BF16), ((64, 256), BF16)],
        [pltpu.VMEM((4, 64, 256), BF16)],
        limit=12,
        flops=1 << 28,
        moved=3 << 20,
    )
    (both,) = launch(
        second_kernel,
        (*around_cols(second), inverses[1], solved),
        [((32, 2048), BF16)],
        [pltpu.VMEM((4, 64, 256), BF16)],
        limit=12,
        flops=1 << 28,
        moved=3 << 20,
    )
    (rows,) = launch(
        scatter_kernel,
        (own, arrived),
        [((1024, 1024), BF16)],
        [pltpu.VMEM((1024, 1024), BF16), pltpu.VMEM((1024, 1024), BF16), pltpu.SemaphoreType.DMA],
        specs=[VMEM, ANY],
        limit=20,
        flops=1 << 31,
        moved=4 << 20,
    )
    line = [both] + [send(both, along_first(i)) for i in range(3)]
    line = jnp.concatenate(line, axis=0)
    side0 = send(line, along_second(0))
    side2 = send(line, along_second(2))
    side1 = send(line, along_second(1))
    line_other = send(line, other_core)
    side0_other, side2_other = send(side0, other_core), send(side2, other_core)
    side1_other = send(side1, other_core)
    places = [((0, n), (1, n)) for n in (3, 0, 2, 1)]
    part0 = update(update_kernel, places[0], (line, line_other), panels, rows)
    part1 = update(update_kernel, places[1], (side0, side0_other), panels, rows)
    part2 = update(update_kernel, places[2], (side2, side2_other), panels, rows)
    kernel = functools.partial(last_kernel, places[:3])
    pieces = (side1, side1_other, part0, part1, part2)
    extra = (pltpu.VMEM((1024, 1024), BF16), pltpu.SemaphoreType.DMA((4,)))
    updated = update(kernel, places[3], pieces, panels, rows, 1024, extra, HBM)
    return updated.reshape(8, 1, 128, 1024)


def solution(mesh):
    return jax.shard_map(
        steps,
        mesh=mesh,
        in_specs=(
            P(("row", "col"), None),
            P(("row", "col")),
            P(None, None, "row", "col", None),
            P(),
        ),
        out_specs=P(None, "row", "col", None),
        check_vma=False,
    )
```

```python
import functools

import jax
import jax.numpy as jnp
from jax import lax
from jax.experimental import pallas as pl
from jax.experimental.pallas import tpu as pltpu
from jax.sharding import PartitionSpec as P

AXES = ("row", "col")
BF16 = jnp.bfloat16
F32 = jnp.float32
VMEM = pl.BlockSpec(memory_space=pltpu.VMEM)


def device_id(x, y, z, k):
    return (x % 4 * 4 + y % 4) * 8 + z % 4 * 2 + k


def send(value, move, only=None):
    pairs = []
    for x in range(4):
        for y in range(4):
            for z in range(4):
                for k in range(2):
                    if only is None or only(x, y, z, k):
                        pairs.append((device_id(x, y, z, k), device_id(*move(x, y, z, k))))
    return lax.ppermute(value, AXES, pairs)


def swap(kind, at):
    return (at ^ 1, 3 - at, at ^ 2)[kind]


def along_first(kind):
    return lambda x, y, z, k: (swap(kind, x), y, z, k) if k == 0 else (x, swap(kind, y), z, k)


def along_second(kind):
    return lambda x, y, z, k: (x, swap(kind, y), z, k) if k == 0 else (swap(kind, x), y, z, k)


def along_z(kind):
    return lambda x, y, z, k: (x, y, swap(kind, z), k)


def other_core(x, y, z, k):
    return (x, y, z, 1 - k)


def iota(shape, axis):
    return lax.broadcasted_iota(jnp.int32, shape, axis)


def dot(a, b, contract):
    return lax.dot_general(a, b, ((contract[:1], contract[1:]), ((), ())), preferred_element_type=F32)


def order_kernel(points_ref, rows_hbm, out_hbm, rows_ref, out_ref, perm_ref, head_ref, in_sems, out_sems):
    count = rows_ref.shape[0]
    load = pltpu.make_async_copy(rows_hbm, rows_ref, in_sems.at[0])
    load.start()
    points = points_ref[...]
    block = points >> 10
    offset = points & 1023
    target = (block & 15) * 8 + (offset >> 7)
    local = (block >> 4) * 128 + (offset & 127)
    wanted = (iota((128, count), 0) == target).astype(F32)
    earlier = (iota((count, count), 0) < iota((count, count), 1)).astype(F32).astype(BF16)
    seen = dot(wanted.astype(BF16), earlier, (1, 0))
    rank = jnp.sum(wanted * seen, axis=0, keepdims=True).astype(jnp.int32)
    slot = target * 8 + rank
    perm_ref[...] = (iota((count, count), 0) == slot).astype(F32).astype(BF16)
    part = iota((128, count), 0)
    digit = jnp.where(part % 2 == 0, local >> 5, local & 31)
    digits = jnp.where((part >= 64) & (part < 72), digit, 0).astype(F32).astype(BF16)
    ids = dot(perm_ref[...], digits, (1, 1))
    lane = iota((64, 128), 1)

    def both(value, first, odd):
        tiles = [value[first + 16 * z + 8 * odd : first + 16 * z + 8 * odd + 8] for z in range(4)]
        return jnp.concatenate([t for t in tiles for _ in range(2)], axis=0)

    shared = [both(ids, 0, 0), both(ids, 0, 1), ids[64:128]]
    stores = []
    load.wait()
    for x in range(4):
        chunk = slice(x * 256, x * 256 + 256)
        part_rows = dot(perm_ref[chunk, :], rows_ref[...], (1, 0))
        out_ref[chunk, 256:1280] = part_rows.astype(BF16)
        if x == 0:
            head_ref[...] = part_rows[0:128]
        for y in range(4):
            rows = slice(x * 256 + y * 64, x * 256 + y * 64 + 64)
            mixed = ids[rows]
            for i in range(3):
                mixed = jnp.where(lane < 66 + 2 * i, mixed, shared[i])
            cut = []
            for p in range(6):
                tile, at = (y, 32 * x) if p % 2 == 0 else (4 + x, 32 * y)
                tile = head_ref[:, 128 * tile : 128 * tile + 128]
                tile = both(tile, 0, p // 2) if p < 4 else tile[64:128]
                shift = (32 * (p % 4) - at) % 128
                cut.append(pltpu.roll(tile, shift, 1) if shift else tile)
            lead = jnp.where(lane < 64, jnp.where(lane < 32, cut[0], cut[1]), jnp.where(lane < 96, cut[2], cut[3]))
            out_ref[rows, 0:128] = lead.astype(BF16)
            follow = jnp.where(lane < 64, jnp.where(lane < 32, cut[4], cut[5]), mixed)
            out_ref[rows, 128:256] = follow.astype(BF16)
        span = pl.ds(x * 256, 256)
        stores.append(pltpu.make_async_copy(out_ref.at[span], out_hbm.at[span], out_sems.at[x]))
        stores[x].start()
    for store in stores:
        store.wait()


def compact_kernel(early_ref, own_ref, lead_ref, next_ref):
    count = early_ref.shape[0]
    pick = iota((8, 128), 0)
    lane = iota((8, 128), 1) - 64
    weight = jnp.where(lane == 2 * pick, 32.0, jnp.where(lane == 2 * pick + 1, 1.0, 0.0))
    weight = jnp.where(pick < 4, weight, 0.0).astype(BF16)
    locals_ = dot(weight, early_ref[:, 128:256], (1, 1)).astype(jnp.int32)
    own_ref[...] = locals_
    place = iota((128, count), 0)
    hits = [(place == locals_[i : i + 1]).astype(F32).astype(BF16) for i in (1, 2, 3)]
    for odd in range(2):
        found = dot(early_ref[:, 0:128], hits[odd], (0, 1))[64 * odd : 64 * odd + 64]
        lead_ref[:, 128 * odd : 128 * odd + 128] = found.astype(BF16)
    next_ref[...] = dot(early_ref[:, 128:256], hits[2], (0, 1))[0:64].astype(BF16)


def gather_cols(refs, scratch):
    z = lax.axis_index("col") // 2
    for ref, at in zip(refs, (z, z ^ 1, 3 - z, z ^ 2)):
        scratch[at] = ref[...]
    return jnp.concatenate([scratch[i] for i in range(4)], axis=1)


def first_kernel(p0, p1, p2, p3, inverse_ref, next_ref, l0, l1, l2, l3, solved_ref, second_ref, scratch):
    lead = gather_cols((p0, p1, p2, p3), scratch)
    solved = dot(lead, inverse_ref[...], (1, 1)).astype(BF16)
    solved_ref[...] = solved
    link = (l0[...] + l1[...]) + (l2[...] + l3[...])
    second_ref[...] = (next_ref[...].astype(F32) - dot(solved, link, (1, 1))).astype(BF16)


def second_kernel(p0, p1, p2, p3, inverse_ref, solved_ref, both_ref, scratch):
    z = lax.axis_index("col") // 2
    k = lax.axis_index("col") % 2
    for ref, at in zip((p0, p1, p2, p3), (z, z ^ 1, 3 - z, z ^ 2)):
        scratch[2 * at + k] = ref[0:64]
        scratch[2 * at + 1 - k] = ref[64:128]
    second = jnp.concatenate([scratch[i] for i in range(8)], axis=1)
    solved = dot(second, inverse_ref[...], (1, 1)).astype(BF16)
    even = lax.axis_index("col") % 2 == 0
    both_ref[:, 0:1024] = jnp.where(even, solved_ref[0:32], solved_ref[32:64])
    both_ref[:, 1024:2048] = jnp.where(even, solved[0:32], solved[32:64])


def scatter_kernel(own_ref, arrived_ref, out_ref, hit_ref, rows_ref, sem):
    count = arrived_ref.shape[0]
    copy = pltpu.make_async_copy(arrived_ref.at[:, 256:1280], rows_ref, sem)
    copy.start()
    hit_ref[...] = (iota((count, count), 0) == own_ref[0:1]).astype(F32).astype(BF16)
    copy.wait()
    for q in range(4):
        cols = slice(q * 256, q * 256 + 256)
        out_ref[:, cols] = dot(hit_ref[...], rows_ref[:, cols], (1, 0)).astype(BF16)


def place_of(kind):
    row = lax.axis_index("row")
    core = lax.axis_index("col") % 2
    x, y = row // 4, row % 4
    if kind:
        core = 1 - core
    return jnp.where(core == 0, x, y), jnp.where(core == 0, y, x), core


def load_kernel(source_hbm, first_ref, second_ref, sems):
    copies = [pltpu.make_async_copy(source_hbm.at[i], ref, sems.at[i]) for i, ref in enumerate((first_ref, second_ref))]
    for copy in copies:
        copy.start()
    for copy in copies:
        copy.wait()


def heads_of(panels_ref, head_ref):
    row = lax.axis_index("row")
    col = lax.axis_index("col")
    unit = (iota((128, 1024), 1) == iota((128, 1024), 0) + col * 128).astype(F32) * -1.0
    for p in range(2):
        kept = jnp.where(row < 2, 0.0, panels_ref[p, 0, 0].astype(F32))
        head_ref[p] = jnp.where(row == p, unit, kept).astype(BF16)


def product(panels_ref, head_ref, solved_t):
    s0 = solved_t[:, 0:1024]
    s1 = solved_t[:, 1024:2048]
    head = dot(head_ref[0], s0, (1, 1)) + dot(head_ref[1], s1, (1, 1))
    tail0 = panels_ref[0, 1:8, 0].reshape(896, 1024)
    tail1 = panels_ref[1, 1:8, 0].reshape(896, 1024)
    return head, dot(tail0, s0, (1, 1)) + dot(tail1, s1, (1, 1))


def updated_blocks(blocks, pieces, panels_ref, rows_ref, solved_t, head_ref, write):
    keep = jnp.where(lax.axis_index("row") < 2, 0.0, 1.0)
    heads_of(panels_ref, head_ref)
    place_blocks(blocks, pieces, solved_t)
    head, tail = product(panels_ref, head_ref, solved_t)
    for n in range(2):
        draws = draws_of(blocks[n])
        part = slice(128 * n, 128 * n + 128)
        write(n, slice(0, 128), rows_ref[0:128, draws].astype(F32) * keep - head[:, part])
        write(n, slice(128, 1024), rows_ref[128:1024, draws].astype(F32) - tail[:, part])


def place_blocks(blocks, pieces, solved_t):
    for i, (kind, _) in enumerate(blocks):
        first, _, _ = place_of(kind)
        for j, place in enumerate((first, first ^ 1, 3 - first, first ^ 2)):
            at = pl.multiple_of(128 * i + 32 * place, 32)
            solved_t[pl.ds(at, 32), :] = pieces[i][j * 32 : j * 32 + 32, :]


def draws_of(block):
    kind, which = block
    _, second, core = place_of(kind)
    at = second if which == 3 else swap(which, second)
    return pl.ds(pl.multiple_of(128 * (4 * core + at), 128), 128)


def update_kernel(blocks, a_ref, b_ref, panels_ref, rows_ref, out_ref, solved_t, head_ref):
    def write(n, rows, value):
        out_ref[rows, 128 * n : 128 * n + 128] = value.astype(BF16)

    updated_blocks(blocks, (a_ref, b_ref), panels_ref, rows_ref, solved_t, head_ref, write)


def last_kernel(before, blocks, a_ref, b_ref, *refs):
    done, (panels_ref, rows_ref, out_hbm, solved_t, head_ref, out_ref, sems) = refs[: len(before)], refs[len(before) :]
    keep = jnp.where(lax.axis_index("row") < 2, 0.0, 1.0)
    heads_of(panels_ref, head_ref)
    place_blocks(blocks, (a_ref, b_ref), solved_t)
    stores = []
    for q in range(4):
        value = 0.0
        for p in range(2):
            solved = solved_t[:, p * 1024 : p * 1024 + 1024]
            if q == 0:
                factor = jnp.concatenate([head_ref[p], panels_ref[p, 1, 0]], axis=0)
            else:
                factor = panels_ref[p, 2 * q : 2 * q + 2, 0].reshape(256, 1024)
            value = value + dot(factor, solved, (1, 1))
        span = slice(q * 256, q * 256 + 256)
        for held, ref in zip(before, done):
            for n, block in enumerate(held):
                out_ref[span, draws_of(block)] = ref[span, 128 * n : 128 * n + 128]
        for n in range(2):
            draws = draws_of(blocks[n])
            rest = rows_ref[span, draws].astype(F32)
            if q == 0:
                rest = rest * jnp.where(iota((256, 128), 0) < 128, keep, 1.0)
            out_ref[span, draws] = (rest - value[:, 128 * n : 128 * n + 128]).astype(BF16)
        stores.append(pltpu.make_async_copy(out_ref.at[pl.ds(q * 256, 256)], out_hbm.at[pl.ds(q * 256, 256)], sems.at[q]))
        stores[q].start()
    for store in stores:
        store.wait()


HBM = pl.BlockSpec(memory_space=pltpu.HBM)
ANY = pl.BlockSpec(memory_space=pl.ANY)


def launch(kernel, args, outs, scratch=(), specs=None, out_specs=None, aliases=None, limit=16, flops=0, moved=0):
    return pl.pallas_call(
        kernel,
        out_shape=[jax.ShapeDtypeStruct(s, d) for s, d in outs],
        grid=(1,),
        in_specs=specs or [VMEM] * len(args),
        out_specs=out_specs or [VMEM] * len(outs),
        scratch_shapes=list(scratch),
        input_output_aliases=aliases or {},
        compiler_params=pltpu.CompilerParams(vmem_limit_bytes=int(limit * (1 << 20))),
        cost_estimate=pl.CostEstimate(flops=flops, bytes_accessed=moved, transcendentals=0),
    )(*args)


def spread_along(value, first, source):
    def move(kind):
        return along_first(kind) if first else along_second(kind)

    return [send(value, move(kind), source) for kind in range(3)]


def spread_first(piece):
    return spread_along(piece, True, lambda x, y, z, k: x == 0 and y == 1)


def spread_second(piece):
    return spread_along(piece, False, lambda x, y, z, k: y == 1 if k == 0 else x == 0)


def around_cols(piece):
    return (piece, send(piece, along_z(0)), send(piece, along_z(1)), send(piece, along_z(2)))


def update(kernel, blocks, pieces, panels, rows, width=256, extra=(), out=VMEM):
    return launch(
        functools.partial(kernel, blocks),
        (*pieces, panels, rows),
        [((1024, width), BF16)],
        [pltpu.VMEM((256, 2048), BF16), pltpu.VMEM((2, 128, 1024), BF16), *extra],
        out_specs=[out],
        limit=16,
        flops=1 << 30,
        moved=2 << 20,
    )[0]


def steps(b_ingest, source_point, panels, diag_inverse):
    (ordered,) = launch(
        order_kernel,
        (source_point.reshape(1, 1024), b_ingest),
        [((1024, 1280), BF16)],
        [
            pltpu.VMEM((1024, 1024), BF16),
            pltpu.VMEM((1024, 1280), BF16),
            pltpu.VMEM((1024, 1024), BF16),
            pltpu.VMEM((128, 1024), F32),
            pltpu.SemaphoreType.DMA((1,)),
            pltpu.SemaphoreType.DMA((4,)),
        ],
        specs=[VMEM, HBM],
        out_specs=[HBM],
        limit=61.4,
        flops=3 << 30,
        moved=5 << 20,
    )
    piece = panels[0, 0, 0]
    line = spread_first(piece)
    line = jnp.where(lax.axis_index("row") == 1, piece, jnp.zeros_like(piece)) + line[0] + line[1] + line[2]
    plane = spread_second(line)
    arrived = lax.all_to_all(ordered.reshape(128, 8, 1280), AXES, split_axis=0, concat_axis=0, tiled=True)
    inverses, _ = lax.optimization_barrier((diag_inverse, ordered))
    inverses = launch(
        load_kernel,
        (inverses,),
        [((1024, 1024), BF16)] * 2,
        [pltpu.SemaphoreType.DMA((2,))],
        specs=[HBM],
        limit=6,
        moved=8 << 20,
    )
    arrived = arrived.reshape(1024, 1280)
    own, lead, follow = launch(
        compact_kernel,
        (arrived,),
        [((8, 1024), jnp.int32), ((64, 256), BF16), ((64, 128), BF16)],
        specs=[pl.BlockSpec((1024, 256), lambda i: (0, 0))],
        limit=12,
        flops=1 << 27,
        moved=1 << 20,
    )
    solved, second = launch(
        first_kernel,
        (*around_cols(lead), inverses[0], follow, line, *plane),
        [((64, 1024), BF16), ((64, 128), BF16)],
        [pltpu.VMEM((4, 64, 256), BF16)],
        limit=12,
        flops=1 << 28,
        moved=3 << 20,
    )
    second = jnp.concatenate([second, send(second, other_core)], axis=0)
    (both,) = launch(
        second_kernel,
        (*around_cols(second), inverses[1], solved),
        [((32, 2048), BF16)],
        [pltpu.VMEM((8, 64, 128), BF16)],
        limit=12,
        flops=1 << 28,
        moved=3 << 20,
    )
    (rows,) = launch(
        scatter_kernel,
        (own, arrived),
        [((1024, 1024), BF16)],
        [pltpu.VMEM((1024, 1024), BF16), pltpu.VMEM((1024, 1024), BF16), pltpu.SemaphoreType.DMA],
        specs=[VMEM, ANY],
        limit=20,
        flops=1 << 31,
        moved=4 << 20,
    )
    line = [both] + [send(both, along_first(i)) for i in range(3)]
    line = jnp.concatenate(line, axis=0)
    side0 = send(line, along_second(0))
    side2 = send(line, along_second(2))
    side1 = send(line, along_second(1))
    line_other = send(line, other_core)
    side0_other, side2_other = send(side0, other_core), send(side2, other_core)
    side1_other = send(side1, other_core)
    places = [((0, n), (1, n)) for n in (3, 0, 2, 1)]
    part0 = update(update_kernel, places[0], (line, line_other), panels, rows)
    part1 = update(update_kernel, places[1], (side0, side0_other), panels, rows)
    part2 = update(update_kernel, places[2], (side2, side2_other), panels, rows)
    kernel = functools.partial(last_kernel, places[:3])
    pieces = (side1, side1_other, part0, part1, part2)
    extra = (pltpu.VMEM((1024, 1024), BF16), pltpu.SemaphoreType.DMA((4,)))
    updated = update(kernel, places[3], pieces, panels, rows, 1024, extra, HBM)
    return updated.reshape(8, 1, 128, 1024)


def solution(mesh):
    return jax.shard_map(
        steps,
        mesh=mesh,
        in_specs=(
            P(("row", "col"), None),
            P(("row", "col")),
            P(None, None, "row", "col", None),
            P(),
        ),
        out_specs=P(None, "row", "col", None),
        check_vma=False,
    )
```

```python
import functools

import jax
import jax.numpy as jnp
from jax import lax
from jax.experimental import pallas as pl
from jax.experimental.pallas import tpu as pltpu
from jax.sharding import PartitionSpec as P

AXES = ("row", "col")
BF16 = jnp.bfloat16
F32 = jnp.float32
VMEM = pl.BlockSpec(memory_space=pltpu.VMEM)


def device_id(x, y, z, k):
    return (x % 4 * 4 + y % 4) * 8 + z % 4 * 2 + k


def send(value, move, only=None):
    pairs = []
    for x in range(4):
        for y in range(4):
            for z in range(4):
                for k in range(2):
                    if only is None or only(x, y, z, k):
                        pairs.append((device_id(x, y, z, k), device_id(*move(x, y, z, k))))
    return lax.ppermute(value, AXES, pairs)


def swap(kind, at):
    return (at ^ 1, 3 - at, at ^ 2)[kind]


def along_first(kind):
    return lambda x, y, z, k: (swap(kind, x), y, z, k) if k == 0 else (x, swap(kind, y), z, k)


def along_second(kind):
    return lambda x, y, z, k: (x, swap(kind, y), z, k) if k == 0 else (swap(kind, x), y, z, k)


def along_z(kind):
    return lambda x, y, z, k: (x, y, swap(kind, z), k)


def other_core(x, y, z, k):
    return (x, y, z, 1 - k)


def iota(shape, axis):
    return lax.broadcasted_iota(jnp.int32, shape, axis)


def dot(a, b, contract):
    return lax.dot_general(a, b, ((contract[:1], contract[1:]), ((), ())), preferred_element_type=F32)


def order_kernel(points_ref, rows_hbm, out_hbm, rows_ref, out_ref, perm_ref, head_ref, in_sems, out_sems):
    count = rows_ref.shape[0]
    load = pltpu.make_async_copy(rows_hbm, rows_ref, in_sems.at[0])
    load.start()
    points = points_ref[...]
    block = points >> 10
    offset = points & 1023
    target = (block & 15) * 8 + (offset >> 7)
    local = (block >> 4) * 128 + (offset & 127)
    wanted = (iota((128, count), 0) == target).astype(F32)
    earlier = (iota((count, count), 0) < iota((count, count), 1)).astype(F32).astype(BF16)
    seen = dot(wanted.astype(BF16), earlier, (1, 0))
    rank = jnp.sum(wanted * seen, axis=0, keepdims=True).astype(jnp.int32)
    slot = target * 8 + rank
    perm_ref[...] = (iota((count, count), 0) == slot).astype(F32).astype(BF16)
    part = iota((128, count), 0)
    digit = jnp.where(part % 2 == 0, local >> 5, local & 31)
    digits = jnp.where((part >= 64) & (part < 72), digit, 0).astype(F32).astype(BF16)
    ids = dot(perm_ref[...], digits, (1, 1))
    lane = iota((64, 128), 1)

    def both(value, first, odd):
        tiles = [value[first + 16 * z + 8 * odd : first + 16 * z + 8 * odd + 8] for z in range(4)]
        return jnp.concatenate([t for t in tiles for _ in range(2)], axis=0)

    shared = [both(ids, 0, 0), both(ids, 0, 1), ids[64:128]]
    stores = []
    load.wait()
    for x in range(4):
        chunk = slice(x * 256, x * 256 + 256)
        part_rows = dot(perm_ref[chunk, :], rows_ref[...], (1, 0))
        out_ref[chunk, 256:1280] = part_rows.astype(BF16)
        if x == 0:
            head_ref[...] = part_rows[0:128]
        for y in range(4):
            rows = slice(x * 256 + y * 64, x * 256 + y * 64 + 64)
            mixed = ids[rows]
            for i in range(3):
                mixed = jnp.where(lane < 66 + 2 * i, mixed, shared[i])
            cut = []
            for p in range(6):
                tile, at = (y, 32 * x) if p % 2 == 0 else (4 + x, 32 * y)
                tile = head_ref[:, 128 * tile : 128 * tile + 128]
                tile = both(tile, 0, p // 2) if p < 4 else tile[64:128]
                shift = (32 * (p % 4) - at) % 128
                cut.append(pltpu.roll(tile, shift, 1) if shift else tile)
            lead = jnp.where(lane < 64, jnp.where(lane < 32, cut[0], cut[1]), jnp.where(lane < 96, cut[2], cut[3]))
            out_ref[rows, 0:128] = lead.astype(BF16)
            follow = jnp.where(lane < 64, jnp.where(lane < 32, cut[4], cut[5]), mixed)
            out_ref[rows, 128:256] = follow.astype(BF16)
        span = pl.ds(x * 256, 256)
        stores.append(pltpu.make_async_copy(out_ref.at[span], out_hbm.at[span], out_sems.at[x]))
        stores[x].start()
    for store in stores:
        store.wait()


def compact_kernel(early_ref, own_ref, lead_ref, next_ref):
    count = early_ref.shape[0]
    pick = iota((8, 128), 0)
    lane = iota((8, 128), 1) - 64
    weight = jnp.where(lane == 2 * pick, 32.0, jnp.where(lane == 2 * pick + 1, 1.0, 0.0))
    weight = jnp.where(pick < 4, weight, 0.0).astype(BF16)
    locals_ = dot(weight, early_ref[:, 128:256], (1, 1)).astype(jnp.int32)
    own_ref[...] = locals_
    place = iota((128, count), 0)
    hits = [(place == locals_[i : i + 1]).astype(F32).astype(BF16) for i in (1, 2, 3)]
    for odd in range(2):
        found = dot(early_ref[:, 0:128], hits[odd], (0, 1))[64 * odd : 64 * odd + 64]
        lead_ref[:, 128 * odd : 128 * odd + 128] = found.astype(BF16)
    next_ref[...] = dot(early_ref[:, 128:256], hits[2], (0, 1))[0:64].astype(BF16)


def gather_cols(refs, scratch):
    z = lax.axis_index("col") // 2
    for ref, at in zip(refs, (z, z ^ 1, 3 - z, z ^ 2)):
        scratch[at] = ref[...]
    return jnp.concatenate([scratch[i] for i in range(4)], axis=1)


def first_kernel(p0, p1, p2, p3, inverse_ref, next_ref, l0, l1, l2, l3, solved_ref, second_ref, scratch, link_ref, sems):
    loads = [pltpu.make_async_copy(ref, link_ref.at[i], sems.at[i]) for i, ref in enumerate((l0, l1, l2, l3))]
    for load in loads:
        load.start()
    lead = gather_cols((p0, p1, p2, p3), scratch)
    solved = dot(lead, inverse_ref[...], (1, 1)).astype(BF16)
    solved_ref[...] = solved
    for load in loads:
        load.wait()
    link = (link_ref[0] + link_ref[1]) + (link_ref[2] + link_ref[3])
    second_ref[...] = (next_ref[...].astype(F32) - dot(solved, link, (1, 1))).astype(BF16)


def second_kernel(p0, p1, p2, p3, inverse_ref, solved_ref, both_ref, scratch):
    z = lax.axis_index("col") // 2
    k = lax.axis_index("col") % 2
    for ref, at in zip((p0, p1, p2, p3), (z, z ^ 1, 3 - z, z ^ 2)):
        scratch[2 * at + k] = ref[0:64]
        scratch[2 * at + 1 - k] = ref[64:128]
    second = jnp.concatenate([scratch[i] for i in range(8)], axis=1)
    solved = dot(second, inverse_ref[...], (1, 1)).astype(BF16)
    even = lax.axis_index("col") % 2 == 0
    both_ref[:, 0:1024] = jnp.where(even, solved_ref[0:32], solved_ref[32:64])
    both_ref[:, 1024:2048] = jnp.where(even, solved[0:32], solved[32:64])


def scatter_kernel(own_ref, arrived_ref, out_ref, hit_ref, rows_ref, sem):
    count = arrived_ref.shape[0]
    copy = pltpu.make_async_copy(arrived_ref.at[:, 256:1280], rows_ref, sem)
    copy.start()
    hit_ref[...] = (iota((count, count), 0) == own_ref[0:1]).astype(F32).astype(BF16)
    copy.wait()
    for q in range(4):
        cols = slice(q * 256, q * 256 + 256)
        out_ref[:, cols] = dot(hit_ref[...], rows_ref[:, cols], (1, 0)).astype(BF16)


def place_of(kind):
    row = lax.axis_index("row")
    core = lax.axis_index("col") % 2
    x, y = row // 4, row % 4
    if kind:
        core = 1 - core
    return jnp.where(core == 0, x, y), jnp.where(core == 0, y, x), core


def load_kernel(source_hbm, first_ref, second_ref, sems):
    copies = [pltpu.make_async_copy(source_hbm.at[i], ref, sems.at[i]) for i, ref in enumerate((first_ref, second_ref))]
    for copy in copies:
        copy.start()
    for copy in copies:
        copy.wait()


def heads_of(panels_ref, head_ref):
    row = lax.axis_index("row")
    col = lax.axis_index("col")
    unit = (iota((128, 1024), 1) == iota((128, 1024), 0) + col * 128).astype(F32) * -1.0
    for p in range(2):
        kept = jnp.where(row < 2, 0.0, panels_ref[p, 0, 0].astype(F32))
        head_ref[p] = jnp.where(row == p, unit, kept).astype(BF16)


def product(panels_ref, head_ref, solved_t):
    s0 = solved_t[:, 0:1024]
    s1 = solved_t[:, 1024:2048]
    head = dot(head_ref[0], s0, (1, 1)) + dot(head_ref[1], s1, (1, 1))
    tail0 = panels_ref[0, 1:8, 0].reshape(896, 1024)
    tail1 = panels_ref[1, 1:8, 0].reshape(896, 1024)
    return head, dot(tail0, s0, (1, 1)) + dot(tail1, s1, (1, 1))


def updated_blocks(blocks, pieces, panels_ref, rows_ref, solved_t, head_ref, write):
    keep = jnp.where(lax.axis_index("row") < 2, 0.0, 1.0)
    heads_of(panels_ref, head_ref)
    place_blocks(blocks, pieces, solved_t)
    head, tail = product(panels_ref, head_ref, solved_t)
    for n in range(2):
        draws = draws_of(blocks[n])
        part = slice(128 * n, 128 * n + 128)
        write(n, slice(0, 128), rows_ref[0:128, draws].astype(F32) * keep - head[:, part])
        write(n, slice(128, 1024), rows_ref[128:1024, draws].astype(F32) - tail[:, part])


def place_blocks(blocks, pieces, solved_t):
    for i, (kind, _) in enumerate(blocks):
        first, _, _ = place_of(kind)
        for j, place in enumerate((first, first ^ 1, 3 - first, first ^ 2)):
            at = pl.multiple_of(128 * i + 32 * place, 32)
            solved_t[pl.ds(at, 32), :] = pieces[i][j * 32 : j * 32 + 32, :]


def draws_of(block):
    kind, which = block
    _, second, core = place_of(kind)
    at = second if which == 3 else swap(which, second)
    return pl.ds(pl.multiple_of(128 * (4 * core + at), 128), 128)


def update_kernel(blocks, a_ref, b_ref, panels_ref, rows_ref, out_ref, solved_t, head_ref):
    def write(n, rows, value):
        out_ref[rows, 128 * n : 128 * n + 128] = value.astype(BF16)

    updated_blocks(blocks, (a_ref, b_ref), panels_ref, rows_ref, solved_t, head_ref, write)


def last_kernel(before, blocks, a_ref, b_ref, *refs):
    done, (panels_ref, rows_ref, out_hbm, solved_t, head_ref, out_ref, sems) = refs[: len(before)], refs[len(before) :]
    keep = jnp.where(lax.axis_index("row") < 2, 0.0, 1.0)
    heads_of(panels_ref, head_ref)
    place_blocks(blocks, (a_ref, b_ref), solved_t)
    stores = []
    for q in range(4):
        value = 0.0
        for p in range(2):
            solved = solved_t[:, p * 1024 : p * 1024 + 1024]
            if q == 0:
                factor = jnp.concatenate([head_ref[p], panels_ref[p, 1, 0]], axis=0)
            else:
                factor = panels_ref[p, 2 * q : 2 * q + 2, 0].reshape(256, 1024)
            value = value + dot(factor, solved, (1, 1))
        span = slice(q * 256, q * 256 + 256)
        for held, ref in zip(before, done):
            for n, block in enumerate(held):
                out_ref[span, draws_of(block)] = ref[span, 128 * n : 128 * n + 128]
        for n in range(2):
            draws = draws_of(blocks[n])
            rest = rows_ref[span, draws].astype(F32)
            if q == 0:
                rest = rest * jnp.where(iota((256, 128), 0) < 128, keep, 1.0)
            out_ref[span, draws] = (rest - value[:, 128 * n : 128 * n + 128]).astype(BF16)
        stores.append(pltpu.make_async_copy(out_ref.at[pl.ds(q * 256, 256)], out_hbm.at[pl.ds(q * 256, 256)], sems.at[q]))
        stores[q].start()
    for store in stores:
        store.wait()


HBM = pl.BlockSpec(memory_space=pltpu.HBM)
ANY = pl.BlockSpec(memory_space=pl.ANY)


def launch(kernel, args, outs, scratch=(), specs=None, out_specs=None, aliases=None, limit=16, flops=0, moved=0):
    return pl.pallas_call(
        kernel,
        out_shape=[jax.ShapeDtypeStruct(s, d) for s, d in outs],
        grid=(1,),
        in_specs=specs or [VMEM] * len(args),
        out_specs=out_specs or [VMEM] * len(outs),
        scratch_shapes=list(scratch),
        input_output_aliases=aliases or {},
        compiler_params=pltpu.CompilerParams(vmem_limit_bytes=int(limit * (1 << 20))),
        cost_estimate=pl.CostEstimate(flops=flops, bytes_accessed=moved, transcendentals=0),
    )(*args)


def spread_along(value, first, source):
    def move(kind):
        return along_first(kind) if first else along_second(kind)

    return [send(value, move(kind), source) for kind in range(3)]


def spread_first(piece):
    moved = [send(piece, along_first(kind)) for kind in range(3)]
    first, second, core = place_of(0)
    source = jnp.where(core == 0, 0, 1)
    line = jnp.where(first ^ 1 == source, moved[0], jnp.where(3 - first == source, moved[1], moved[2]))
    line = jnp.where(first == source, piece, line)
    return jnp.where(second == 1 - source, line, jnp.zeros_like(line))


def spread_second(piece):
    return spread_along(piece, False, lambda x, y, z, k: y == 1 if k == 0 else x == 0)


def around_cols(piece):
    return (piece, send(piece, along_z(0)), send(piece, along_z(1)), send(piece, along_z(2)))


def update(kernel, blocks, pieces, panels, rows, width=256, extra=(), out=VMEM):
    return launch(
        functools.partial(kernel, blocks),
        (*pieces, panels, rows),
        [((1024, width), BF16)],
        [pltpu.VMEM((256, 2048), BF16), pltpu.VMEM((2, 128, 1024), BF16), *extra],
        out_specs=[out],
        limit=16,
        flops=1 << 30,
        moved=2 << 20,
    )[0]


def steps(b_ingest, source_point, panels, diag_inverse):
    (ordered,) = launch(
        order_kernel,
        (source_point.reshape(1, 1024), b_ingest),
        [((1024, 1280), BF16)],
        [
            pltpu.VMEM((1024, 1024), BF16),
            pltpu.VMEM((1024, 1280), BF16),
            pltpu.VMEM((1024, 1024), BF16),
            pltpu.VMEM((128, 1024), F32),
            pltpu.SemaphoreType.DMA((1,)),
            pltpu.SemaphoreType.DMA((4,)),
        ],
        specs=[VMEM, HBM],
        out_specs=[HBM],
        limit=61.4,
        flops=3 << 30,
        moved=5 << 20,
    )
    piece = panels[0, 0, 0]
    line = spread_first(piece)
    plane = spread_second(line)
    arrived = lax.all_to_all(ordered.reshape(128, 8, 1280), AXES, split_axis=0, concat_axis=0, tiled=True)
    inverses, _ = lax.optimization_barrier((diag_inverse, ordered))
    inverses = launch(
        load_kernel,
        (inverses,),
        [((1024, 1024), BF16)] * 2,
        [pltpu.SemaphoreType.DMA((2,))],
        specs=[HBM],
        limit=6,
        moved=8 << 20,
    )
    arrived = arrived.reshape(1024, 1280)
    own, lead, follow = launch(
        compact_kernel,
        (arrived,),
        [((8, 1024), jnp.int32), ((64, 256), BF16), ((64, 128), BF16)],
        specs=[pl.BlockSpec((1024, 256), lambda i: (0, 0))],
        limit=12,
        flops=1 << 27,
        moved=1 << 20,
    )
    solved, second = launch(
        first_kernel,
        (*around_cols(lead), inverses[0], follow, line, *plane),
        [((64, 1024), BF16), ((64, 128), BF16)],
        [pltpu.VMEM((4, 64, 256), BF16), pltpu.VMEM((4, 128, 1024), BF16), pltpu.SemaphoreType.DMA((4,))],
        specs=[VMEM] * 6 + [HBM] * 4,
        limit=12,
        flops=1 << 28,
        moved=3 << 20,
    )
    second = jnp.concatenate([second, send(second, other_core)], axis=0)
    (both,) = launch(
        second_kernel,
        (*around_cols(second), inverses[1], solved),
        [((32, 2048), BF16)],
        [pltpu.VMEM((8, 64, 128), BF16)],
        limit=12,
        flops=1 << 28,
        moved=3 << 20,
    )
    (rows,) = launch(
        scatter_kernel,
        (own, arrived),
        [((1024, 1024), BF16)],
        [pltpu.VMEM((1024, 1024), BF16), pltpu.VMEM((1024, 1024), BF16), pltpu.SemaphoreType.DMA],
        specs=[VMEM, ANY],
        limit=20,
        flops=1 << 31,
        moved=4 << 20,
    )
    line = [both] + [send(both, along_first(i)) for i in range(3)]
    line = jnp.concatenate(line, axis=0)
    side0 = send(line, along_second(0))
    side2 = send(line, along_second(2))
    side1 = send(line, along_second(1))
    line_other = send(line, other_core)
    side0_other, side2_other = send(side0, other_core), send(side2, other_core)
    side1_other = send(side1, other_core)
    places = [((0, n), (1, n)) for n in (3, 0, 2, 1)]
    part0 = update(update_kernel, places[0], (line, line_other), panels, rows)
    part1 = update(update_kernel, places[1], (side0, side0_other), panels, rows)
    part2 = update(update_kernel, places[2], (side2, side2_other), panels, rows)
    kernel = functools.partial(last_kernel, places[:3])
    pieces = (side1, side1_other, part0, part1, part2)
    extra = (pltpu.VMEM((1024, 1024), BF16), pltpu.SemaphoreType.DMA((4,)))
    updated = update(kernel, places[3], pieces, panels, rows, 1024, extra, HBM)
    return updated.reshape(8, 1, 128, 1024)


def solution(mesh):
    return jax.shard_map(
        steps,
        mesh=mesh,
        in_specs=(
            P(("row", "col"), None),
            P(("row", "col")),
            P(None, None, "row", "col", None),
            P(),
        ),
        out_specs=P(None, "row", "col", None),
        check_vma=False,
    )
```

```python
import functools

import jax
import jax.numpy as jnp
from jax import lax
from jax.experimental import pallas as pl
from jax.experimental.pallas import tpu as pltpu
from jax.sharding import PartitionSpec as P

AXES = ("row", "col")
BF16 = jnp.bfloat16
F32 = jnp.float32
VMEM = pl.BlockSpec(memory_space=pltpu.VMEM)


def device_id(x, y, z, k):
    return (x % 4 * 4 + y % 4) * 8 + z % 4 * 2 + k


def send(value, move, only=None):
    pairs = []
    for x in range(4):
        for y in range(4):
            for z in range(4):
                for k in range(2):
                    if only is None or only(x, y, z, k):
                        pairs.append((device_id(x, y, z, k), device_id(*move(x, y, z, k))))
    return lax.ppermute(value, AXES, pairs)


def swap(kind, at):
    return (at ^ 1, 3 - at, at ^ 2)[kind]


def along_first(kind):
    return lambda x, y, z, k: (swap(kind, x), y, z, k) if k == 0 else (x, swap(kind, y), z, k)


def along_second(kind):
    return lambda x, y, z, k: (x, swap(kind, y), z, k) if k == 0 else (swap(kind, x), y, z, k)


def along_z(kind):
    return lambda x, y, z, k: (x, y, swap(kind, z), k)


def other_core(x, y, z, k):
    return (x, y, z, 1 - k)


def iota(shape, axis):
    return lax.broadcasted_iota(jnp.int32, shape, axis)


def dot(a, b, contract):
    return lax.dot_general(a, b, ((contract[:1], contract[1:]), ((), ())), preferred_element_type=F32)


def order_kernel(points_ref, rows_hbm, panels_hbm, out_hbm, piece_hbm, rows_ref, out_ref, perm_ref, head_ref, piece_ref, in_sems, out_sems):
    count = rows_ref.shape[0]
    load = pltpu.make_async_copy(rows_hbm, rows_ref, in_sems.at[0])
    load.start()
    piece = pltpu.make_async_copy(panels_hbm.at[0, 0, 0], piece_ref, in_sems.at[1])
    piece.start()
    points = points_ref[...]
    block = points >> 10
    offset = points & 1023
    target = (block & 15) * 8 + (offset >> 7)
    local = (block >> 4) * 128 + (offset & 127)
    wanted = (iota((128, count), 0) == target).astype(F32)
    earlier = (iota((count, count), 0) < iota((count, count), 1)).astype(F32).astype(BF16)
    seen = dot(wanted.astype(BF16), earlier, (1, 0))
    rank = jnp.sum(wanted * seen, axis=0, keepdims=True).astype(jnp.int32)
    slot = target * 8 + rank
    perm_ref[...] = (iota((count, count), 0) == slot).astype(F32).astype(BF16)
    part = iota((128, count), 0)
    digit = jnp.where(part % 2 == 0, local >> 5, local & 31)
    digits = jnp.where((part >= 64) & (part < 72), digit, 0).astype(F32).astype(BF16)
    ids = dot(perm_ref[...], digits, (1, 1))
    lane = iota((64, 128), 1)

    def both(value, first, odd):
        tiles = [value[first + 16 * z + 8 * odd : first + 16 * z + 8 * odd + 8] for z in range(4)]
        return jnp.concatenate([t for t in tiles for _ in range(2)], axis=0)

    shared = [both(ids, 0, 0), both(ids, 0, 1), ids[64:128]]
    stores = []
    load.wait()
    piece.wait()
    keep_piece = pltpu.make_async_copy(piece_ref, piece_hbm, out_sems.at[4])
    keep_piece.start()
    for x in range(4):
        chunk = slice(x * 256, x * 256 + 256)
        part_rows = dot(perm_ref[chunk, :], rows_ref[...], (1, 0))
        out_ref[chunk, 256:1280] = part_rows.astype(BF16)
        if x == 0:
            head_ref[...] = part_rows[0:128]
        for y in range(4):
            rows = slice(x * 256 + y * 64, x * 256 + y * 64 + 64)
            mixed = ids[rows]
            for i in range(3):
                mixed = jnp.where(lane < 66 + 2 * i, mixed, shared[i])
            cut = []
            for p in range(6):
                tile, at = (y, 32 * x) if p % 2 == 0 else (4 + x, 32 * y)
                tile = head_ref[:, 128 * tile : 128 * tile + 128]
                tile = both(tile, 0, p // 2) if p < 4 else tile[64:128]
                shift = (32 * (p % 4) - at) % 128
                cut.append(pltpu.roll(tile, shift, 1) if shift else tile)
            lead = jnp.where(lane < 64, jnp.where(lane < 32, cut[0], cut[1]), jnp.where(lane < 96, cut[2], cut[3]))
            out_ref[rows, 0:128] = lead.astype(BF16)
            follow = jnp.where(lane < 64, jnp.where(lane < 32, cut[4], cut[5]), mixed)
            out_ref[rows, 128:256] = follow.astype(BF16)
        span = pl.ds(x * 256, 256)
        stores.append(pltpu.make_async_copy(out_ref.at[span], out_hbm.at[span], out_sems.at[x]))
        stores[x].start()
    keep_piece.wait()
    for store in stores:
        store.wait()


def compact_kernel(early_ref, own_ref, lead_ref, next_ref):
    count = early_ref.shape[0]
    pick = iota((8, 128), 0)
    lane = iota((8, 128), 1) - 64
    weight = jnp.where(lane == 2 * pick, 32.0, jnp.where(lane == 2 * pick + 1, 1.0, 0.0))
    weight = jnp.where(pick < 4, weight, 0.0).astype(BF16)
    locals_ = dot(weight, early_ref[:, 128:256], (1, 1)).astype(jnp.int32)
    own_ref[...] = locals_
    place = iota((128, count), 0)
    hits = [(place == locals_[i : i + 1]).astype(F32).astype(BF16) for i in (1, 2, 3)]
    for odd in range(2):
        found = dot(early_ref[:, 0:128], hits[odd], (0, 1))[64 * odd : 64 * odd + 64]
        lead_ref[:, 128 * odd : 128 * odd + 128] = found.astype(BF16)
    next_ref[...] = dot(early_ref[:, 128:256], hits[2], (0, 1))[0:64].astype(BF16)


def gather_cols(refs, scratch):
    z = lax.axis_index("col") // 2
    for ref, at in zip(refs, (z, z ^ 1, 3 - z, z ^ 2)):
        scratch[at] = ref[...]
    return jnp.concatenate([scratch[i] for i in range(4)], axis=1)


def first_kernel(p0, p1, p2, p3, inverse_ref, next_ref, l0, l1, l2, l3, solved_ref, second_ref, scratch, link_ref, sems):
    loads = [pltpu.make_async_copy(ref, link_ref.at[i], sems.at[i]) for i, ref in enumerate((l0, l1, l2, l3))]
    for load in loads:
        load.start()
    lead = gather_cols((p0, p1, p2, p3), scratch)
    solved = dot(lead, inverse_ref[...], (1, 1)).astype(BF16)
    solved_ref[...] = solved
    for load in loads:
        load.wait()
    link = (link_ref[0] + link_ref[1]) + (link_ref[2] + link_ref[3])
    second_ref[...] = (next_ref[...].astype(F32) - dot(solved, link, (1, 1))).astype(BF16)


def second_kernel(p0, p1, p2, p3, inverse_ref, solved_ref, both_ref, scratch):
    z = lax.axis_index("col") // 2
    k = lax.axis_index("col") % 2
    for ref, at in zip((p0, p1, p2, p3), (z, z ^ 1, 3 - z, z ^ 2)):
        scratch[2 * at + k] = ref[0:64]
        scratch[2 * at + 1 - k] = ref[64:128]
    second = jnp.concatenate([scratch[i] for i in range(8)], axis=1)
    solved = dot(second, inverse_ref[...], (1, 1)).astype(BF16)
    even = lax.axis_index("col") % 2 == 0
    both_ref[:, 0:1024] = jnp.where(even, solved_ref[0:32], solved_ref[32:64])
    both_ref[:, 1024:2048] = jnp.where(even, solved[0:32], solved[32:64])


def scatter_kernel(own_ref, arrived_ref, out_ref, hit_ref, rows_ref, sem):
    count = arrived_ref.shape[0]
    copy = pltpu.make_async_copy(arrived_ref.at[:, 256:1280], rows_ref, sem)
    copy.start()
    hit_ref[...] = (iota((count, count), 0) == own_ref[0:1]).astype(F32).astype(BF16)
    copy.wait()
    for q in range(4):
        cols = slice(q * 256, q * 256 + 256)
        out_ref[:, cols] = dot(hit_ref[...], rows_ref[:, cols], (1, 0)).astype(BF16)


def place_of(kind):
    row = lax.axis_index("row")
    core = lax.axis_index("col") % 2
    x, y = row // 4, row % 4
    if kind:
        core = 1 - core
    return jnp.where(core == 0, x, y), jnp.where(core == 0, y, x), core


def load_kernel(source_hbm, first_ref, second_ref, sems):
    copies = [pltpu.make_async_copy(source_hbm.at[i], ref, sems.at[i]) for i, ref in enumerate((first_ref, second_ref))]
    for copy in copies:
        copy.start()
    for copy in copies:
        copy.wait()


def heads_of(panels_ref, head_ref):
    row = lax.axis_index("row")
    col = lax.axis_index("col")
    unit = (iota((128, 1024), 1) == iota((128, 1024), 0) + col * 128).astype(F32) * -1.0
    for p in range(2):
        kept = jnp.where(row < 2, 0.0, panels_ref[p, 0, 0].astype(F32))
        head_ref[p] = jnp.where(row == p, unit, kept).astype(BF16)


def product(panels_ref, head_ref, solved_t):
    s0 = solved_t[:, 0:1024]
    s1 = solved_t[:, 1024:2048]
    head = dot(head_ref[0], s0, (1, 1)) + dot(head_ref[1], s1, (1, 1))
    tail0 = panels_ref[0, 1:8, 0].reshape(896, 1024)
    tail1 = panels_ref[1, 1:8, 0].reshape(896, 1024)
    return head, dot(tail0, s0, (1, 1)) + dot(tail1, s1, (1, 1))


def updated_blocks(blocks, pieces, panels_ref, rows_ref, solved_t, head_ref, write):
    keep = jnp.where(lax.axis_index("row") < 2, 0.0, 1.0)
    heads_of(panels_ref, head_ref)
    place_blocks(blocks, pieces, solved_t)
    head, tail = product(panels_ref, head_ref, solved_t)
    for n in range(2):
        draws = draws_of(blocks[n])
        part = slice(128 * n, 128 * n + 128)
        write(n, slice(0, 128), rows_ref[0:128, draws].astype(F32) * keep - head[:, part])
        write(n, slice(128, 1024), rows_ref[128:1024, draws].astype(F32) - tail[:, part])


def place_blocks(blocks, pieces, solved_t):
    for i, (kind, _) in enumerate(blocks):
        first, _, _ = place_of(kind)
        for j, place in enumerate((first, first ^ 1, 3 - first, first ^ 2)):
            at = pl.multiple_of(128 * i + 32 * place, 32)
            solved_t[pl.ds(at, 32), :] = pieces[i][j * 32 : j * 32 + 32, :]


def draws_of(block):
    kind, which = block
    _, second, core = place_of(kind)
    at = second if which == 3 else swap(which, second)
    return pl.ds(pl.multiple_of(128 * (4 * core + at), 128), 128)


def update_kernel(blocks, a_ref, b_ref, panels_ref, rows_ref, out_ref, solved_t, head_ref):
    def write(n, rows, value):
        out_ref[rows, 128 * n : 128 * n + 128] = value.astype(BF16)

    updated_blocks(blocks, (a_ref, b_ref), panels_ref, rows_ref, solved_t, head_ref, write)


def last_kernel(before, blocks, a_ref, b_ref, *refs):
    done, (panels_ref, rows_ref, out_hbm, solved_t, head_ref, out_ref, sems) = refs[: len(before)], refs[len(before) :]
    keep = jnp.where(lax.axis_index("row") < 2, 0.0, 1.0)
    heads_of(panels_ref, head_ref)
    place_blocks(blocks, (a_ref, b_ref), solved_t)
    stores = []
    for q in range(4):
        value = 0.0
        for p in range(2):
            solved = solved_t[:, p * 1024 : p * 1024 + 1024]
            if q == 0:
                factor = jnp.concatenate([head_ref[p], panels_ref[p, 1, 0]], axis=0)
            else:
                factor = panels_ref[p, 2 * q : 2 * q + 2, 0].reshape(256, 1024)
            value = value + dot(factor, solved, (1, 1))
        span = slice(q * 256, q * 256 + 256)
        for held, ref in zip(before, done):
            for n, block in enumerate(held):
                out_ref[span, draws_of(block)] = ref[span, 128 * n : 128 * n + 128]
        for n in range(2):
            draws = draws_of(blocks[n])
            rest = rows_ref[span, draws].astype(F32)
            if q == 0:
                rest = rest * jnp.where(iota((256, 128), 0) < 128, keep, 1.0)
            out_ref[span, draws] = (rest - value[:, 128 * n : 128 * n + 128]).astype(BF16)
        stores.append(pltpu.make_async_copy(out_ref.at[pl.ds(q * 256, 256)], out_hbm.at[pl.ds(q * 256, 256)], sems.at[q]))
        stores[q].start()
    for store in stores:
        store.wait()


HBM = pl.BlockSpec(memory_space=pltpu.HBM)
ANY = pl.BlockSpec(memory_space=pl.ANY)


def launch(kernel, args, outs, scratch=(), specs=None, out_specs=None, aliases=None, limit=16, flops=0, moved=0):
    return pl.pallas_call(
        kernel,
        out_shape=[jax.ShapeDtypeStruct(s, d) for s, d in outs],
        grid=(1,),
        in_specs=specs or [VMEM] * len(args),
        out_specs=out_specs or [VMEM] * len(outs),
        scratch_shapes=list(scratch),
        input_output_aliases=aliases or {},
        compiler_params=pltpu.CompilerParams(vmem_limit_bytes=int(limit * (1 << 20))),
        cost_estimate=pl.CostEstimate(flops=flops, bytes_accessed=moved, transcendentals=0),
    )(*args)


def spread_along(value, first, source):
    def move(kind):
        return along_first(kind) if first else along_second(kind)

    return [send(value, move(kind), source) for kind in range(3)]


def spread_first(piece):
    moved = [send(piece, along_first(kind)) for kind in range(3)]
    first, second, core = place_of(0)
    source = jnp.where(core == 0, 0, 1)
    line = jnp.where(first ^ 1 == source, moved[0], jnp.where(3 - first == source, moved[1], moved[2]))
    line = jnp.where(first == source, piece, line)
    return jnp.where(second == 1 - source, line, jnp.zeros_like(line))


def spread_second(piece):
    return spread_along(piece, False, lambda x, y, z, k: y == 1 if k == 0 else x == 0)


def around_cols(piece):
    return (piece, send(piece, along_z(0)), send(piece, along_z(1)), send(piece, along_z(2)))


def update(kernel, blocks, pieces, panels, rows, width=256, extra=(), out=VMEM):
    return launch(
        functools.partial(kernel, blocks),
        (*pieces, panels, rows),
        [((1024, width), BF16)],
        [pltpu.VMEM((256, 2048), BF16), pltpu.VMEM((2, 128, 1024), BF16), *extra],
        out_specs=[out],
        limit=16,
        flops=1 << 30,
        moved=2 << 20,
    )[0]


def steps(b_ingest, source_point, panels, diag_inverse):
    ordered, piece = launch(
        order_kernel,
        (source_point.reshape(1, 1024), b_ingest, panels),
        [((1024, 1280), BF16), ((128, 1024), BF16)],
        [
            pltpu.VMEM((1024, 1024), BF16),
            pltpu.VMEM((1024, 1280), BF16),
            pltpu.VMEM((1024, 1024), BF16),
            pltpu.VMEM((128, 1024), F32),
            pltpu.VMEM((128, 1024), BF16),
            pltpu.SemaphoreType.DMA((2,)),
            pltpu.SemaphoreType.DMA((5,)),
        ],
        specs=[VMEM, HBM, HBM],
        out_specs=[HBM, HBM],
        limit=61.4,
        flops=3 << 30,
        moved=5 << 20,
    )
    line = spread_first(piece)
    plane = spread_second(line)
    arrived = lax.all_to_all(ordered.reshape(128, 8, 1280), AXES, split_axis=0, concat_axis=0, tiled=True)
    inverses, _ = lax.optimization_barrier((diag_inverse, ordered))
    inverses = launch(
        load_kernel,
        (inverses,),
        [((1024, 1024), BF16)] * 2,
        [pltpu.SemaphoreType.DMA((2,))],
        specs=[HBM],
        limit=6,
        moved=8 << 20,
    )
    arrived = arrived.reshape(1024, 1280)
    own, lead, follow = launch(
        compact_kernel,
        (arrived,),
        [((8, 1024), jnp.int32), ((64, 256), BF16), ((64, 128), BF16)],
        specs=[pl.BlockSpec((1024, 256), lambda i: (0, 0))],
        limit=12,
        flops=1 << 27,
        moved=1 << 20,
    )
    solved, second = launch(
        first_kernel,
        (*around_cols(lead), inverses[0], follow, line, *plane),
        [((64, 1024), BF16), ((64, 128), BF16)],
        [pltpu.VMEM((4, 64, 256), BF16), pltpu.VMEM((4, 128, 1024), BF16), pltpu.SemaphoreType.DMA((4,))],
        specs=[VMEM] * 6 + [HBM] * 4,
        limit=12,
        flops=1 << 28,
        moved=3 << 20,
    )
    second = jnp.concatenate([second, send(second, other_core)], axis=0)
    (both,) = launch(
        second_kernel,
        (*around_cols(second), inverses[1], solved),
        [((32, 2048), BF16)],
        [pltpu.VMEM((8, 64, 128), BF16)],
        limit=12,
        flops=1 << 28,
        moved=3 << 20,
    )
    (rows,) = launch(
        scatter_kernel,
        (own, arrived),
        [((1024, 1024), BF16)],
        [pltpu.VMEM((1024, 1024), BF16), pltpu.VMEM((1024, 1024), BF16), pltpu.SemaphoreType.DMA],
        specs=[VMEM, ANY],
        limit=20,
        flops=1 << 31,
        moved=4 << 20,
    )
    line = [both] + [send(both, along_first(i)) for i in range(3)]
    line = jnp.concatenate(line, axis=0)
    side0 = send(line, along_second(0))
    side2 = send(line, along_second(2))
    side1 = send(line, along_second(1))
    line_other = send(line, other_core)
    side0_other, side2_other = send(side0, other_core), send(side2, other_core)
    side1_other = send(side1, other_core)
    places = [((0, n), (1, n)) for n in (3, 0, 2, 1)]
    part0 = update(update_kernel, places[0], (line, line_other), panels, rows)
    part1 = update(update_kernel, places[1], (side0, side0_other), panels, rows)
    part2 = update(update_kernel, places[2], (side2, side2_other), panels, rows)
    kernel = functools.partial(last_kernel, places[:3])
    pieces = (side1, side1_other, part0, part1, part2)
    extra = (pltpu.VMEM((1024, 1024), BF16), pltpu.SemaphoreType.DMA((4,)))
    updated = update(kernel, places[3], pieces, panels, rows, 1024, extra, HBM)
    return updated.reshape(8, 1, 128, 1024)


def solution(mesh):
    return jax.shard_map(
        steps,
        mesh=mesh,
        in_specs=(
            P(("row", "col"), None),
            P(("row", "col")),
            P(None, None, "row", "col", None),
            P(),
        ),
        out_specs=P(None, "row", "col", None),
        check_vma=False,
    )
```

```python
import functools

import jax
import jax.numpy as jnp
from jax import lax
from jax.experimental import pallas as pl
from jax.experimental.pallas import tpu as pltpu
from jax.sharding import PartitionSpec as P

AXES = ("row", "col")
BF16 = jnp.bfloat16
F32 = jnp.float32
VMEM = pl.BlockSpec(memory_space=pltpu.VMEM)


def device_id(x, y, z, k):
    return (x % 4 * 4 + y % 4) * 8 + z % 4 * 2 + k


def send(value, move, only=None):
    pairs = []
    for x in range(4):
        for y in range(4):
            for z in range(4):
                for k in range(2):
                    if only is None or only(x, y, z, k):
                        pairs.append((device_id(x, y, z, k), device_id(*move(x, y, z, k))))
    return lax.ppermute(value, AXES, pairs)


def swap(kind, at):
    return (at ^ 1, 3 - at, at ^ 2)[kind]


def along_first(kind):
    return lambda x, y, z, k: (swap(kind, x), y, z, k) if k == 0 else (x, swap(kind, y), z, k)


def along_second(kind):
    return lambda x, y, z, k: (x, swap(kind, y), z, k) if k == 0 else (swap(kind, x), y, z, k)


def along_z(kind):
    return lambda x, y, z, k: (x, y, swap(kind, z), k)


def other_core(x, y, z, k):
    return (x, y, z, 1 - k)


def iota(shape, axis):
    return lax.broadcasted_iota(jnp.int32, shape, axis)


def dot(a, b, contract):
    return lax.dot_general(a, b, ((contract[:1], contract[1:]), ((), ())), preferred_element_type=F32)


def order_kernel(points_ref, rows_hbm, panels_hbm, out_hbm, piece_hbm, rows_ref, out_ref, perm_ref, head_ref, piece_ref, in_sems, out_sems):
    count = rows_ref.shape[0]
    loads = []
    for i in range(8):
        span = pl.ds(i * 128, 128)
        loads.append(pltpu.make_async_copy(rows_hbm.at[span], rows_ref.at[span], in_sems.at[1 + i]))
        loads[i].start()
    piece = pltpu.make_async_copy(panels_hbm.at[0, 0, 0], piece_ref, in_sems.at[0])
    piece.start()
    points = points_ref[...]
    block = points >> 10
    offset = points & 1023
    target = (block & 15) * 8 + (offset >> 7)
    local = (block >> 4) * 128 + (offset & 127)
    wanted = (iota((128, count), 0) == target).astype(F32)
    earlier = (iota((count, count), 0) < iota((count, count), 1)).astype(F32).astype(BF16)
    seen = dot(wanted.astype(BF16), earlier, (1, 0))
    rank = jnp.sum(wanted * seen, axis=0, keepdims=True).astype(jnp.int32)
    slot = target * 8 + rank
    perm_ref[...] = (iota((count, count), 0) == slot).astype(F32).astype(BF16)
    part = iota((128, count), 0)
    digit = jnp.where(part % 2 == 0, local >> 5, local & 31)
    digits = jnp.where((part >= 64) & (part < 72), digit, 0).astype(F32).astype(BF16)
    ids = dot(perm_ref[...], digits, (1, 1))
    lane = iota((64, 128), 1)

    def both(value, first, odd):
        tiles = [value[first + 16 * z + 8 * odd : first + 16 * z + 8 * odd + 8] for z in range(4)]
        return jnp.concatenate([t for t in tiles for _ in range(2)], axis=0)

    shared = [both(ids, 0, 0), both(ids, 0, 1), ids[64:128]]
    stores = []
    for load in loads:
        load.wait()
    piece.wait()
    keep_piece = pltpu.make_async_copy(piece_ref, piece_hbm, out_sems.at[4])
    keep_piece.start()
    for x in range(4):
        chunk = slice(x * 256, x * 256 + 256)
        part_rows = dot(perm_ref[chunk, :], rows_ref[...], (1, 0))
        out_ref[chunk, 256:1280] = part_rows.astype(BF16)
        if x == 0:
            head_ref[...] = part_rows[0:128]
        for y in range(4):
            rows = slice(x * 256 + y * 64, x * 256 + y * 64 + 64)
            mixed = ids[rows]
            for i in range(3):
                mixed = jnp.where(lane < 66 + 2 * i, mixed, shared[i])
            cut = []
            for p in range(6):
                tile, at = (y, 32 * x) if p % 2 == 0 else (4 + x, 32 * y)
                tile = head_ref[:, 128 * tile : 128 * tile + 128]
                tile = both(tile, 0, p // 2) if p < 4 else tile[64:128]
                shift = (32 * (p % 4) - at) % 128
                cut.append(pltpu.roll(tile, shift, 1) if shift else tile)
            lead = jnp.where(lane < 64, jnp.where(lane < 32, cut[0], cut[1]), jnp.where(lane < 96, cut[2], cut[3]))
            out_ref[rows, 0:128] = lead.astype(BF16)
            follow = jnp.where(lane < 64, jnp.where(lane < 32, cut[4], cut[5]), mixed)
            out_ref[rows, 128:256] = follow.astype(BF16)
        span = pl.ds(x * 256, 256)
        stores.append(pltpu.make_async_copy(out_ref.at[span], out_hbm.at[span], out_sems.at[x]))
        stores[x].start()
    keep_piece.wait()
    for store in stores:
        store.wait()


def compact_kernel(early_ref, own_ref, lead_ref, next_ref):
    count = early_ref.shape[0]
    pick = iota((8, 128), 0)
    lane = iota((8, 128), 1) - 64
    weight = jnp.where(lane == 2 * pick, 32.0, jnp.where(lane == 2 * pick + 1, 1.0, 0.0))
    weight = jnp.where(pick < 4, weight, 0.0).astype(BF16)
    locals_ = dot(weight, early_ref[:, 128:256], (1, 1)).astype(jnp.int32)
    own_ref[...] = locals_
    place = iota((128, count), 0)
    hits = [(place == locals_[i : i + 1]).astype(F32).astype(BF16) for i in (1, 2, 3)]
    for odd in range(2):
        found = dot(early_ref[:, 0:128], hits[odd], (0, 1))[64 * odd : 64 * odd + 64]
        lead_ref[:, 128 * odd : 128 * odd + 128] = found.astype(BF16)
    next_ref[...] = dot(early_ref[:, 128:256], hits[2], (0, 1))[0:64].astype(BF16)


def gather_cols(refs, scratch):
    z = lax.axis_index("col") // 2
    for ref, at in zip(refs, (z, z ^ 1, 3 - z, z ^ 2)):
        scratch[at] = ref[...]
    return jnp.concatenate([scratch[i] for i in range(4)], axis=1)


def first_kernel(p0, p1, p2, p3, inverse_ref, next_ref, l0, l1, l2, l3, solved_ref, second_ref, scratch, link_ref, sems):
    loads = [pltpu.make_async_copy(ref, link_ref.at[i], sems.at[i]) for i, ref in enumerate((l0, l1, l2, l3))]
    for load in loads:
        load.start()
    lead = gather_cols((p0, p1, p2, p3), scratch)
    solved = dot(lead, inverse_ref[...], (1, 1)).astype(BF16)
    solved_ref[...] = solved
    for load in loads:
        load.wait()
    link = (link_ref[0] + link_ref[1]) + (link_ref[2] + link_ref[3])
    second_ref[...] = (next_ref[...].astype(F32) - dot(solved, link, (1, 1))).astype(BF16)


def second_kernel(p0, p1, p2, p3, inverse_ref, solved_ref, both_ref, scratch):
    z = lax.axis_index("col") // 2
    k = lax.axis_index("col") % 2
    for ref, at in zip((p0, p1, p2, p3), (z, z ^ 1, 3 - z, z ^ 2)):
        scratch[2 * at + k] = ref[0:64]
        scratch[2 * at + 1 - k] = ref[64:128]
    second = jnp.concatenate([scratch[i] for i in range(8)], axis=1)
    solved = dot(second, inverse_ref[...], (1, 1)).astype(BF16)
    even = lax.axis_index("col") % 2 == 0
    both_ref[:, 0:1024] = jnp.where(even, solved_ref[0:32], solved_ref[32:64])
    both_ref[:, 1024:2048] = jnp.where(even, solved[0:32], solved[32:64])


def scatter_kernel(own_ref, arrived_ref, out_ref, hit_ref, rows_ref, sems):
    count = arrived_ref.shape[0]
    loads = []
    for i in range(4):
        span = pl.ds(i * 256, 256)
        loads.append(pltpu.make_async_copy(arrived_ref.at[span, 256:1280], rows_ref.at[span], sems.at[i]))
        loads[i].start()
    hit_ref[...] = (iota((count, count), 0) == own_ref[0:1]).astype(F32).astype(BF16)
    for load in loads:
        load.wait()
    for q in range(4):
        cols = slice(q * 256, q * 256 + 256)
        out_ref[:, cols] = dot(hit_ref[...], rows_ref[:, cols], (1, 0)).astype(BF16)


def place_of(kind):
    row = lax.axis_index("row")
    core = lax.axis_index("col") % 2
    x, y = row // 4, row % 4
    if kind:
        core = 1 - core
    return jnp.where(core == 0, x, y), jnp.where(core == 0, y, x), core


def load_kernel(source_hbm, first_ref, second_ref, sems):
    copies = [pltpu.make_async_copy(source_hbm.at[i], ref, sems.at[i]) for i, ref in enumerate((first_ref, second_ref))]
    for copy in copies:
        copy.start()
    for copy in copies:
        copy.wait()


def heads_of(panels_ref, head_ref):
    row = lax.axis_index("row")
    col = lax.axis_index("col")
    unit = (iota((128, 1024), 1) == iota((128, 1024), 0) + col * 128).astype(F32) * -1.0
    for p in range(2):
        kept = jnp.where(row < 2, 0.0, panels_ref[p, 0, 0].astype(F32))
        head_ref[p] = jnp.where(row == p, unit, kept).astype(BF16)


def product(panels_ref, head_ref, solved_t):
    s0 = solved_t[:, 0:1024]
    s1 = solved_t[:, 1024:2048]
    head = dot(head_ref[0], s0, (1, 1)) + dot(head_ref[1], s1, (1, 1))
    tail0 = panels_ref[0, 1:8, 0].reshape(896, 1024)
    tail1 = panels_ref[1, 1:8, 0].reshape(896, 1024)
    return head, dot(tail0, s0, (1, 1)) + dot(tail1, s1, (1, 1))


def updated_blocks(blocks, pieces, panels_ref, rows_ref, solved_t, head_ref, write):
    keep = jnp.where(lax.axis_index("row") < 2, 0.0, 1.0)
    heads_of(panels_ref, head_ref)
    place_blocks(blocks, pieces, solved_t)
    head, tail = product(panels_ref, head_ref, solved_t)
    for n in range(2):
        draws = draws_of(blocks[n])
        part = slice(128 * n, 128 * n + 128)
        write(n, slice(0, 128), rows_ref[0:128, draws].astype(F32) * keep - head[:, part])
        write(n, slice(128, 1024), rows_ref[128:1024, draws].astype(F32) - tail[:, part])


def place_blocks(blocks, pieces, solved_t):
    for i, (kind, _) in enumerate(blocks):
        first, _, _ = place_of(kind)
        for j, place in enumerate((first, first ^ 1, 3 - first, first ^ 2)):
            at = pl.multiple_of(128 * i + 32 * place, 32)
            solved_t[pl.ds(at, 32), :] = pieces[i][j * 32 : j * 32 + 32, :]


def draws_of(block):
    kind, which = block
    _, second, core = place_of(kind)
    at = second if which == 3 else swap(which, second)
    return pl.ds(pl.multiple_of(128 * (4 * core + at), 128), 128)


def update_kernel(blocks, a_ref, b_ref, panels_ref, rows_ref, out_ref, solved_t, head_ref):
    def write(n, rows, value):
        out_ref[rows, 128 * n : 128 * n + 128] = value.astype(BF16)

    updated_blocks(blocks, (a_ref, b_ref), panels_ref, rows_ref, solved_t, head_ref, write)


def last_kernel(before, blocks, a_ref, b_ref, *refs):
    done, (panels_ref, rows_ref, out_hbm, solved_t, head_ref, out_ref, sems) = refs[: len(before)], refs[len(before) :]
    keep = jnp.where(lax.axis_index("row") < 2, 0.0, 1.0)
    heads_of(panels_ref, head_ref)
    place_blocks(blocks, (a_ref, b_ref), solved_t)
    stores = []
    for q in range(4):
        value = 0.0
        for p in range(2):
            solved = solved_t[:, p * 1024 : p * 1024 + 1024]
            if q == 0:
                factor = jnp.concatenate([head_ref[p], panels_ref[p, 1, 0]], axis=0)
            else:
                factor = panels_ref[p, 2 * q : 2 * q + 2, 0].reshape(256, 1024)
            value = value + dot(factor, solved, (1, 1))
        span = slice(q * 256, q * 256 + 256)
        for held, ref in zip(before, done):
            for n, block in enumerate(held):
                out_ref[span, draws_of(block)] = ref[span, 128 * n : 128 * n + 128]
        for n in range(2):
            draws = draws_of(blocks[n])
            rest = rows_ref[span, draws].astype(F32)
            if q == 0:
                rest = rest * jnp.where(iota((256, 128), 0) < 128, keep, 1.0)
            out_ref[span, draws] = (rest - value[:, 128 * n : 128 * n + 128]).astype(BF16)
        stores.append(pltpu.make_async_copy(out_ref.at[pl.ds(q * 256, 256)], out_hbm.at[pl.ds(q * 256, 256)], sems.at[q]))
        stores[q].start()
    for store in stores:
        store.wait()


HBM = pl.BlockSpec(memory_space=pltpu.HBM)
ANY = pl.BlockSpec(memory_space=pl.ANY)


def launch(kernel, args, outs, scratch=(), specs=None, out_specs=None, aliases=None, limit=16, flops=0, moved=0):
    return pl.pallas_call(
        kernel,
        out_shape=[jax.ShapeDtypeStruct(s, d) for s, d in outs],
        grid=(1,),
        in_specs=specs or [VMEM] * len(args),
        out_specs=out_specs or [VMEM] * len(outs),
        scratch_shapes=list(scratch),
        input_output_aliases=aliases or {},
        compiler_params=pltpu.CompilerParams(vmem_limit_bytes=int(limit * (1 << 20))),
        cost_estimate=pl.CostEstimate(flops=flops, bytes_accessed=moved, transcendentals=0),
    )(*args)


def spread_along(value, first, source):
    def move(kind):
        return along_first(kind) if first else along_second(kind)

    return [send(value, move(kind), source) for kind in range(3)]


def spread_first(piece):
    moved = [send(piece, along_first(kind)) for kind in range(3)]
    first, second, core = place_of(0)
    source = jnp.where(core == 0, 0, 1)
    line = jnp.where(first ^ 1 == source, moved[0], jnp.where(3 - first == source, moved[1], moved[2]))
    line = jnp.where(first == source, piece, line)
    return jnp.where(second == 1 - source, line, jnp.zeros_like(line))


def spread_second(piece):
    return spread_along(piece, False, lambda x, y, z, k: y == 1 if k == 0 else x == 0)


def around_cols(piece):
    return (piece, send(piece, along_z(0)), send(piece, along_z(1)), send(piece, along_z(2)))


def update(kernel, blocks, pieces, panels, rows, width=256, extra=(), out=VMEM):
    return launch(
        functools.partial(kernel, blocks),
        (*pieces, panels, rows),
        [((1024, width), BF16)],
        [pltpu.VMEM((256, 2048), BF16), pltpu.VMEM((2, 128, 1024), BF16), *extra],
        out_specs=[out],
        limit=16,
        flops=1 << 30,
        moved=2 << 20,
    )[0]


def steps(b_ingest, source_point, panels, diag_inverse):
    ordered, piece = launch(
        order_kernel,
        (source_point.reshape(1, 1024), b_ingest, panels),
        [((1024, 1280), BF16), ((128, 1024), BF16)],
        [
            pltpu.VMEM((1024, 1024), BF16),
            pltpu.VMEM((1024, 1280), BF16),
            pltpu.VMEM((1024, 1024), BF16),
            pltpu.VMEM((128, 1024), F32),
            pltpu.VMEM((128, 1024), BF16),
            pltpu.SemaphoreType.DMA((9,)),
            pltpu.SemaphoreType.DMA((5,)),
        ],
        specs=[VMEM, HBM, HBM],
        out_specs=[HBM, HBM],
        limit=61.4,
        flops=3 << 30,
        moved=5 << 20,
    )
    line = spread_first(piece)
    plane = spread_second(line)
    arrived = lax.all_to_all(ordered.reshape(128, 8, 1280), AXES, split_axis=0, concat_axis=0, tiled=True)
    inverses, _ = lax.optimization_barrier((diag_inverse, ordered))
    inverses = launch(
        load_kernel,
        (inverses,),
        [((1024, 1024), BF16)] * 2,
        [pltpu.SemaphoreType.DMA((2,))],
        specs=[HBM],
        limit=6,
        moved=8 << 20,
    )
    arrived = arrived.reshape(1024, 1280)
    own, lead, follow = launch(
        compact_kernel,
        (arrived,),
        [((8, 1024), jnp.int32), ((64, 256), BF16), ((64, 128), BF16)],
        specs=[pl.BlockSpec((1024, 256), lambda i: (0, 0))],
        limit=12,
        flops=1 << 27,
        moved=1 << 20,
    )
    solved, second = launch(
        first_kernel,
        (*around_cols(lead), inverses[0], follow, line, *plane),
        [((64, 1024), BF16), ((64, 128), BF16)],
        [pltpu.VMEM((4, 64, 256), BF16), pltpu.VMEM((4, 128, 1024), BF16), pltpu.SemaphoreType.DMA((4,))],
        specs=[VMEM] * 6 + [HBM] * 4,
        limit=12,
        flops=1 << 28,
        moved=3 << 20,
    )
    second = jnp.concatenate([second, send(second, other_core)], axis=0)
    (both,) = launch(
        second_kernel,
        (*around_cols(second), inverses[1], solved),
        [((32, 2048), BF16)],
        [pltpu.VMEM((8, 64, 128), BF16)],
        limit=12,
        flops=1 << 28,
        moved=3 << 20,
    )
    (rows,) = launch(
        scatter_kernel,
        (own, arrived),
        [((1024, 1024), BF16)],
        [pltpu.VMEM((1024, 1024), BF16), pltpu.VMEM((1024, 1024), BF16), pltpu.SemaphoreType.DMA((4,))],
        specs=[VMEM, ANY],
        limit=20,
        flops=1 << 31,
        moved=4 << 20,
    )
    line = [both] + [send(both, along_first(i)) for i in range(3)]
    line = jnp.concatenate(line, axis=0)
    side0 = send(line, along_second(0))
    side1 = send(line, along_second(1))
    side2 = send(line, along_second(2))
    line_other = send(line, other_core)
    side0_other, side1_other = send(side0, other_core), send(side1, other_core)
    side2_other = send(side2, other_core)
    places = [((0, n), (1, n)) for n in (3, 0, 1, 2)]
    part0 = update(update_kernel, places[0], (line, line_other), panels, rows)
    part1 = update(update_kernel, places[1], (side0, side0_other), panels, rows)
    part2 = update(update_kernel, places[2], (side1, side1_other), panels, rows)
    kernel = functools.partial(last_kernel, places[:3])
    pieces = (side2, side2_other, part0, part1, part2)
    extra = (pltpu.VMEM((1024, 1024), BF16), pltpu.SemaphoreType.DMA((4,)))
    updated = update(kernel, places[3], pieces, panels, rows, 1024, extra, HBM)
    return updated.reshape(8, 1, 128, 1024)


def solution(mesh):
    return jax.shard_map(
        steps,
        mesh=mesh,
        in_specs=(
            P(("row", "col"), None),
            P(("row", "col")),
            P(None, None, "row", "col", None),
            P(),
        ),
        out_specs=P(None, "row", "col", None),
        check_vma=False,
    )
```

```python
import functools

import jax
import jax.numpy as jnp
from jax import lax
from jax.experimental import pallas as pl
from jax.experimental.pallas import tpu as pltpu
from jax.sharding import PartitionSpec as P

AXES = ("row", "col")
BF16 = jnp.bfloat16
F32 = jnp.float32
VMEM = pl.BlockSpec(memory_space=pltpu.VMEM)


def device_id(x, y, z, k):
    return (x % 4 * 4 + y % 4) * 8 + z % 4 * 2 + k


def send(value, move, only=None):
    pairs = []
    for x in range(4):
        for y in range(4):
            for z in range(4):
                for k in range(2):
                    if only is None or only(x, y, z, k):
                        pairs.append((device_id(x, y, z, k), device_id(*move(x, y, z, k))))
    return lax.ppermute(value, AXES, pairs)


def swap(kind, at):
    return (at ^ 1, 3 - at, at ^ 2)[kind]


def along_first(kind):
    return lambda x, y, z, k: (swap(kind, x), y, z, k) if k == 0 else (x, swap(kind, y), z, k)


def along_second(kind):
    return lambda x, y, z, k: (x, swap(kind, y), z, k) if k == 0 else (swap(kind, x), y, z, k)


def along_z(kind):
    return lambda x, y, z, k: (x, y, swap(kind, z), k)


def other_core(x, y, z, k):
    return (x, y, z, 1 - k)


def iota(shape, axis):
    return lax.broadcasted_iota(jnp.int32, shape, axis)


def dot(a, b, contract):
    return lax.dot_general(a, b, ((contract[:1], contract[1:]), ((), ())), preferred_element_type=F32)


def order_kernel(points_ref, rows_hbm, panels_hbm, out_hbm, piece_hbm, rows_ref, out_ref, perm_ref, head_ref, piece_ref, in_sems, out_sems):
    count = rows_ref.shape[0]
    loads = []
    for i in range(8):
        span = pl.ds(i * 128, 128)
        loads.append(pltpu.make_async_copy(rows_hbm.at[span], rows_ref.at[span], in_sems.at[1 + i]))
        loads[i].start()
    piece = pltpu.make_async_copy(panels_hbm.at[0, 0, 0], piece_ref, in_sems.at[0])
    piece.start()
    points = points_ref[...]
    block = points >> 10
    offset = points & 1023
    target = (block & 15) * 8 + (offset >> 7)
    local = (block >> 4) * 128 + (offset & 127)
    wanted = (iota((128, count), 0) == target).astype(F32)
    earlier = (iota((count, count), 0) < iota((count, count), 1)).astype(F32).astype(BF16)
    seen = dot(wanted.astype(BF16), earlier, (1, 0))
    rank = jnp.sum(wanted * seen, axis=0, keepdims=True).astype(jnp.int32)
    slot = target * 8 + rank
    perm_ref[...] = (iota((count, count), 0) == slot).astype(F32).astype(BF16)
    part = iota((128, count), 0)
    digit = jnp.where(part % 2 == 0, local >> 5, local & 31)
    digits = jnp.where((part >= 64) & (part < 72), digit, 0).astype(F32).astype(BF16)
    ids = dot(perm_ref[...], digits, (1, 1))
    lane = iota((64, 128), 1)

    def both(value, first, odd):
        tiles = [value[first + 16 * z + 8 * odd : first + 16 * z + 8 * odd + 8] for z in range(4)]
        return jnp.concatenate([t for t in tiles for _ in range(2)], axis=0)

    shared = [both(ids, 0, 0), both(ids, 0, 1), ids[64:128]]
    stores = []
    for load in loads:
        load.wait()
    piece.wait()
    keep_piece = pltpu.make_async_copy(piece_ref, piece_hbm, out_sems.at[4])
    keep_piece.start()
    for x in range(4):
        chunk = slice(x * 256, x * 256 + 256)
        part_rows = dot(perm_ref[chunk, :], rows_ref[...], (1, 0))
        out_ref[chunk, 256:1280] = part_rows.astype(BF16)
        if x == 0:
            head_ref[...] = part_rows[0:128]
        for y in range(4):
            rows = slice(x * 256 + y * 64, x * 256 + y * 64 + 64)
            mixed = ids[rows]
            for i in range(3):
                mixed = jnp.where(lane < 66 + 2 * i, mixed, shared[i])
            cut = []
            for p in range(6):
                tile, at = (y, 32 * x) if p % 2 == 0 else (4 + x, 32 * y)
                tile = head_ref[:, 128 * tile : 128 * tile + 128]
                tile = both(tile, 0, p // 2) if p < 4 else tile[64:128]
                shift = (32 * (p % 4) - at) % 128
                cut.append(pltpu.roll(tile, shift, 1) if shift else tile)
            lead = jnp.where(lane < 64, jnp.where(lane < 32, cut[0], cut[1]), jnp.where(lane < 96, cut[2], cut[3]))
            out_ref[rows, 0:128] = lead.astype(BF16)
            follow = jnp.where(lane < 64, jnp.where(lane < 32, cut[4], cut[5]), mixed)
            out_ref[rows, 128:256] = follow.astype(BF16)
        span = pl.ds(x * 256, 256)
        stores.append(pltpu.make_async_copy(out_ref.at[span], out_hbm.at[span], out_sems.at[x]))
        stores[x].start()
    keep_piece.wait()
    for store in stores:
        store.wait()


def compact_kernel(early_ref, own_ref, lead_ref, next_ref):
    count = early_ref.shape[0]
    pick = iota((8, 128), 0)
    lane = iota((8, 128), 1) - 64
    weight = jnp.where(lane == 2 * pick, 32.0, jnp.where(lane == 2 * pick + 1, 1.0, 0.0))
    weight = jnp.where(pick < 4, weight, 0.0).astype(BF16)
    locals_ = dot(weight, early_ref[:, 128:256], (1, 1)).astype(jnp.int32)
    own_ref[...] = locals_
    place = iota((128, count), 0)
    hits = [(place == locals_[i : i + 1]).astype(F32).astype(BF16) for i in (1, 2, 3)]
    for odd in range(2):
        found = dot(early_ref[:, 0:128], hits[odd], (0, 1))[64 * odd : 64 * odd + 64]
        lead_ref[:, 128 * odd : 128 * odd + 128] = found.astype(BF16)
    next_ref[...] = dot(early_ref[:, 128:256], hits[2], (0, 1))[0:64].astype(BF16)


def gather_cols(refs, scratch):
    z = lax.axis_index("col") // 2
    for ref, at in zip(refs, (z, z ^ 1, 3 - z, z ^ 2)):
        scratch[at] = ref[...]
    return jnp.concatenate([scratch[i] for i in range(4)], axis=1)


def first_kernel(p0, p1, p2, p3, inverse_ref, next_ref, l0, l1, l2, l3, solved_ref, second_ref, scratch, link_ref, sems):
    loads = [pltpu.make_async_copy(ref, link_ref.at[i], sems.at[i]) for i, ref in enumerate((l0, l1, l2, l3))]
    for load in loads:
        load.start()
    lead = gather_cols((p0, p1, p2, p3), scratch)
    solved = dot(lead, inverse_ref[...], (1, 1)).astype(BF16)
    solved_ref[...] = solved
    for load in loads:
        load.wait()
    link = (link_ref[0] + link_ref[1]) + (link_ref[2] + link_ref[3])
    second_ref[...] = (next_ref[...].astype(F32) - dot(solved, link, (1, 1))).astype(BF16)


def second_kernel(p0, p1, p2, p3, inverse_ref, solved_ref, both_ref, scratch):
    z = lax.axis_index("col") // 2
    k = lax.axis_index("col") % 2
    for ref, at in zip((p0, p1, p2, p3), (z, z ^ 1, 3 - z, z ^ 2)):
        scratch[2 * at + k] = ref[0:64]
        scratch[2 * at + 1 - k] = ref[64:128]
    second = jnp.concatenate([scratch[i] for i in range(8)], axis=1)
    solved = dot(second, inverse_ref[...], (1, 1)).astype(BF16)
    even = lax.axis_index("col") % 2 == 0
    both_ref[:, 0:1024] = jnp.where(even, solved_ref[0:32], solved_ref[32:64])
    both_ref[:, 1024:2048] = jnp.where(even, solved[0:32], solved[32:64])


def scatter_kernel(own_ref, arrived_ref, out_ref, hit_ref, rows_ref, sems):
    count = arrived_ref.shape[0]
    loads = []
    for i in range(4):
        span = pl.ds(i * 256, 256)
        loads.append(pltpu.make_async_copy(arrived_ref.at[span, 256:1280], rows_ref.at[span], sems.at[i]))
        loads[i].start()
    hit_ref[...] = (iota((count, count), 0) == own_ref[0:1]).astype(F32).astype(BF16)
    for load in loads:
        load.wait()
    for q in range(4):
        cols = slice(q * 256, q * 256 + 256)
        out_ref[:, cols] = dot(hit_ref[...], rows_ref[:, cols], (1, 0)).astype(BF16)


def place_of(kind):
    row = lax.axis_index("row")
    core = lax.axis_index("col") % 2
    x, y = row // 4, row % 4
    if kind:
        core = 1 - core
    return jnp.where(core == 0, x, y), jnp.where(core == 0, y, x), core


def load_kernel(source_hbm, first_ref, second_ref, sems):
    copies = [pltpu.make_async_copy(source_hbm.at[i], ref, sems.at[i]) for i, ref in enumerate((first_ref, second_ref))]
    for copy in copies:
        copy.start()
    for copy in copies:
        copy.wait()


def heads_of(panels_ref, head_ref):
    row = lax.axis_index("row")
    col = lax.axis_index("col")
    unit = (iota((128, 1024), 1) == iota((128, 1024), 0) + col * 128).astype(F32) * -1.0
    for p in range(2):
        kept = jnp.where(row < 2, 0.0, panels_ref[p, 0, 0].astype(F32))
        head_ref[p] = jnp.where(row == p, unit, kept).astype(BF16)


def product(panels_ref, head_ref, solved_t):
    s0 = solved_t[:, 0:1024]
    s1 = solved_t[:, 1024:2048]
    head = dot(head_ref[0], s0, (1, 1)) + dot(head_ref[1], s1, (1, 1))
    tail0 = panels_ref[0, 1:8, 0].reshape(896, 1024)
    tail1 = panels_ref[1, 1:8, 0].reshape(896, 1024)
    return head, dot(tail0, s0, (1, 1)) + dot(tail1, s1, (1, 1))


def updated_blocks(blocks, pieces, panels_ref, rows_ref, solved_t, head_ref, write):
    keep = jnp.where(lax.axis_index("row") < 2, 0.0, 1.0)
    heads_of(panels_ref, head_ref)
    place_blocks(blocks, pieces, solved_t)
    head, tail = product(panels_ref, head_ref, solved_t)
    for n in range(2):
        draws = draws_of(blocks[n])
        part = slice(128 * n, 128 * n + 128)
        write(n, slice(0, 128), rows_ref[0:128, draws].astype(F32) * keep - head[:, part])
        write(n, slice(128, 1024), rows_ref[128:1024, draws].astype(F32) - tail[:, part])


def place_blocks(blocks, pieces, solved_t):
    for i, (kind, _) in enumerate(blocks):
        first, _, _ = place_of(kind)
        for j, place in enumerate((first, first ^ 1, 3 - first, first ^ 2)):
            at = pl.multiple_of(128 * i + 32 * place, 32)
            solved_t[pl.ds(at, 32), :] = pieces[i][j * 32 : j * 32 + 32, :]


def draws_of(block):
    kind, which = block
    _, second, core = place_of(kind)
    at = second if which == 3 else swap(which, second)
    return pl.ds(pl.multiple_of(128 * (4 * core + at), 128), 128)


def update_kernel(blocks, a_ref, b_ref, panels_ref, rows_ref, out_ref, solved_t, head_ref):
    def write(n, rows, value):
        out_ref[rows, 128 * n : 128 * n + 128] = value.astype(BF16)

    updated_blocks(blocks, (a_ref, b_ref), panels_ref, rows_ref, solved_t, head_ref, write)


def last_kernel(before, blocks, a_ref, b_ref, *refs):
    done, (panels_ref, rows_ref, out_hbm, solved_t, head_ref, out_ref, sems) = refs[: len(before)], refs[len(before) :]
    keep = jnp.where(lax.axis_index("row") < 2, 0.0, 1.0)
    heads_of(panels_ref, head_ref)
    place_blocks(blocks, (a_ref, b_ref), solved_t)
    stores = []
    for q in range(4):
        value = 0.0
        for p in range(2):
            solved = solved_t[:, p * 1024 : p * 1024 + 1024]
            if q == 0:
                factor = jnp.concatenate([head_ref[p], panels_ref[p, 1, 0]], axis=0)
            else:
                factor = panels_ref[p, 2 * q : 2 * q + 2, 0].reshape(256, 1024)
            value = value + dot(factor, solved, (1, 1))
        span = slice(q * 256, q * 256 + 256)
        for held, ref in zip(before, done):
            for n, block in enumerate(held):
                out_ref[span, draws_of(block)] = ref[span, 128 * n : 128 * n + 128]
        for n in range(2):
            draws = draws_of(blocks[n])
            rest = rows_ref[span, draws].astype(F32)
            if q == 0:
                rest = rest * jnp.where(iota((256, 128), 0) < 128, keep, 1.0)
            out_ref[span, draws] = (rest - value[:, 128 * n : 128 * n + 128]).astype(BF16)
        stores.append(pltpu.make_async_copy(out_ref.at[pl.ds(q * 256, 256)], out_hbm.at[pl.ds(q * 256, 256)], sems.at[q]))
        stores[q].start()
    for store in stores:
        store.wait()


HBM = pl.BlockSpec(memory_space=pltpu.HBM)
ANY = pl.BlockSpec(memory_space=pl.ANY)


def launch(kernel, args, outs, scratch=(), specs=None, out_specs=None, aliases=None, limit=16, flops=0, moved=0):
    return pl.pallas_call(
        kernel,
        out_shape=[jax.ShapeDtypeStruct(s, d) for s, d in outs],
        grid=(1,),
        in_specs=specs or [VMEM] * len(args),
        out_specs=out_specs or [VMEM] * len(outs),
        scratch_shapes=list(scratch),
        input_output_aliases=aliases or {},
        compiler_params=pltpu.CompilerParams(vmem_limit_bytes=int(limit * (1 << 20))),
        cost_estimate=pl.CostEstimate(flops=flops, bytes_accessed=moved, transcendentals=0),
    )(*args)


def spread_along(value, first, source):
    def move(kind):
        return along_first(kind) if first else along_second(kind)

    return [send(value, move(kind), source) for kind in range(3)]


def spread_first(piece):
    moved = []
    for kind in range(3):
        moved.append(send(piece, along_first(kind)))
    first, second, core = place_of(0)
    source = jnp.where(core == 0, 0, 1)
    line = jnp.where(first ^ 1 == source, moved[0], jnp.where(3 - first == source, moved[1], moved[2]))
    line = jnp.where(first == source, piece, line)
    return jnp.where(second == 1 - source, line, jnp.zeros_like(line))


def spread_second(piece):
    return spread_along(piece, False, lambda x, y, z, k: y == 1 if k == 0 else x == 0)


def around_cols(piece):
    return (piece, send(piece, along_z(0)), send(piece, along_z(1)), send(piece, along_z(2)))


def update(kernel, blocks, pieces, panels, rows, width=256, extra=(), out=VMEM):
    return launch(
        functools.partial(kernel, blocks),
        (*pieces, panels, rows),
        [((1024, width), BF16)],
        [pltpu.VMEM((256, 2048), BF16), pltpu.VMEM((2, 128, 1024), BF16), *extra],
        out_specs=[out],
        limit=16,
        flops=1 << 30,
        moved=2 << 20,
    )[0]


def steps(b_ingest, source_point, panels, diag_inverse):
    ordered, piece = launch(
        order_kernel,
        (source_point.reshape(1, 1024), b_ingest, panels),
        [((1024, 1280), BF16), ((128, 1024), BF16)],
        [
            pltpu.VMEM((1024, 1024), BF16),
            pltpu.VMEM((1024, 1280), BF16),
            pltpu.VMEM((1024, 1024), BF16),
            pltpu.VMEM((128, 1024), F32),
            pltpu.VMEM((128, 1024), BF16),
            pltpu.SemaphoreType.DMA((9,)),
            pltpu.SemaphoreType.DMA((5,)),
        ],
        specs=[VMEM, HBM, HBM],
        out_specs=[HBM, HBM],
        limit=61.4,
        flops=3 << 30,
        moved=5 << 20,
    )
    line = spread_first(piece)
    plane = spread_second(line)
    arrived = lax.all_to_all(ordered.reshape(128, 8, 1280), AXES, split_axis=0, concat_axis=0, tiled=True)
    inverses, _ = lax.optimization_barrier((diag_inverse, ordered))
    inverses = launch(
        load_kernel,
        (inverses,),
        [((1024, 1024), BF16)] * 2,
        [pltpu.SemaphoreType.DMA((2,))],
        specs=[HBM],
        limit=6,
        moved=8 << 20,
    )
    arrived = arrived.reshape(1024, 1280)
    own, lead, follow = launch(
        compact_kernel,
        (arrived,),
        [((8, 1024), jnp.int32), ((64, 256), BF16), ((64, 128), BF16)],
        specs=[pl.BlockSpec((1024, 256), lambda i: (0, 0))],
        limit=12,
        flops=1 << 27,
        moved=1 << 20,
    )
    solved, second = launch(
        first_kernel,
        (*around_cols(lead), inverses[0], follow, line, *plane),
        [((64, 1024), BF16), ((64, 128), BF16)],
        [pltpu.VMEM((4, 64, 256), BF16), pltpu.VMEM((4, 128, 1024), BF16), pltpu.SemaphoreType.DMA((4,))],
        specs=[VMEM] * 6 + [HBM] * 4,
        limit=12,
        flops=1 << 28,
        moved=3 << 20,
    )
    second = jnp.concatenate([second, send(second, other_core)], axis=0)
    (both,) = launch(
        second_kernel,
        (*around_cols(second), inverses[1], solved),
        [((32, 2048), BF16)],
        [pltpu.VMEM((8, 64, 128), BF16)],
        limit=12,
        flops=1 << 28,
        moved=3 << 20,
    )
    (rows,) = launch(
        scatter_kernel,
        (own, arrived),
        [((1024, 1024), BF16)],
        [pltpu.VMEM((1024, 1024), BF16), pltpu.VMEM((1024, 1024), BF16), pltpu.SemaphoreType.DMA((4,))],
        specs=[VMEM, ANY],
        limit=20,
        flops=1 << 31,
        moved=4 << 20,
    )
    line = [both] + [send(both, along_first(i)) for i in range(3)]
    line = jnp.concatenate(line, axis=0)
    side0 = send(line, along_second(0))
    side2 = send(line, along_second(2))
    side1 = send(line, along_second(1))
    line_other = send(line, other_core)
    side0_other, side2_other = send(side0, other_core), send(side2, other_core)
    side1_other = send(side1, other_core)
    places = [((0, n), (1, n)) for n in (3, 0, 2, 1)]
    part0 = update(update_kernel, places[0], (line, line_other), panels, rows)
    part1 = update(update_kernel, places[1], (side0, side0_other), panels, rows)
    part2 = update(update_kernel, places[2], (side2, side2_other), panels, rows)
    kernel = functools.partial(last_kernel, places[:3])
    pieces = (side1, side1_other, part0, part1, part2)
    extra = (pltpu.VMEM((1024, 1024), BF16), pltpu.SemaphoreType.DMA((4,)))
    updated = update(kernel, places[3], pieces, panels, rows, 1024, extra, HBM)
    return updated.reshape(8, 1, 128, 1024)


def solution(mesh):
    return jax.shard_map(
        steps,
        mesh=mesh,
        in_specs=(
            P(("row", "col"), None),
            P(("row", "col")),
            P(None, None, "row", "col", None),
            P(),
        ),
        out_specs=P(None, "row", "col", None),
        check_vma=False,
    )
```
